32 devices in a mesh: ctx: 16 (over z, y, x), fsdp: 2 (over core).
Axes of the slice: x: 2, y: 2, z: 4, core: 2. Of those that a mesh axis runs over, the one named last changes fastest.
Arguments:
- inputs: bfloat16 [2, 2, 2048, 960], P(None, 'fsdp', 'ctx'), may hold values from -6 to 6
- gain_attn: bfloat16 [960], P('fsdp'), may hold values from 0.099609375 to 1.8984375
- w_query: bfloat16 [960, 960], P('fsdp'), may hold values from -0.1875 to 0.1875
- w_keyval: bfloat16 [960, 640], P('fsdp'), may hold values from -0.1875 to 0.1875
- w_out: bfloat16 [960, 960], P('fsdp'), may hold values from -0.75 to 0.75
- gain_mlp: bfloat16 [960], P('fsdp'), may hold values from 0.099609375 to 1.8984375
- w_gate: bfloat16 [960, 2560], P('fsdp'), may hold values from -0.1875 to 0.1875
- w_up: bfloat16 [960, 2560], P('fsdp'), may hold values from -0.1875 to 0.1875
- w_down: bfloat16 [2560, 960], P('fsdp'), may hold values from -0.125 to 0.125
- cotangent: bfloat16 [2, 2, 2048, 960], P(None, 'fsdp', 'ctx'), may hold values from -6 to 6
- seq_blocks: int32 [2, 2, 2], replicated, may hold values from 8 to 8, as said below
- block_slots: int32 [2, 2, 16], replicated, may hold values from 0 to 15, each once within a row
Outputs:
- layer_out: bfloat16 [2, 2, 2048, 960], P(None, 'fsdp', 'ctx')
- input_grad: float32 [2, 2, 2048, 960], P(None, 'fsdp', 'ctx')
- gain_attn_grad: float32 [960], P('fsdp')
- query_grad: float32 [960, 960], P('fsdp')
- keyval_grad: float32 [960, 640], P('fsdp')
- out_grad: float32 [960, 960], P('fsdp')
- gain_mlp_grad: float32 [960], P('fsdp')
- gate_grad: float32 [960, 2560], P('fsdp')
- up_grad: float32 [960, 2560], P('fsdp')
- down_grad: float32 [2560, 960], P('fsdp')
The draws below stay inside these ranges and needn't reach their ends.
Inputs may be any that keep to these rules, and one draw needn't show every extreme that they name: `seq_blocks`: each row holds the lengths in blocks of 128 tokens of the 2 sequences of one group, in natural order; they sum to 16. `block_slots`: each row is a permutation of the slots of one group.
All inputs are finite; a program needn't handle non-finite values.
Results may differ from the reference program's by a relative error of at most 0.015.
Values may be sent and summed in bfloat16 or wider, within the bound.
No kernel may reach another device: no remote copies, remote signals or barrier semaphores. Data moves between devices by JAX's collectives and lax.ppermute only.
A program may use at most 320 MiB of HBM per device.

```python
import jax
import jax.numpy as jnp
from jax import lax

D = 960
HEADS = 15
KVH = 5
HD = 64
FF = 2560
WINDOW = 2048
BLK = 128
MINB = 8
MB = 2
QD = 960
KVD = 320
GTOK = 2048
GBLK = 16
N_FSDP = 2


def draw_seq_blocks(key, part):
    first_key = jax.random.fold_in(key, 11)
    pick_key = jax.random.fold_in(key, 23)
    first = jax.random.randint(first_key, (MB * N_FSDP,), MINB, GBLK - MINB + 1, dtype=jnp.int32)
    chosen = jax.random.randint(pick_key, (), 0, MB * N_FSDP, dtype=jnp.int32)
    indices = jnp.arange(MB * N_FSDP, dtype=jnp.int32)
    first = jnp.where(indices == chosen, jnp.int32(MINB), first).astype(jnp.int32)
    first = first.reshape(MB, N_FSDP)
    second = (GBLK - first).astype(jnp.int32)
    return jnp.stack([first, second], axis=-1).astype(jnp.int32)


def steps_of(rng, dims, cuts, smallest, largest):
    factor_of = 1.0
    for dim, shards_of in cuts:
        draws = jax.random.uniform(jax.random.fold_in(jax.random.fold_in(rng, 6), dim), (shards_of,), jnp.float32, smallest / len(cuts), largest / len(cuts))
        factor_of = factor_of * jnp.repeat(jnp.exp(draws), dims[dim] // shards_of).reshape((-1,) + (1,) * (len(dims) - 1 - dim))
    return factor_of


def gaussian(stream_key, dims, scale, limit, cuts=(), kind=jnp.bfloat16):
    factor_of = steps_of(stream_key, dims, cuts, -0.22, 0.18) if cuts else 1.0
    values = jax.random.normal(stream_key, dims, jnp.float32) * scale * factor_of
    return jnp.minimum(jnp.maximum(values, -limit), limit).astype(kind)


def setup_inputs(seed: int = 0) -> dict:
    seeds = jax.random.split(jax.random.key(seed), 13)
    inputs = gaussian(seeds[0], (MB, N_FSDP, GTOK, D), 1.0, 6.0, ((1, 2), (2, 16)))
    gain_attn = jnp.clip(1.0 + 0.18 * jax.random.normal(seeds[1], (D,), jnp.float32), 0.099609375, 1.8984375).astype(jnp.bfloat16)
    w_query = gaussian(seeds[2], (D, QD), D ** -0.5, 0.1875, ((0, 2),))
    w_keyval = gaussian(seeds[3], (D, 2 * KVD), D ** -0.5, 0.1875, ((0, 2),))
    w_out = gaussian(seeds[4], (QD, D), (QD // 16) ** -0.5, 0.75, ((0, 2),))
    gain_mlp = jnp.clip(1.0 + 0.18 * jax.random.normal(seeds[5], (D,), jnp.float32), 0.099609375, 1.8984375).astype(jnp.bfloat16)
    w_gate = gaussian(seeds[6], (D, FF), D ** -0.5, 0.1875, ((0, 2),))
    w_up = gaussian(seeds[7], (D, FF), D ** -0.5, 0.1875, ((0, 2),))
    w_down = gaussian(seeds[8], (FF, D), FF ** -0.5, 0.125, ((0, 2),))
    cotangent = gaussian(seeds[9], (MB, N_FSDP, GTOK, D), 1.0, 6.0, ((1, 2), (2, 16)))
    seq_blocks = draw_seq_blocks(jax.random.fold_in(seeds[12], 71), 0)
    block_slots = jax.vmap(lambda own: jax.random.permutation(own, GBLK))(jax.random.split(seeds[11], MB * N_FSDP)).reshape((MB, N_FSDP, GBLK)).astype(jnp.int32)
    return dict(inputs=inputs, gain_attn=gain_attn, w_query=w_query, w_keyval=w_keyval, w_out=w_out, gain_mlp=gain_mlp, w_gate=w_gate, w_up=w_up, w_down=w_down, cotangent=cotangent, seq_blocks=seq_blocks, block_slots=block_slots)


@jax.custom_vjp
def low(v):
    return lax.optimization_barrier(v.astype(jnp.bfloat16)).astype(jnp.float32)

@jax.custom_vjp
def low_back(v):
    return v

def low_keep(v):
    return (low(v), None)

def reduced_precision_pass(kept, grad):
    return (grad,)

def back_keep(v):
    return (v, None)

def back_low(kept, grad):
    return (low(grad),)
low.defvjp(low_keep, reduced_precision_pass)
low_back.defvjp(back_keep, back_low)
EPS = 1e-05
NEG = -1e+30
HIGH = lax.Precision.HIGHEST

def matmul(left, right):
    return jnp.dot(left, right, precision=HIGH, preferred_element_type=jnp.float32)

def rms_gain(values, gain):
    return values * lax.rsqrt(lax.optimization_barrier(jnp.mean(values * values, axis=-1, keepdims=True)) + EPS) * gain

def token_sequences(sequence_lengths_row):
    blocks = jnp.arange(GBLK, dtype=jnp.int32)
    block_ends = jnp.cumsum(sequence_lengths_row).astype(jnp.int32)
    per_block = lax.optimization_barrier(jnp.sum((block_ends[None, :] <= blocks[:, None]).astype(jnp.int32), axis=1)).astype(jnp.int32)
    return jnp.repeat(per_block, BLK)

def attention(queries, key_rows, values, sequence):
    group_size = HEADS // KVH
    logit_scale_factor = HD ** (-0.5)
    block_rows = min(512, GTOK)
    key_span = WINDOW + block_rows
    key_pad = jnp.concatenate([jnp.zeros((WINDOW, KVH * HD), jnp.float32), key_rows], axis=0)
    value_pad = jnp.concatenate([jnp.zeros((WINDOW, KVH * HD), jnp.float32), values], axis=0)
    sequence_padding = jnp.concatenate([jnp.full((WINDOW,), -1, jnp.int32), sequence.astype(jnp.int32)])

    def one_block(start):
        query_blk = lax.dynamic_slice_in_dim(queries, start, block_rows, 0).reshape(block_rows, KVH, group_size, HD)
        key_blk = lax.dynamic_slice_in_dim(key_pad, start, key_span, 0).reshape(key_span, KVH, HD)
        value_blk = lax.dynamic_slice_in_dim(value_pad, start, key_span, 0).reshape(key_span, KVH, HD)
        query_seq = lax.dynamic_slice_in_dim(sequence.astype(jnp.int32), start, block_rows, 0)
        key_seq = lax.dynamic_slice_in_dim(sequence_padding, start, key_span, 0)
        query_pos = start + jnp.arange(block_rows, dtype=jnp.int32)
        key_pos = start - WINDOW + jnp.arange(key_span, dtype=jnp.int32)
        allowed = (query_seq[:, None] == key_seq[None, :]) & (key_pos[None, :] <= query_pos[:, None]) & (query_pos[:, None] - key_pos[None, :] < WINDOW)
        scores = low_back(jnp.einsum('qgrd,kgd->grqk', query_blk, key_blk, precision=HIGH) * logit_scale_factor)
        scores = jnp.where(allowed, scores, NEG)
        highest = lax.optimization_barrier(jnp.max(scores, axis=-1, keepdims=True))
        weights = jnp.where(allowed, jnp.exp(scores - highest), 0.0)
        probabilities = low(weights / lax.optimization_barrier(jnp.sum(weights, axis=-1, keepdims=True)))
        result = jnp.einsum('grqk,kgd->qgrd', probabilities, value_blk, precision=HIGH)
        return result.reshape(block_rows, HEADS * HD)
    starts = jnp.arange(GTOK // block_rows, dtype=jnp.int32) * block_rows
    return lax.map(jax.checkpoint(one_block), starts).reshape(GTOK, HEADS * HD)

def layer(in_rows, gain_attn, w_query, w_keyval, w_out, gain_mlp, w_gate, w_up, w_down, sequence):
    kv_width = KVH * HD
    normed = low(rms_gain(in_rows, gain_attn))
    queries = low(low_back(matmul(normed, w_query)))
    keyvals = low(low_back(matmul(normed, w_keyval)))
    attended = low(low_back(attention(queries, keyvals[:, :kv_width], keyvals[:, kv_width:], sequence)))
    mixed = in_rows + low_back(matmul(attended, w_out))
    normed_mlp = low(rms_gain(mixed, gain_mlp))
    gate_pre = low_back(matmul(normed_mlp, w_gate))
    up_pre = low_back(matmul(normed_mlp, w_up))
    hidden = low(jax.nn.silu(gate_pre) * up_pre)
    return mixed + matmul(hidden, w_down)

def reference(inputs, gain_attn, w_query, w_keyval, w_out, gain_mlp, w_gate, w_up, w_down, cotangent, seq_blocks, block_slots):
    sequences = [[token_sequences(seq_blocks[micro_index, shard_index]) for shard_index in range(N_FSDP)] for micro_index in range(MB)]

    def natural(array, micro_index, shard_index):
        blocked = array[micro_index, shard_index].reshape(GBLK, BLK, -1)
        return blocked[block_slots[micro_index, shard_index]].reshape(GTOK, -1)

    def dealt(array, micro_index, shard_index):
        blocked = array[micro_index, shard_index].reshape(GBLK, BLK, -1)
        placed = jnp.zeros_like(blocked).at[block_slots[micro_index, shard_index]].set(blocked)
        return placed.reshape(GTOK, -1)

    def regroup(array, mapping):
        return jnp.stack([jnp.stack([mapping(array, micro_index, shard_index) for shard_index in range(N_FSDP)]) for micro_index in range(MB)])
    in_natural = regroup(inputs, natural).astype(jnp.float32)
    cot_natural = regroup(cotangent, natural).astype(jnp.float32)
    params = (gain_attn.astype(jnp.float32), w_query.astype(jnp.float32), w_keyval.astype(jnp.float32), w_out.astype(jnp.float32), gain_mlp.astype(jnp.float32), w_gate.astype(jnp.float32), w_up.astype(jnp.float32), w_down.astype(jnp.float32))

    def forward(in_all, *weights):
        stacked = []
        for micro_index in range(MB):
            row_list = []
            for shard_index in range(N_FSDP):
                row_list.append(layer(in_all[micro_index, shard_index], *weights, sequences[micro_index][shard_index]))
            stacked.append(jnp.stack(row_list))
        return jnp.stack(stacked)
    result, pullback = jax.vjp(forward, in_natural, *params)
    gradients = pullback(cot_natural)
    layer_out = regroup(result, dealt).astype(jnp.bfloat16)
    input_grad = regroup(gradients[0], dealt)
    return (layer_out, input_grad, gradients[1], gradients[2], gradients[3], gradients[4], gradients[5], gradients[6], gradients[7], gradients[8])
```

```python
import functools

import jax
import jax.numpy as jnp
from jax import lax
from jax.experimental import pallas as pl
from jax.experimental.pallas import tpu as pltpu
from jax.sharding import PartitionSpec as P

HEADS = 15
KVH = 5
HD = 64
REP = HEADS // KVH
WINDOW = 2048
BLK = 128
HALF = BLK // 2
KVW = 2 * KVH * HD
EPS = 1e-05
NEG = -1e30
SCALE = HD ** (-0.5)
LANES = 128
GCOLS = REP * BLK

bf16 = jnp.bfloat16
f32 = jnp.float32


def dot(left, right, left_dim, right_dim):
    return lax.dot_general(
        left, right, (((left_dim,), (right_dim,)), ((), ())), preferred_element_type=f32
    )


def flip_ctx(value, bit):
    size = lax.axis_size("ctx")
    return lax.ppermute(value, "ctx", [(i, i ^ (1 << bit)) for i in range(size)])


def swap_fsdp(value):
    return lax.ppermute(value, "fsdp", [(0, 1), (1, 0)])


def bit_orders(size):
    count = size.bit_length() - 1
    high = list(range(count - 1, 1, -1))
    return (high + [1, 0], high + [0, 1])


def gather_blocks(piece, order):
    held = piece[None]
    for bit in order:
        held = jnp.concatenate([held, flip_ctx(held, bit)], axis=0)
    return held


def scatter_blocks(held, order):
    for bit in reversed(order):
        half = held.shape[0] // 2
        arrived = flip_ctx(held[half:], bit)
        held = (held[:half].astype(f32) + arrived.astype(f32)).astype(bf16)
    return held[0]


def place_of(relative, order):
    place = jnp.zeros_like(relative)
    for position, bit in enumerate(order):
        place = place | (((relative >> bit) & 1) << position)
    return place


def sum_stages(size, first_swapped):
    count = size.bit_length() - 1
    low = [1, 0] if first_swapped else [0, 1]
    return low + list(range(2, count))


def reduce_chunk(grad, stages):
    me = lax.axis_index("ctx")
    for bit, dim in stages:
        half = grad.shape[dim] // 2
        own = (me >> bit) & 1
        sent = lax.dynamic_slice_in_dim(grad, (1 - own) * half, half, dim).astype(bf16)
        kept = lax.dynamic_slice_in_dim(grad, own * half, half, dim)
        grad = (kept.astype(f32) + flip_ctx(sent, bit).astype(f32)).astype(bf16)
    return grad


def gather_chunk(chunk, stages, last_type):
    me = lax.axis_index("ctx")
    for number, (bit, dim) in enumerate(reversed(stages)):
        low = ((me >> bit) & 1) == 0
        arrived = flip_ctx(chunk, bit)
        if number == len(stages) - 1:
            chunk, arrived = chunk.astype(last_type), arrived.astype(last_type)
        chunk = jnp.concatenate(
            [jnp.where(low, chunk, arrived), jnp.where(low, arrived, chunk)], axis=dim
        )
    return chunk


def sum_vector(vector):
    count = lax.axis_size("ctx").bit_length() - 1
    for bit in range(count):
        vector = vector + flip_ctx(vector, bit)
    return vector


def key_tile(first_ref, second_ref, first, second, unit):
    lanes = pl.ds((unit // 2) * LANES, LANES)
    return jnp.concatenate([first_ref[first, :, lanes], second_ref[second, :, lanes]], axis=0)


def heads_t(rows_t, group, unit):
    parts = [
        rows_t[(group * REP + r) * HD : (group * REP + r + 1) * HD, :] for r in range(REP)
    ]
    block = jnp.concatenate(parts, axis=1)
    zero = jnp.zeros_like(block)
    return jnp.concatenate([zero, block] if unit % 2 else [block, zero], axis=0)


def half_rows(tile_t, unit):
    return tile_t[(unit % 2) * HD : (unit % 2 + 1) * HD, :]


def block_mask(kind):
    key = lax.broadcasted_iota(jnp.int32, (BLK, GCOLS), 0)
    query = lax.broadcasted_iota(jnp.int32, (BLK, GCOLS), 1) % BLK
    return key <= query if kind == "first" else key > query


def forward_kernel(far, table, first_ref, second_ref, query_ref, out_ref, lse_ref):
    count = table[0, 0]
    queries = query_ref[...]
    for group in range(KVH):
        q_pad = heads_t(queries, group, group)
        value_unit = KVH + group

        def step(index, carried, mask):
            high, total, acc = carried
            first, second = table[1, index], table[2, index]
            keys = key_tile(first_ref, second_ref, first, second, group)
            values = key_tile(first_ref, second_ref, first, second, value_unit)
            scores = dot(keys, q_pad, 1, 0) * SCALE
            if mask is not None:
                scores = jnp.where(mask, scores, NEG)
            new_high = jnp.maximum(high, jnp.max(scores, axis=0, keepdims=True))
            weights = jnp.exp(scores - new_high)
            fade = jnp.exp(high - new_high)
            total = total * fade + jnp.sum(weights, axis=0, keepdims=True)
            values_t = half_rows(values.T, value_unit)
            acc = acc * fade + dot(values_t, weights.astype(bf16), 1, 0)
            return (new_high, total, acc)

        start = (
            jnp.full((1, GCOLS), NEG, f32),
            jnp.zeros((1, GCOLS), f32),
            jnp.zeros((HD, GCOLS), f32),
        )
        carried = step(0, start, block_mask("first"))
        near = jnp.minimum(count, WINDOW // BLK) if far else count
        carried = lax.fori_loop(1, near, lambda i, c: step(i, c, None), carried)
        if far:
            carried = lax.fori_loop(
                near, count, lambda i, c: step(i, c, block_mask("last")), carried
            )
        high, total, acc = carried
        acc = acc / total
        lse = high + jnp.log(total)
        for r in range(REP):
            head = group * REP + r
            columns = slice(r * BLK, (r + 1) * BLK)
            out_ref[head * HD : (head + 1) * HD, :] = acc[:, columns]
        lse_ref[:, group * GCOLS : (group + 1) * GCOLS] = lse


def backward_kernel(
    far,
    table,
    first_ref,
    second_ref,
    query_ref,
    grad_ref,
    out_ref,
    lse_ref,
    dq_ref,
    dfirst_ref,
    dsecond_ref,
    right_ref,
    delta_ref,
    left_ref,
    acc_ref,
):
    count = table[0, 0]
    queries = query_ref[...]
    grads = grad_ref[...]
    product = grads.astype(f32) * out_ref[...]
    for head in range(HEADS):
        delta_ref[:, head * BLK : (head + 1) * BLK] = jnp.sum(
            product[head * HD : (head + 1) * HD, :], axis=0, keepdims=True
        )
    for unit in range(2 * KVH):
        group = unit % KVH
        source = queries if unit < KVH else grads
        padded = heads_t(source, group, unit)
        right_ref[unit * GCOLS : (unit + 1) * GCOLS, :] = padded.astype(f32).T.astype(bf16)
    dfirst_ref[...] = jnp.zeros_like(dfirst_ref)
    dsecond_ref[...] = jnp.zeros_like(dsecond_ref)
    acc_ref[...] = jnp.zeros_like(acc_ref)

    def step(index, mask):
        first, second = table[1, index], table[2, index]
        for group in range(KVH):
            value_unit = KVH + group
            columns = slice(group * GCOLS, (group + 1) * GCOLS)
            q_pad = heads_t(queries, group, group)
            g_pad = heads_t(grads, group, value_unit)
            keys = key_tile(first_ref, second_ref, first, second, group)
            values = key_tile(first_ref, second_ref, first, second, value_unit)
            scores = dot(keys, q_pad, 1, 0) * SCALE
            probs = jnp.exp(scores - lse_ref[:, columns])
            if mask is not None:
                probs = jnp.where(mask, probs, 0.0)
            grad_probs = dot(values, g_pad, 1, 0)
            grad_scores = (probs * (grad_probs - delta_ref[:, columns])).astype(bf16)
            left_ref[:, columns] = grad_scores
            left_ref[:, (KVH * GCOLS) + group * GCOLS : (KVH * GCOLS) + (group + 1) * GCOLS] = (
                probs.astype(bf16)
            )
            keys_t = half_rows(keys.T, group)
            acc_ref[:, columns] += dot(keys_t, grad_scores, 1, 0)
        for tile in range(KVH):
            rows = slice(2 * tile * GCOLS, 2 * (tile + 1) * GCOLS)
            lanes = slice(tile * LANES, (tile + 1) * LANES)
            block = dot(left_ref[:, rows], right_ref[rows, :], 1, 0)
            lane = lax.broadcasted_iota(jnp.int32, (1, LANES), 1) + tile * LANES
            block = block * jnp.where(lane < KVH * HD, SCALE, 1.0)
            dfirst_ref[first, :, lanes] = block[:HALF].astype(bf16)
            dsecond_ref[second, :, lanes] = block[HALF:].astype(bf16)

    step(0, block_mask("first"))
    near = jnp.minimum(count, WINDOW // BLK) if far else count

    @pl.loop(1, near)
    def _(index):
        step(index, None)

    if far:

        @pl.loop(near, count)
        def _(index):
            step(index, block_mask("last"))

    for head in range(HEADS):
        columns = slice(head * BLK, (head + 1) * BLK)
        dq_ref[head * HD : (head + 1) * HD, :] = (acc_ref[:, columns] * SCALE).astype(bf16)


VMEM_SPEC = pl.BlockSpec(memory_space=pltpu.VMEM)
SMEM_SPEC = pl.BlockSpec(memory_space=pltpu.SMEM)


def attention_forward(table, first, second, queries_t):
    steps = first.shape[0]
    far = steps > WINDOW // BLK
    return pl.pallas_call(
        functools.partial(forward_kernel, far),
        out_shape=(
            jax.ShapeDtypeStruct((HEADS * HD, BLK), f32),
            jax.ShapeDtypeStruct((1, HEADS * BLK), f32),
        ),
        in_specs=[SMEM_SPEC] + [VMEM_SPEC] * 3,
        out_specs=(VMEM_SPEC,) * 2,
        compiler_params=pltpu.CompilerParams(vmem_limit_bytes=40 << 20),
        cost_estimate=pl.CostEstimate(
            flops=4 * HEADS * HD * BLK * BLK * 8,
            bytes_accessed=first.size * 4,
            transcendentals=HEADS * BLK * BLK * 8,
        ),
        name="attention_forward",
    )(table, first, second, queries_t)


def attention_backward(table, first, second, queries_t, grads_t, out_t, lse):
    steps = first.shape[0]
    far = steps > WINDOW // BLK
    return pl.pallas_call(
        functools.partial(backward_kernel, far),
        out_shape=(
            jax.ShapeDtypeStruct((HEADS * HD, BLK), bf16),
            jax.ShapeDtypeStruct(first.shape, bf16),
            jax.ShapeDtypeStruct(second.shape, bf16),
        ),
        in_specs=[SMEM_SPEC] + [VMEM_SPEC] * 6,
        out_specs=(VMEM_SPEC,) * 3,
        scratch_shapes=[
            pltpu.VMEM((2 * KVH * GCOLS, LANES), bf16),
            pltpu.VMEM((1, HEADS * BLK), f32),
            pltpu.VMEM((BLK, 2 * KVH * GCOLS), bf16),
            pltpu.VMEM((HD, HEADS * BLK), f32),
        ],
        compiler_params=pltpu.CompilerParams(vmem_limit_bytes=48 << 20),
        cost_estimate=pl.CostEstimate(
            flops=10 * HEADS * HD * BLK * BLK * 8,
            bytes_accessed=first.size * 8,
            transcendentals=HEADS * BLK * BLK * 8,
        ),
        name="attention_backward",
    )(table, first, second, queries_t, grads_t, out_t, lse)


def block_table(lengths, slots, orders):
    me = lax.axis_index("ctx")
    count = slots.shape[0]
    naturals = jnp.arange(count, dtype=jnp.int32)
    own = jnp.sum(jnp.where(slots == me, naturals, 0))
    end = jnp.int32(0)
    start = jnp.int32(0)
    for i in range(lengths.shape[0]):
        end = end + lengths[i]
        start = jnp.where(end <= own, end, start)
    lowest = jnp.maximum(start, own - WINDOW // BLK)
    wanted = jnp.maximum(own - naturals, 0)
    match = wanted[:, None] == naturals[None, :]
    slot_back = jnp.sum(jnp.where(match, slots[None, :], 0), axis=1)
    relative = slot_back ^ me
    head = jnp.broadcast_to(own - lowest + 1, (count,))
    return jnp.stack([head, place_of(relative, orders[0]), place_of(relative, orders[1])])


def rms_back(values, inverse, normalized_gradient, gain):
    scaled = normalized_gradient * gain
    gain_part = jnp.sum(normalized_gradient * values * inverse, axis=0)
    cubed = inverse * inverse * inverse
    input_part = inverse * scaled - values * cubed * jnp.mean(
        scaled * values, axis=-1, keepdims=True
    )
    return (input_part, gain_part)


def rms_inverse(values):
    return lax.rsqrt(jnp.mean(values * values, axis=-1, keepdims=True) + EPS)


def per_device(
    inputs,
    gain_attn,
    w_query,
    w_keyval,
    w_out,
    gain_mlp,
    w_gate,
    w_up,
    w_down,
    cotangent,
    seq_blocks,
    block_slots,
):
    micro = inputs.shape[0]
    size = lax.axis_size("ctx")
    shard = lax.axis_index("fsdp")
    orders = bit_orders(size)
    is_low = shard == 0

    def joined(part):
        other = swap_fsdp(part)
        return jnp.concatenate(
            [jnp.where(is_low, part, other), jnp.where(is_low, other, part)], axis=0
        )

    def whole(part):
        return lax.all_gather(part, "fsdp", axis=0, tiled=True)

    def halves(value, dim):
        half = value.shape[dim] // 2
        mine = lax.dynamic_slice_in_dim(value, shard * half, half, dim)
        theirs = lax.dynamic_slice_in_dim(value, (1 - shard) * half, half, dim)
        return mine, theirs

    attn_gain = joined(gain_attn).astype(f32)
    keyval_full = joined(w_keyval)
    query_full = joined(w_query)
    mlp_gain = joined(gain_mlp).astype(f32)
    out_full = whole(w_out)
    gate_full = whole(w_gate)
    up_full = whole(w_up)
    down_full = whole(w_down)

    rows = micro * BLK
    in_rows = inputs[:, 0].reshape(rows, -1).astype(f32)
    grad_out = cotangent[:, 0].reshape(rows, -1)
    inverse_attn = rms_inverse(in_rows)
    normed = (in_rows * inverse_attn * attn_gain).astype(bf16)
    keyvals = dot(normed, keyval_full, 1, 0).astype(bf16)

    tables, firsts, seconds = [], [], []
    for m in range(micro):
        lengths = lax.dynamic_index_in_dim(seq_blocks[m], shard, 0, keepdims=False)
        slots = lax.dynamic_index_in_dim(block_slots[m], shard, 0, keepdims=False)
        tables.append(block_table(lengths, slots, orders))
        firsts.append(gather_blocks(keyvals[m * BLK : m * BLK + HALF], orders[0]))
        seconds.append(gather_blocks(keyvals[m * BLK + HALF : (m + 1) * BLK], orders[1]))

    queries_t = dot(query_full, normed, 0, 1).astype(bf16)
    normed_mine, normed_theirs = halves(normed, 1)
    normed_other = swap_fsdp(normed_theirs)
    grad_out_other = swap_fsdp(grad_out)

    queries, outs, lses = [], [], []
    for m in range(micro):
        queries.append(queries_t[:, m * BLK : (m + 1) * BLK])
        out_t, lse = attention_forward(tables[m], firsts[m], seconds[m], queries[m])
        outs.append(out_t)
        lses.append(lse)
    attended_t = jnp.concatenate(outs, axis=1).astype(bf16)

    mixed = in_rows + dot(attended_t, out_full, 0, 0)
    inverse_mlp = rms_inverse(mixed)
    normed_mlp = (mixed * inverse_mlp * mlp_gain).astype(bf16)
    gate_pre = dot(normed_mlp, gate_full, 1, 0)
    up_pre = dot(normed_mlp, up_full, 1, 0)
    sigmoid_gate = jax.nn.sigmoid(gate_pre)
    hidden = (gate_pre * sigmoid_gate * up_pre).astype(bf16)
    layer_out = (mixed + dot(hidden, down_full, 1, 0)).astype(bf16)

    hidden_mine, hidden_theirs = halves(hidden, 1)
    hidden_other = swap_fsdp(hidden_theirs)
    down_grad = (
        dot(hidden_mine, grad_out, 0, 0) + dot(hidden_other, grad_out_other, 0, 0)
    ).astype(bf16)

    grad_hidden = dot(grad_out, down_full, 1, 1)
    grad_gate = (
        grad_hidden * up_pre * sigmoid_gate * (1.0 + gate_pre * (1.0 - sigmoid_gate))
    ).astype(bf16)
    grad_up = (grad_hidden * gate_pre * sigmoid_gate).astype(bf16)
    mlp_mine, mlp_theirs = halves(normed_mlp, 1)
    mlp_other = swap_fsdp(mlp_theirs)
    gate_grad = (
        dot(mlp_mine, grad_gate, 0, 0) + dot(mlp_other, swap_fsdp(grad_gate), 0, 0)
    ).astype(bf16)
    up_grad = (
        dot(mlp_mine, grad_up, 0, 0) + dot(mlp_other, swap_fsdp(grad_up), 0, 0)
    ).astype(bf16)
    grad_normed_mlp = dot(grad_gate, gate_full, 1, 1) + dot(grad_up, up_full, 1, 1)
    mlp_part, mlp_gain_grad = rms_back(mixed, inverse_mlp, grad_normed_mlp, mlp_gain)
    grad_mixed = grad_out.astype(f32) + mlp_part
    grad_mixed_low = grad_mixed.astype(bf16)

    grad_attended_t = dot(out_full, grad_mixed_low, 1, 1).astype(bf16)
    query_grads, keyval_grads = [], []
    for m in range(micro):
        dq_t, dfirst, dsecond = attention_backward(
            tables[m],
            firsts[m],
            seconds[m],
            queries[m],
            grad_attended_t[:, m * BLK : (m + 1) * BLK],
            outs[m],
            lses[m],
        )
        query_grads.append(dq_t)
        keyval_grads.append(scatter_blocks(dfirst, orders[0]))
        keyval_grads.append(scatter_blocks(dsecond, orders[1]))
    grad_queries_t = jnp.concatenate(query_grads, axis=1)
    grad_keyvals = jnp.concatenate(keyval_grads, axis=0)

    attended_mine, attended_theirs = halves(attended_t, 0)
    attended_other = swap_fsdp(attended_theirs)
    out_grad = dot(attended_mine, grad_mixed_low, 1, 0) + dot(
        attended_other, swap_fsdp(grad_mixed_low), 1, 0
    )
    query_grad = dot(normed_mine, grad_queries_t, 0, 1) + dot(
        normed_other, swap_fsdp(grad_queries_t), 0, 1
    )
    keyval_grad = dot(normed_mine, grad_keyvals, 0, 0) + dot(
        normed_other, swap_fsdp(grad_keyvals), 0, 0
    )
    attn_grad = jnp.concatenate([query_grad, out_grad, keyval_grad], axis=1).astype(bf16)

    normalized_gradient = dot(grad_queries_t, query_full, 0, 1) + dot(
        grad_keyvals, keyval_full, 1, 1
    )
    attn_part, attn_gain_grad = rms_back(in_rows, inverse_attn, normalized_gradient, attn_gain)
    input_grad = grad_mixed + attn_part

    def wide(first_swapped):
        bits = sum_stages(size, first_swapped)
        return [(bit, 0 if number < 2 else 1) for number, bit in enumerate(bits)]

    def tall(first_swapped):
        return [(bit, 0) for bit in sum_stages(size, first_swapped)]

    def summed(grad, stages):
        return gather_chunk(reduce_chunk(grad, stages), stages, f32)

    cut = down_grad.shape[0] // 2
    down_sum = jnp.concatenate(
        [summed(down_grad[:cut], tall(False)), summed(down_grad[cut:], tall(True))], axis=0
    )
    gate_sum = summed(gate_grad, wide(False))
    up_sum = summed(up_grad, wide(True))
    cut = attn_grad.shape[1] // 2
    attn_sum = jnp.concatenate(
        [summed(attn_grad[:, :cut], wide(False)), summed(attn_grad[:, cut:], wide(True))], axis=1
    )

    def summed_gain(vector):
        mine, theirs = halves(vector, 0)
        return sum_vector(mine + swap_fsdp(theirs))

    mlp_gain_sum = summed_gain(mlp_gain_grad)
    attn_gain_sum = summed_gain(attn_gain_grad)
    width = query_grad.shape[1]
    shape = (micro, 1, BLK, in_rows.shape[1])
    return (
        layer_out.reshape(shape),
        input_grad.reshape(shape),
        attn_gain_sum,
        attn_sum[:, :width],
        attn_sum[:, 2 * width :],
        attn_sum[:, width : 2 * width],
        mlp_gain_sum,
        gate_sum,
        up_sum,
        down_sum,
    )


def solution(mesh):
    tokens = P(None, "fsdp", "ctx", None)
    vector = P("fsdp")
    matrix = P("fsdp", None)
    return jax.shard_map(
        per_device,
        mesh=mesh,
        in_specs=(
            tokens,
            vector,
            matrix,
            matrix,
            matrix,
            vector,
            matrix,
            matrix,
            matrix,
            tokens,
            P(),
            P(),
        ),
        out_specs=(
            tokens,
            tokens,
            vector,
            matrix,
            matrix,
            matrix,
            vector,
            matrix,
            matrix,
            matrix,
        ),
        check_vma=False,
    )
```

```python
import functools

import jax
import jax.numpy as jnp
from jax import lax
from jax.experimental import pallas as pl
from jax.experimental.pallas import tpu as pltpu
from jax.sharding import PartitionSpec as P

HEADS = 15
KVH = 5
HD = 64
REP = HEADS // KVH
WINDOW = 2048
BLK = 128
HALF = BLK // 2
KVW = 2 * KVH * HD
EPS = 1e-05
NEG = -1e30
SCALE = HD ** (-0.5)
LANES = 128
GCOLS = REP * BLK

bf16 = jnp.bfloat16
f32 = jnp.float32


def dot(left, right, left_dim, right_dim):
    return lax.dot_general(
        left, right, (((left_dim,), (right_dim,)), ((), ())), preferred_element_type=f32
    )


def flip_ctx(value, bit):
    size = lax.axis_size("ctx")
    return lax.ppermute(value, "ctx", [(i, i ^ (1 << bit)) for i in range(size)])


def swap_fsdp(value):
    return lax.ppermute(value, "fsdp", [(0, 1), (1, 0)])


def tie(values):
    return lax.optimization_barrier(tuple(values))


def own_bit(bit):
    return (lax.axis_index("ctx") >> bit) & 1


def high_bits():
    return list(range(2, lax.axis_size("ctx").bit_length() - 1))


def add_low(kept, arrived):
    return (kept.astype(f32) + arrived.astype(f32)).astype(bf16)


def by_bit(bit, mine, arrived):
    low = own_bit(bit) == 0
    return jnp.where(low, mine, arrived), jnp.where(low, arrived, mine)


def in_order(bit, mine, arrived, dim):
    return jnp.concatenate(by_bit(bit, mine, arrived), axis=dim)


class GatherBlocks:
    def __init__(self, block):
        self.held = block[None]
        self.stages = high_bits()[::-1] + [None, None]
        self.halves = None

    def operands(self):
        if self.stages[0] is not None:
            return [(self.held, self.stages[0])]
        if self.halves is None:
            self.halves = [self.held[:, :HALF], self.held[:, HALF:]]
            self.bits = (1, 0)
        return list(zip(self.halves, self.bits))

    def absorb(self, arrived):
        if self.stages.pop(0) is not None:
            self.held = jnp.concatenate([self.held, arrived[0]], axis=0)
        else:
            self.halves = [
                jnp.concatenate([h, a], axis=0) for h, a in zip(self.halves, arrived)
            ]
            self.bits = (0, 1)


class ScatterBlocks:
    def __init__(self, firsts, seconds):
        self.halves = [firsts, seconds]
        self.bits = (0, 1)
        self.stages = [None, None] + high_bits()
        self.held = None

    def operands(self):
        if self.stages[0] is None:
            count = self.halves[0][0].shape[0] // 2
            sent = [jnp.stack([b[count:] for b in half]) for half in self.halves]
            return list(zip(sent, self.bits))
        if self.held is None:
            self.held = [jnp.concatenate([a, b], axis=1) for a, b in zip(*self.halves)]
        count = self.held[0].shape[0] // 2
        return [(jnp.stack([b[count:] for b in self.held]), self.stages[0])]

    def absorb(self, arrived):
        def add(blocks, sums):
            count = blocks[0].shape[0] // 2
            return [add_low(b[:count], sums[m]) for m, b in enumerate(blocks)]

        if self.stages.pop(0) is None:
            self.halves = [add(half, a) for half, a in zip(self.halves, arrived)]
            self.bits = (1, 0)
        else:
            self.held = add(self.held, arrived[0])


class Reduce:
    def __init__(self, first, second):
        self.ready = [first, second]
        self.stages = [(0, 1), (1, 0)] + high_bits()

    def cut(self, value, bit, dim):
        half = value.shape[dim] // 2
        own = own_bit(bit)
        sent = lax.dynamic_slice_in_dim(value, (1 - own) * half, half, dim)
        return lax.dynamic_slice_in_dim(value, own * half, half, dim), sent

    def operands(self):
        stage = self.stages[0]
        if isinstance(stage, tuple):
            if self.ready is None:
                self.ready = [self.cut(v, b, 0)[::-1] for v, b in zip(self.pair, stage)]
            self.kept = [r[1] for r in self.ready]
            sent = [(r[0], b) for r, b in zip(self.ready, stage)]
            self.ready = None
            return sent
        if self.pair is not None:
            kept, sent = by_bit(stage, *self.pair)
            self.pair = None
        else:
            kept, sent = self.cut(self.held, stage, 1)
        self.kept = [kept]
        return [(sent, stage)]

    def absorb(self, arrived):
        sums = [add_low(k, a) for k, a in zip(self.kept, arrived)]
        if isinstance(self.stages.pop(0), tuple):
            self.pair = sums
        else:
            self.held = sums[0]


class Spread:
    def __init__(self, chunk):
        self.held = chunk
        self.stages = high_bits()[::-1] + [(1, 0), (0, 1)]
        self.pair = None

    def operands(self):
        stage = self.stages[0]
        if isinstance(stage, tuple):
            return list(zip(self.pair, stage))
        return [(self.held, stage)]

    def absorb(self, arrived):
        stage = self.stages.pop(0)
        if isinstance(stage, tuple):
            kind = bf16 if self.stages else f32
            self.pair = [
                in_order(b, v.astype(kind), a.astype(kind), 0)
                for v, a, b in zip(self.pair, arrived, stage)
            ]
        elif stage == 2:
            self.pair = list(by_bit(stage, self.held, arrived[0]))
        else:
            self.held = in_order(stage, self.held, arrived[0], 1)


class Solo:
    def __init__(self, value):
        self.value = value
        high = [(bit, None) for bit in high_bits()]
        self.stages = [(0, True), (1, True)] + high + [(1, False), (0, False)]

    def operands(self):
        bit, cuts = self.stages[0]
        if not cuts:
            return [(self.value, bit)]
        half = self.value.shape[0] // 2
        own = own_bit(bit)
        sent = lax.dynamic_slice_in_dim(self.value, (1 - own) * half, half, 0)
        self.value = lax.dynamic_slice_in_dim(self.value, own * half, half, 0)
        return [(sent, bit)]

    def absorb(self, arrived):
        bit, cuts = self.stages.pop(0)
        if cuts is not False:
            self.value = add_low(self.value, arrived[0])
        else:
            kind = bf16 if self.stages else f32
            self.value = in_order(bit, self.value.astype(kind), arrived[0].astype(kind), 0)


class Rounds:
    def __init__(self):
        self.flying = {}

    def begin(self, *jobs):
        for job in jobs:
            self.flying[job] = [flip_ctx(v, b) for v, b in job.operands()]

    def end(self, jobs, values=()):
        values = list(values)
        arrived = [a for job in jobs for a in self.flying[job]]
        tied = tie(values + arrived)
        rest = list(tied[len(values) :])
        for job in jobs:
            count = len(self.flying.pop(job))
            job.absorb(rest[:count])
            rest = rest[count:]
        return tied[: len(values)]


def key_tile(first_ref, second_ref, places, unit):
    lanes = pl.ds((unit // 2) * LANES, LANES)
    parts = []
    for first, second in places:
        parts += [first_ref[first, :, lanes], second_ref[second, :, lanes]]
    return jnp.concatenate(parts, axis=0)


def heads_t(rows_t, group, unit):
    parts = [
        rows_t[(group * REP + r) * HD : (group * REP + r + 1) * HD, :] for r in range(REP)
    ]
    block = jnp.concatenate(parts, axis=1)
    zero = jnp.zeros_like(block)
    return jnp.concatenate([zero, block] if unit % 2 else [block, zero], axis=0)


def half_rows(tile_t, unit):
    return tile_t[(unit % 2) * HD : (unit % 2 + 1) * HD, :]


def seen_blocks(bits, which, ids, lengths, slots):
    me, shard = ids[0], ids[1]

    def look(j, own):
        return jnp.where(slots[which, shard, j] == me, j, own)

    own = lax.fori_loop(0, slots.shape[2], look, jnp.int32(0))
    end = jnp.int32(0)
    start = jnp.int32(0)
    for i in range(lengths.shape[2]):
        end = end + lengths[which, shard, i]
        start = jnp.where(end <= own, end, start)
    lowest = jnp.maximum(start, own - WINDOW // BLK)

    def places(index):
        relative = slots[which, shard, jnp.maximum(own - index, 0)] ^ me
        high = jnp.int32(0)
        for position, bit in enumerate(range(bits - 1, 1, -1)):
            high = high | (((relative >> bit) & 1) << position)
        one = (relative & 1) << (bits - 1)
        two = ((relative >> 1) & 1) << (bits - 2)
        swapped = ((relative & 1) << (bits - 2)) | (((relative >> 1) & 1) << (bits - 1))
        return high | one | two, high | swapped

    return own - lowest + 1, places


def pair_mask(far, count, index):
    key = lax.broadcasted_iota(jnp.int32, (BLK, GCOLS), 0)
    query = lax.broadcasted_iota(jnp.int32, (BLK, GCOLS), 1) & (BLK - 1)
    ahead = key - query
    masks = []
    for i in (index, index + 1):
        most = jnp.where(i < count, i * BLK, -2 * BLK)
        mask = ahead <= most
        if far:
            mask = mask & (ahead > i * BLK - WINDOW)
        masks.append(mask)
    return jnp.concatenate(masks, axis=0)


def forward_kernel(
    far, bits, which, ids, lengths, slots, first_ref, second_ref, query_ref, out_ref, lse_ref, pad_ref
):
    count, places = seen_blocks(bits, which, ids, lengths, slots)
    queries = query_ref[...]
    for group in range(KVH):
        pad_ref[:, group * GCOLS : (group + 1) * GCOLS] = heads_t(queries, group, group)

    for group in range(KVH):
        columns = slice(group * GCOLS, (group + 1) * GCOLS)
        value_unit = KVH + group

        def step(pair, carried):
            high, total, acc = carried
            index = 2 * pair
            held = (places(index), places(index + 1))
            keys = key_tile(first_ref, second_ref, held, group)
            values = key_tile(first_ref, second_ref, held, value_unit)
            scores = dot(keys, pad_ref[:, columns], 1, 0) * SCALE
            scores = jnp.where(pair_mask(far, count, index), scores, NEG)
            new_high = jnp.maximum(high, jnp.max(scores, axis=0, keepdims=True))
            weights = jnp.exp(scores - new_high)
            fade = jnp.exp(high - new_high)
            total = total * fade + jnp.sum(weights, axis=0, keepdims=True)
            values_t = half_rows(values.T, value_unit)
            acc = acc * fade + dot(values_t, weights.astype(bf16), 1, 0)
            return (new_high, total, acc)

        start = (
            jnp.full((1, GCOLS), NEG, f32),
            jnp.zeros((1, GCOLS), f32),
            jnp.zeros((HD, GCOLS), f32),
        )
        high, total, acc = lax.fori_loop(0, (count + 1) // 2, step, start)
        acc = acc / total
        for r in range(REP):
            head = group * REP + r
            out_ref[head * HD : (head + 1) * HD, :] = acc[:, r * BLK : (r + 1) * BLK]
        lse_ref[:, columns] = high + jnp.log(total)


def backward_kernel(
    far,
    bits,
    which,
    ids,
    lengths,
    slots,
    first_ref,
    second_ref,
    query_ref,
    grad_ref,
    out_ref,
    lse_ref,
    dq_ref,
    dfirst_ref,
    dsecond_ref,
    pad_ref,
    right_ref,
    delta_ref,
    left_ref,
    acc_ref,
):
    count, places = seen_blocks(bits, which, ids, lengths, slots)
    queries = query_ref[...]
    grads = grad_ref[...]
    product = grads.astype(f32) * out_ref[...]
    for head in range(HEADS):
        delta_ref[:, head * BLK : (head + 1) * BLK] = jnp.sum(
            product[head * HD : (head + 1) * HD, :], axis=0, keepdims=True
        )
    for unit in range(2 * KVH):
        padded = heads_t(queries if unit < KVH else grads, unit % KVH, unit)
        rows = slice(unit * GCOLS, (unit + 1) * GCOLS)
        pad_ref[:, rows] = padded
        right_ref[rows, :] = padded.T
    dfirst_ref[...] = jnp.zeros_like(dfirst_ref)
    dsecond_ref[...] = jnp.zeros_like(dsecond_ref)
    acc_ref[...] = jnp.zeros_like(acc_ref)

    @pl.loop(0, (count + 1) // 2)
    def _(pair):
        index = 2 * pair
        held = (places(index), places(index + 1))
        mask = pair_mask(far, count, index)
        for group in range(KVH):
            value_unit = KVH + group
            columns = slice(group * GCOLS, (group + 1) * GCOLS)
            value_columns = slice(value_unit * GCOLS, (value_unit + 1) * GCOLS)
            keys = key_tile(first_ref, second_ref, held, group)
            values = key_tile(first_ref, second_ref, held, value_unit)
            scores = dot(keys, pad_ref[:, columns], 1, 0) * SCALE
            probs = jnp.where(mask, jnp.exp(scores - lse_ref[:, columns]), 0.0)
            grad_probs = dot(values, pad_ref[:, value_columns], 1, 0)
            grad_scores = (probs * (grad_probs - delta_ref[:, columns])).astype(bf16)
            left_ref[:, columns] = grad_scores
            left_ref[:, value_columns] = probs.astype(bf16)
            keys_t = half_rows(keys.T, group)
            acc_ref[:, columns] += dot(keys_t, grad_scores, 1, 0)
        for tile in range(KVH):
            rows = slice(2 * tile * GCOLS, 2 * (tile + 1) * GCOLS)
            lanes = slice(tile * LANES, (tile + 1) * LANES)
            block = dot(left_ref[:, rows], right_ref[rows, :], 1, 0)
            lane = lax.broadcasted_iota(jnp.int32, (1, LANES), 1) + tile * LANES
            block = (block * jnp.where(lane < KVH * HD, SCALE, 1.0)).astype(bf16)
            first, second = held[0]
            dfirst_ref[first, :, lanes] = block[:HALF]
            dsecond_ref[second, :, lanes] = block[HALF:BLK]

            @pl.when(index + 1 < count)
            def _():
                first, second = held[1]
                dfirst_ref[first, :, lanes] = block[BLK : BLK + HALF]
                dsecond_ref[second, :, lanes] = block[BLK + HALF :]

    for head in range(HEADS):
        columns = slice(head * BLK, (head + 1) * BLK)
        dq_ref[head * HD : (head + 1) * HD, :] = (acc_ref[:, columns] * SCALE).astype(bf16)


VMEM_SPEC = pl.BlockSpec(memory_space=pltpu.VMEM)
SMEM_SPEC = pl.BlockSpec(memory_space=pltpu.SMEM)


def attention_forward(which, tables, first, second, queries_t):
    steps = first.shape[0]
    return pl.pallas_call(
        functools.partial(
            forward_kernel, steps > WINDOW // BLK, steps.bit_length() - 1, which
        ),
        out_shape=(
            jax.ShapeDtypeStruct((HEADS * HD, BLK), f32),
            jax.ShapeDtypeStruct((1, HEADS * BLK), f32),
        ),
        in_specs=[SMEM_SPEC] * 3 + [VMEM_SPEC] * 3,
        out_specs=(VMEM_SPEC,) * 2,
        scratch_shapes=[pltpu.VMEM((LANES, HEADS * BLK), bf16)],
        compiler_params=pltpu.CompilerParams(vmem_limit_bytes=40 << 20),
        cost_estimate=pl.CostEstimate(
            flops=4 * HEADS * HD * BLK * BLK * 8,
            bytes_accessed=first.size * 4,
            transcendentals=HEADS * BLK * BLK * 8,
        ),
        name="attention_forward",
    )(*tables, first, second, queries_t)


def attention_backward(which, tables, first, second, queries_t, grads_t, out_t, lse):
    steps = first.shape[0]
    return pl.pallas_call(
        functools.partial(
            backward_kernel, steps > WINDOW // BLK, steps.bit_length() - 1, which
        ),
        out_shape=(
            jax.ShapeDtypeStruct((HEADS * HD, BLK), bf16),
            jax.ShapeDtypeStruct(first.shape, bf16),
            jax.ShapeDtypeStruct(second.shape, bf16),
        ),
        in_specs=[SMEM_SPEC] * 3 + [VMEM_SPEC] * 6,
        out_specs=(VMEM_SPEC,) * 3,
        scratch_shapes=[
            pltpu.VMEM((LANES, 2 * KVH * GCOLS), bf16),
            pltpu.VMEM((2 * KVH * GCOLS, LANES), bf16),
            pltpu.VMEM((1, HEADS * BLK), f32),
            pltpu.VMEM((2 * BLK, 2 * KVH * GCOLS), bf16),
            pltpu.VMEM((HD, HEADS * BLK), f32),
        ],
        compiler_params=pltpu.CompilerParams(vmem_limit_bytes=48 << 20),
        cost_estimate=pl.CostEstimate(
            flops=10 * HEADS * HD * BLK * BLK * 8,
            bytes_accessed=first.size * 8,
            transcendentals=HEADS * BLK * BLK * 8,
        ),
        name="attention_backward",
    )(*tables, first, second, queries_t, grads_t, out_t, lse)


def block_kernel(
    x_ref,
    cot_ref,
    att_ref,
    out_w_ref,
    gain_ref,
    gate_w_ref,
    up_w_ref,
    down_w_ref,
    hidden_ref,
    grads_ref,
    normed_ref,
    layer_ref,
    grad_mixed_ref,
    grad_low_ref,
    grad_att_ref,
    gain_grad_ref,
    mixed,
    normed,
    cot,
    grad_normed,
    layer,
):
    step = pl.program_id(0)

    @pl.when(step == 0)
    def _():
        cot[...] = cot_ref[...].T
        values = x_ref[...].astype(f32).T + dot(att_ref[...], out_w_ref[...], 0, 0)
        mixed[...] = values
        inverse = lax.rsqrt(jnp.mean(values * values, axis=-1, keepdims=True) + EPS)
        low = (values * inverse * gain_ref[...]).astype(bf16)
        normed[...] = low
        normed_ref[...] = low.T
        layer[...] = values
        grad_normed[...] = jnp.zeros_like(grad_normed)

    grad_hidden = dot(cot[...], down_w_ref[...], 1, 0)
    gate = dot(normed[...], gate_w_ref[...], 1, 0)
    up = dot(normed[...], up_w_ref[...], 1, 0)
    sigmoid = jax.nn.sigmoid(gate)
    silu = gate * sigmoid
    hidden = (silu * up).astype(bf16)
    grad_gate = (grad_hidden * up * sigmoid * (1.0 + gate * (1.0 - sigmoid))).astype(bf16)
    grad_up = (grad_hidden * silu).astype(bf16)
    hidden_ref[...] = hidden
    grads_ref[0] = grad_gate
    grads_ref[1] = grad_up
    layer[...] += dot(hidden, down_w_ref[...], 1, 1)
    grad_normed[...] += dot(grad_gate, gate_w_ref[...], 1, 1) + dot(
        grad_up, up_w_ref[...], 1, 1
    )

    @pl.when(step == pl.num_programs(0) - 1)
    def _():
        values = mixed[...]
        layer_ref[...] = layer[...].astype(bf16).T
        inverse = lax.rsqrt(jnp.mean(values * values, axis=-1, keepdims=True) + EPS)
        grads = grad_normed[...]
        gain_grad_ref[...] = jnp.sum(grads * values * inverse, axis=0, keepdims=True)
        scaled = grads * gain_ref[...]
        cubed = inverse * inverse * inverse
        back = inverse * scaled - values * cubed * jnp.mean(
            scaled * values, axis=-1, keepdims=True
        )
        grad_mixed = cot[...].astype(f32) + back
        low = grad_mixed.astype(bf16)
        grad_mixed_ref[...] = grad_mixed.T
        grad_low_ref[...] = low
        grad_att_ref[...] = dot(out_w_ref[...], low, 1, 1).astype(bf16)


def feed_forward(x_t, cot_t, attended_t, out_w, gain, gate_w, up_w, down_w_t):
    width, rows = x_t.shape
    inner = gate_w.shape[1]
    tile = 256

    def fixed(shape):
        return pl.BlockSpec(shape, lambda i: (0,) * len(shape))

    weight = pl.BlockSpec((width, tile), lambda i: (0, i))
    wide = (width, rows)
    return pl.pallas_call(
        block_kernel,
        grid=(inner // tile,),
        in_specs=[fixed(wide)] * 3
        + [fixed(out_w.shape), fixed((1, width)), weight, weight, weight],
        out_specs=(
            pl.BlockSpec((rows, tile), lambda i: (0, i)),
            pl.BlockSpec((2, rows, tile), lambda i: (0, 0, i)),
            fixed(wide),
            fixed(wide),
            fixed(wide),
            fixed((rows, width)),
            fixed(wide),
            fixed((1, width)),
        ),
        out_shape=(
            jax.ShapeDtypeStruct((rows, inner), bf16),
            jax.ShapeDtypeStruct((2, rows, inner), bf16),
            jax.ShapeDtypeStruct(wide, bf16),
            jax.ShapeDtypeStruct(wide, bf16),
            jax.ShapeDtypeStruct(wide, f32),
            jax.ShapeDtypeStruct((rows, width), bf16),
            jax.ShapeDtypeStruct(wide, bf16),
            jax.ShapeDtypeStruct((1, width), f32),
        ),
        scratch_shapes=[
            pltpu.VMEM((rows, width), f32),
            pltpu.VMEM((rows, width), bf16),
            pltpu.VMEM((rows, width), bf16),
            pltpu.VMEM((rows, width), f32),
            pltpu.VMEM((rows, width), f32),
        ],
        compiler_params=pltpu.CompilerParams(vmem_limit_bytes=40 << 20),
        cost_estimate=pl.CostEstimate(
            flops=12 * rows * width * inner,
            bytes_accessed=8 * width * inner,
            transcendentals=rows * inner,
        ),
        name="feed_forward",
    )(x_t, cot_t, attended_t, out_w, gain, gate_w, up_w, down_w_t)


def pair_grad_kernel(sides, ids, *refs):
    count = len(sides)
    ins, outs = refs[: 4 * count], refs[4 * count :]
    for number, (bit, base_row, by_shard, right_t) in enumerate(sides):
        left, left_other, right, right_other = ins[4 * number : 4 * number + 4]
        sent, kept = outs[2 * number : 2 * number + 2]
        rows = sent.shape[0]
        own = (ids[0] >> bit) & 1
        dim = 1 if right_t else 0
        mine = base_row + (ids[1] * (2 * rows) if by_shard else 0)
        pair = ((sent, 1 - own), (kept, own))
        for out, place in pair:
            near = left[pl.ds(pl.multiple_of(mine + place * rows, 8), rows), :]
            base = base_row if not by_shard else 0
            far = left_other[pl.ds(pl.multiple_of(base + place * rows, 8), rows), :]
            value = dot(near, right[...].reshape(right.shape[-2:]), 1, dim) + dot(
                far, right_other[...].reshape(right_other.shape[-2:]), 1, dim
            )
            out[...] = value.astype(bf16)


def pair_grad(name, ids, sides, operands, right_specs, tiles, rows, columns):
    tile = columns // tiles
    specs = []
    for (left, left_other, right, right_other), (spec, spec_other) in zip(operands, right_specs):
        specs += [
            pl.BlockSpec(left.shape, lambda i, ids: (0, 0)),
            pl.BlockSpec(left_other.shape, lambda i, ids: (0, 0)),
            spec,
            spec_other,
        ]
    out = pl.BlockSpec((rows, tile), lambda i, ids: (0, i))
    return pl.pallas_call(
        functools.partial(pair_grad_kernel, sides),
        grid_spec=pltpu.PrefetchScalarGridSpec(
            num_scalar_prefetch=1,
            grid=(tiles,),
            in_specs=specs,
            out_specs=[out] * (2 * len(sides)),
        ),
        out_shape=[jax.ShapeDtypeStruct((rows, columns), bf16)] * (2 * len(sides)),
        compiler_params=pltpu.CompilerParams(vmem_limit_bytes=40 << 20),
        cost_estimate=pl.CostEstimate(
            flops=4 * len(sides) * rows * columns * 512,
            bytes_accessed=8 * rows * columns,
            transcendentals=0,
        ),
        name=name,
    )(ids, *[o for group in operands for o in group])


def per_device(
    inputs,
    gain_attn,
    w_query,
    w_keyval,
    w_out,
    gain_mlp,
    w_gate,
    w_up,
    w_down,
    cotangent,
    seq_blocks,
    block_slots,
):
    micro = inputs.shape[0]
    shard = lax.axis_index("fsdp")
    is_low = shard == 0
    rounds = Rounds()

    def joined(part, other):
        return jnp.concatenate(
            [jnp.where(is_low, part, other), jnp.where(is_low, other, part)], axis=0
        )

    def whole(part):
        return lax.all_gather(part, "fsdp", axis=0, tiled=True)

    def theirs(value, dim):
        half = value.shape[dim] // 2
        return lax.dynamic_slice_in_dim(value, (1 - shard) * half, half, dim)

    def tokens_last(value):
        return jnp.concatenate([value[m, 0].T for m in range(micro)], axis=1)

    out_full = whole(w_out)
    gate_full = whole(w_gate)
    up_full = whole(w_up)
    down_full_t = whole(w_down).T

    attn_gain = joined(gain_attn, swap_fsdp(gain_attn)).astype(f32)[:, None]
    keyval_full = joined(w_keyval, swap_fsdp(w_keyval))
    x_t = tokens_last(inputs)
    in_t = x_t.astype(f32)
    inverse_attn = lax.rsqrt(jnp.mean(in_t * in_t, axis=0, keepdims=True) + EPS)
    normed_t = (in_t * inverse_attn * attn_gain).astype(bf16)
    keyvals = dot(normed_t, keyval_full, 0, 0).astype(bf16)
    gathers = [GatherBlocks(keyvals[m * BLK : (m + 1) * BLK]) for m in range(micro)]

    rounds.begin(gathers[0])
    (w_query, gain_mlp, cotangent, normed_t) = rounds.end(
        gathers[:1], (w_query, gain_mlp, cotangent, normed_t)
    )
    rounds.begin(*gathers[:2])
    query_other, gain_other = swap_fsdp(w_query), swap_fsdp(gain_mlp)
    cot_t = tokens_last(cotangent)
    (query_other, gain_other, cot_t) = rounds.end(
        gathers[:2], (query_other, gain_other, cot_t)
    )
    for step in range(len(gathers[0].stages)):
        rounds.begin(*[g for g in gathers if len(g.stages) > 2 or g is gathers[0]])
        if step == 0:
            query_full = joined(w_query, query_other)
            mlp_gain = joined(gain_mlp, gain_other).astype(f32)[None]
            queries_t = dot(query_full, normed_t, 0, 0).astype(bf16)
            normed_theirs = theirs(normed_t, 0)
            (queries_t, mlp_gain, normed_theirs) = rounds.end(
                list(rounds.flying), (queries_t, mlp_gain, normed_theirs)
            )
        elif step == 1:
            normed_other = swap_fsdp(normed_theirs)
            cot_other = swap_fsdp(cot_t)
            (normed_other, cot_other) = rounds.end(
                list(rounds.flying), (normed_other, cot_other)
            )
        else:
            rounds.end(list(rounds.flying))
    queries = [queries_t[:, m * BLK : (m + 1) * BLK] for m in range(micro)]
    ids = jnp.stack([lax.axis_index("ctx"), shard]).astype(jnp.int32)
    tables = (ids, seq_blocks, block_slots)

    rounds.begin(gathers[1])
    first = attention_forward(0, tables, *gathers[0].halves, queries[0])
    first = rounds.end([gathers[1]], first)
    rounds.begin(gathers[1])
    rounds.end([gathers[1]])
    second = attention_forward(1, tables, *gathers[1].halves, queries[1])
    outs, lses = zip(first, second)
    attended_t = jnp.concatenate(outs, axis=1).astype(bf16)

    attended_other = swap_fsdp(theirs(attended_t, 0))
    (
        hidden,
        grad_inner,
        normed_mlp_t,
        layer_out_t,
        grad_mixed_t,
        grad_mixed_low,
        grad_attended_t,
        mlp_gain_grad,
    ) = feed_forward(
        x_t, cot_t, attended_t, out_full, mlp_gain, gate_full, up_full, down_full_t
    )
    hidden_other = swap_fsdp(theirs(hidden, 1))
    inner_other = swap_fsdp(grad_inner)
    mlp_other = swap_fsdp(theirs(normed_mlp_t, 0))

    part = hidden_other.shape[1]
    width = cot_t.shape[0]
    rows = width // 4
    tokens = hidden.shape[0]
    tiles = 2
    near = pl.BlockSpec((tokens, part // tiles), lambda i, ids: (0, ids[1] * tiles + i))
    far = pl.BlockSpec((tokens, part // tiles), lambda i, ids: (0, i))
    down_parts = pair_grad(
        "down_grad",
        ids,
        ((0, 0, False, False), (1, 2 * rows, False, False)),
        ((cot_t, cot_other, hidden, hidden_other),) * 2,
        ((near, far),) * 2,
        tiles,
        rows,
        part,
    )
    down_job = Reduce(down_parts[:2], down_parts[2:])

    rounds.begin(down_job)
    inner = hidden.shape[1]
    tiles = 5
    specs = [
        pl.BlockSpec((1, tokens, inner // tiles), lambda i, ids, n=n: (n, 0, i)) for n in range(2)
    ]
    inner_parts = pair_grad(
        "inner_grad",
        ids,
        ((0, 0, True, False), (1, 0, True, False)),
        ((normed_mlp_t, mlp_other, grad_inner, inner_other),) * 2,
        [(spec, spec) for spec in specs],
        tiles,
        rows,
        inner,
    )
    inner_parts = rounds.end([down_job], inner_parts)
    mlp_job = Reduce(inner_parts[:2], inner_parts[2:])

    def attention_back(m):
        return attention_backward(
            m,
            tables,
            *gathers[m].halves,
            queries[m],
            grad_attended_t[:, m * BLK : (m + 1) * BLK],
            outs[m],
            lses[m],
        )

    rounds.begin(mlp_job, down_job)
    back_first = attention_back(0)
    back_first = rounds.end([down_job], back_first)
    rounds.begin(down_job)
    mixed_other = swap_fsdp(grad_mixed_low)
    (mixed_other,) = rounds.end([down_job], (mixed_other,))
    while down_job.stages:
        rounds.begin(down_job)
        rounds.end([down_job])
    down_spread = Spread(down_job.held)
    rounds.begin(down_spread)
    back_second = attention_back(1)
    back_second = rounds.end([down_spread, mlp_job], back_second)
    key_job = ScatterBlocks(*zip(back_first[1:], back_second[1:]))
    grad_queries_t = jnp.concatenate([back_first[0], back_second[0]], axis=1)

    rounds.begin(mlp_job, down_spread)
    queries_other = swap_fsdp(grad_queries_t)
    (queries_other,) = rounds.end([mlp_job, down_spread], (queries_other,))
    rounds.begin(key_job, mlp_job)
    half = rows * 2
    flat = pl.BlockSpec((width, tokens), lambda i, ids: (0, 0))
    tall = pl.BlockSpec((tokens, width), lambda i, ids: (0, 0))
    query_parts = pair_grad(
        "query_grad",
        ids,
        ((0, 0, True, True), (1, 0, True, False)),
        (
            (normed_t, normed_other, grad_queries_t, queries_other),
            (attended_t, attended_other, grad_mixed_low, mixed_other),
        ),
        ((flat, flat), (tall, tall)),
        1,
        rows,
        width,
    )
    query_parts = rounds.end([mlp_job], query_parts)
    query_job = Reduce(query_parts[:2], query_parts[2:])
    while mlp_job.stages:
        rounds.begin(mlp_job)
        rounds.end([mlp_job] if len(mlp_job.stages) > 1 else [mlp_job, key_job])
    mlp_spread = Spread(mlp_job.held)
    rounds.begin(key_job, mlp_spread)
    grad_normed_t = dot(query_full, grad_queries_t, 1, 0)
    (grad_normed_t,) = rounds.end([key_job, mlp_spread], (grad_normed_t,))
    while len(mlp_spread.stages) > 3:
        rounds.begin(mlp_spread)
        rounds.end([mlp_spread])
    while len(down_spread.stages) > 2:
        rounds.begin(down_spread)
        rounds.end([down_spread])
    rounds.begin(key_job, query_job)
    rounds.end([key_job, query_job])
    rounds.begin(key_job, query_job, down_spread)
    rounds.end([key_job, query_job, down_spread])
    while key_job.stages:
        rounds.begin(key_job)
        rounds.end([key_job])
    grad_keyvals = jnp.concatenate([b[0] for b in key_job.held], axis=0)

    rounds.begin(mlp_spread, query_job, down_spread)
    keyvals_other = swap_fsdp(grad_keyvals)
    grad_normed_t = grad_normed_t + dot(keyval_full, grad_keyvals, 1, 1)
    attn_gain_grad = jnp.sum(grad_normed_t * in_t * inverse_attn, axis=1)
    scaled = grad_normed_t * attn_gain
    cubed = inverse_attn * inverse_attn * inverse_attn
    input_grad_t = (
        grad_mixed_t
        + inverse_attn * scaled
        - in_t * cubed * jnp.mean(scaled * in_t, axis=0, keepdims=True)
    )
    gains = jnp.stack([attn_gain_grad, mlp_gain_grad[0]], axis=1)
    gains_theirs = theirs(gains, 0)
    normed_mine = lax.dynamic_slice_in_dim(normed_t, shard * half, half, 0)
    keyval_grad = dot(normed_mine, grad_keyvals, 1, 0) + dot(normed_other, keyvals_other, 1, 0)
    gains_mine = lax.dynamic_slice_in_dim(gains, shard * half, half, 0) + swap_fsdp(gains_theirs)
    pad = jnp.zeros((half, LANES - 2), bf16)
    last = jnp.concatenate([keyval_grad.astype(bf16), gains_mine.astype(bf16), pad], axis=1)
    (last, input_grad_t) = rounds.end(
        [mlp_spread, query_job, down_spread], (last, input_grad_t)
    )
    last_job = Solo(last)
    rounds.begin(last_job, mlp_spread, query_job)
    down_sum = jnp.concatenate(down_spread.pair, axis=0)
    (down_sum,) = rounds.end([last_job, mlp_spread, query_job], (down_sum,))
    while query_job.stages:
        rounds.begin(query_job)
        rounds.end([query_job])
    query_spread = Spread(query_job.held)
    rounds.begin(mlp_spread, query_spread, last_job)
    while last_job.stages:
        ahead = len(last_job.stages)
        rounds.end([j for j in rounds.flying if j is not mlp_spread or ahead == 2])
        more = [last_job]
        if len(query_spread.stages) > 2 or ahead <= 3:
            more.append(query_spread)
        rounds.begin(*[j for j in more if j.stages])
    rounds.end(list(rounds.flying))
    while query_spread.stages:
        rounds.begin(query_spread)
        rounds.end([query_spread])

    def by_token(value_t):
        parts = [value_t[:, m * BLK : (m + 1) * BLK].T[None] for m in range(micro)]
        return jnp.stack(parts)

    columns = keyval_grad.shape[1]
    return (
        by_token(layer_out_t),
        by_token(input_grad_t),
        last_job.value[:, columns],
        query_spread.pair[0],
        last_job.value[:, :columns],
        query_spread.pair[1],
        last_job.value[:, columns + 1],
        mlp_spread.pair[0],
        mlp_spread.pair[1],
        down_sum.T,
    )


def solution(mesh):
    tokens = P(None, "fsdp", "ctx", None)
    vector = P("fsdp")
    matrix = P("fsdp", None)
    return jax.shard_map(
        per_device,
        mesh=mesh,
        in_specs=(
            tokens,
            vector,
            matrix,
            matrix,
            matrix,
            vector,
            matrix,
            matrix,
            matrix,
            tokens,
            P(),
            P(),
        ),
        out_specs=(
            tokens,
            tokens,
            vector,
            matrix,
            matrix,
            matrix,
            vector,
            matrix,
            matrix,
            matrix,
        ),
        check_vma=False,
    )
```

```python
import functools

import jax
import jax.numpy as jnp
from jax import lax
from jax.experimental import pallas as pl
from jax.experimental.pallas import tpu as pltpu
from jax.sharding import PartitionSpec as P

HEADS = 15
KVH = 5
HD = 64
REP = HEADS // KVH
WINDOW = 2048
BLK = 128
HALF = BLK // 2
KVW = 2 * KVH * HD
EPS = 1e-05
NEG = -1e30
SCALE = HD ** (-0.5)
LANES = 128
GCOLS = REP * BLK

bf16 = jnp.bfloat16
f32 = jnp.float32


def dot(left, right, left_dim, right_dim):
    return lax.dot_general(
        left, right, (((left_dim,), (right_dim,)), ((), ())), preferred_element_type=f32
    )


def flip_ctx(value, bit):
    size = lax.axis_size("ctx")
    return lax.ppermute(value, "ctx", [(i, i ^ (1 << bit)) for i in range(size)])


def swap_fsdp(value):
    return lax.ppermute(value, "fsdp", [(0, 1), (1, 0)])


def tie(values):
    return lax.optimization_barrier(tuple(values))


def own_bit(bit):
    return (lax.axis_index("ctx") >> bit) & 1


def high_bits():
    return list(range(2, lax.axis_size("ctx").bit_length() - 1))


def add_low(kept, arrived):
    return (kept.astype(f32) + arrived.astype(f32)).astype(bf16)


def by_bit(bit, mine, arrived):
    low = own_bit(bit) == 0
    return jnp.where(low, mine, arrived), jnp.where(low, arrived, mine)


def in_order(bit, mine, arrived, dim):
    return jnp.concatenate(by_bit(bit, mine, arrived), axis=dim)


class GatherBlocks:
    def __init__(self, block):
        self.held = block[None]
        self.stages = high_bits()[::-1] + [None, None]
        self.halves = None

    def operands(self):
        if self.stages[0] is not None:
            return [self.held], [self.stages[0]]
        if self.halves is None:
            self.halves = [self.held[:, :HALF], self.held[:, HALF:]]
            self.bits = (1, 0)
        return self.halves, self.bits

    def absorb(self, arrived):
        if self.stages.pop(0) is not None:
            self.held = jnp.concatenate([self.held, arrived[0]], axis=0)
        else:
            self.halves = [
                jnp.concatenate([h, a], axis=0) for h, a in zip(self.halves, arrived)
            ]
            self.bits = (0, 1)


class ScatterBlocks:
    def __init__(self, first, second):
        self.halves = [first, second]
        self.bits = (0, 1)
        self.stages = [None, None] + high_bits()
        self.held = None

    def operands(self):
        if self.stages[0] is None:
            count = self.halves[0].shape[0] // 2
            return [half[count:] for half in self.halves], self.bits
        if self.held is None:
            self.held = jnp.concatenate(self.halves, axis=1)
        count = self.held.shape[0] // 2
        return [self.held[count:]], [self.stages[0]]

    def absorb(self, arrived):
        def add(blocks, sums):
            return add_low(blocks[: blocks.shape[0] // 2], sums)

        if self.stages.pop(0) is None:
            self.halves = [add(half, a) for half, a in zip(self.halves, arrived)]
            self.bits = (1, 0)
        else:
            self.held = add(self.held, arrived[0])


def cut(value, bit, dim):
    half = value.shape[dim] // 2
    own = own_bit(bit)
    sent = lax.dynamic_slice_in_dim(value, (1 - own) * half, half, dim)
    return lax.dynamic_slice_in_dim(value, own * half, half, dim), sent


class Reduce:
    def __init__(self, parts, dims):
        self.first = [parts[0], parts[2]]
        self.kept = [parts[1], parts[3]]
        self.dims = dims
        self.stages = [(0, 1), (1, 0)] + high_bits()

    def operands(self):
        stage = self.stages[0]
        if self.first is not None:
            sent, self.first = self.first, None
        elif isinstance(stage, tuple):
            parts = [cut(v, b, self.dims[0]) for v, b in zip(self.pair, stage)]
            self.kept = [p[0] for p in parts]
            sent = [p[1] for p in parts]
        else:
            if self.pair is not None:
                kept, out = by_bit(stage, *self.pair)
                self.pair = None
            else:
                kept, out = cut(self.held, stage, self.dims[1])
            self.kept, sent, stage = [kept], [out], [stage]
        return sent, stage

    def absorb(self, arrived):
        sums = [add_low(k, a) for k, a in zip(self.kept, arrived)]
        if isinstance(self.stages.pop(0), tuple):
            self.pair = sums
        else:
            self.held = sums[0]


class Spread:
    def __init__(self, job):
        self.held = job.held
        self.dims = job.dims
        self.stages = high_bits()[::-1] + [(1, 0), (0, 1)]
        self.pair = None

    def operands(self):
        stage = self.stages[0]
        if isinstance(stage, tuple):
            return self.pair, stage
        return [self.held], [stage]

    def absorb(self, arrived):
        stage = self.stages.pop(0)
        if isinstance(stage, tuple):
            kind, dim = (bf16, self.dims[0]) if self.stages else (f32, 0)
            self.pair = [
                in_order(b, v.astype(kind), a.astype(kind), dim)
                for v, a, b in zip(self.pair, arrived, stage)
            ]
        elif stage == 2:
            self.pair = list(by_bit(stage, self.held, arrived[0]))
        else:
            self.held = in_order(stage, self.held, arrived[0], self.dims[1])


class Solo:
    def __init__(self, value):
        self.value = value
        high = [(bit, None) for bit in high_bits()]
        self.stages = [(0, True), (1, True)] + high + [(1, False), (0, False)]

    def operands(self):
        bit, cuts = self.stages[0]
        if not cuts:
            return [self.value], [bit]
        self.value, sent = cut(self.value, bit, 0)
        return [sent], [bit]

    def absorb(self, arrived):
        bit, cuts = self.stages.pop(0)
        if cuts is not False:
            self.value = add_low(self.value, arrived[0])
        else:
            kind = bf16 if self.stages else f32
            self.value = in_order(bit, self.value.astype(kind), arrived[0].astype(kind), 0)


class Rounds:
    def __init__(self):
        self.flying = {}
        self.ready = {}
        self.fresh = []

    def begin(self, *jobs):
        for job in jobs:
            arrays, bits = self.ready.pop(job, None) or job.operands()
            self.flying[job] = [flip_ctx(v, b) for v, b in zip(arrays, bits)]

    def prepare(self, *jobs):
        for job in jobs:
            self.ready[job] = job.operands()
            self.fresh.append(job)

    def end(self, jobs, *values):
        ahead = [job for job in self.fresh if job in self.ready]
        self.fresh = []
        arrays = [a for job in jobs for a in self.flying[job]]
        sent = [a for job in ahead for a in self.ready[job][0]]
        rest = list(tie([*values, *arrays, *sent]))
        values, rest = rest[: len(values)], rest[len(values) :]
        for job in jobs:
            count = len(self.flying.pop(job))
            job.absorb(rest[:count])
            rest = rest[count:]
        for job in ahead:
            count = len(self.ready[job][0])
            self.ready[job] = (rest[:count], self.ready[job][1])
            rest = rest[count:]
        return values

    def run(self, job, left):
        while len(job.stages) > left:
            self.begin(job)
            self.end([job])


def key_tile(first_ref, second_ref, places, unit):
    lanes = pl.ds((unit // 2) * LANES, LANES)
    parts = []
    for first, second in places:
        parts += [first_ref[first, :, lanes], second_ref[second, :, lanes]]
    return jnp.concatenate(parts, axis=0)


def heads_t(rows_t, group, unit):
    parts = [
        rows_t[(group * REP + r) * HD : (group * REP + r + 1) * HD, :] for r in range(REP)
    ]
    block = jnp.concatenate(parts, axis=1)
    zero = jnp.zeros_like(block)
    return jnp.concatenate([zero, block] if unit % 2 else [block, zero], axis=0)


def half_rows(tile_t, unit):
    return tile_t[(unit % 2) * HD : (unit % 2 + 1) * HD, :]


def seen_blocks(bits, which, ids, lengths, slots):
    me, shard = ids[0], ids[1]

    def look(j, own):
        return jnp.where(slots[which, shard, j] == me, j, own)

    own = lax.fori_loop(0, slots.shape[2], look, jnp.int32(0))
    end = jnp.int32(0)
    start = jnp.int32(0)
    for i in range(lengths.shape[2]):
        end = end + lengths[which, shard, i]
        start = jnp.where(end <= own, end, start)
    lowest = jnp.maximum(start, own - WINDOW // BLK)

    def places(index):
        relative = slots[which, shard, jnp.maximum(own - index, 0)] ^ me
        high = jnp.int32(0)
        for position, bit in enumerate(range(bits - 1, 1, -1)):
            high = high | (((relative >> bit) & 1) << position)
        one = (relative & 1) << (bits - 1)
        two = ((relative >> 1) & 1) << (bits - 2)
        swapped = ((relative & 1) << (bits - 2)) | (((relative >> 1) & 1) << (bits - 1))
        return high | one | two, high | swapped

    return own - lowest + 1, places


def pair_mask(far, count, index):
    key = lax.broadcasted_iota(jnp.int32, (BLK, GCOLS), 0)
    query = lax.broadcasted_iota(jnp.int32, (BLK, GCOLS), 1) & (BLK - 1)
    ahead = key - query
    masks = []
    for i in (index, index + 1):
        most = jnp.where(i < count, i * BLK, -2 * BLK)
        mask = ahead <= most
        if far:
            mask = mask & (ahead > i * BLK - WINDOW)
        masks.append(mask)
    return jnp.concatenate(masks, axis=0)


def forward_kernel(
    far, bits, which, ids, lengths, slots, first_ref, second_ref, query_ref, out_ref, lse_ref, pad_ref
):
    count, places = seen_blocks(bits, which, ids, lengths, slots)
    queries = query_ref[...]
    for group in range(KVH):
        pad_ref[:, group * GCOLS : (group + 1) * GCOLS] = heads_t(queries, group, group)

    for group in range(KVH):
        columns = slice(group * GCOLS, (group + 1) * GCOLS)
        value_unit = KVH + group

        def step(pair, carried):
            high, total, acc = carried
            index = 2 * pair
            held = (places(index), places(index + 1))
            keys = key_tile(first_ref, second_ref, held, group)
            values = key_tile(first_ref, second_ref, held, value_unit)
            scores = dot(keys, pad_ref[:, columns], 1, 0) * SCALE
            scores = jnp.where(pair_mask(far, count, index), scores, NEG)
            new_high = jnp.maximum(high, jnp.max(scores, axis=0, keepdims=True))
            weights = jnp.exp(scores - new_high)
            fade = jnp.exp(high - new_high)
            total = total * fade + jnp.sum(weights, axis=0, keepdims=True)
            values_t = half_rows(values.T, value_unit)
            acc = acc * fade + dot(values_t, weights.astype(bf16), 1, 0)
            return (new_high, total, acc)

        start = (
            jnp.full((1, GCOLS), NEG, f32),
            jnp.zeros((1, GCOLS), f32),
            jnp.zeros((HD, GCOLS), f32),
        )
        high, total, acc = lax.fori_loop(0, (count + 1) // 2, step, start)
        acc = acc / total
        for r in range(REP):
            head = group * REP + r
            out_ref[head * HD : (head + 1) * HD, :] = acc[:, r * BLK : (r + 1) * BLK]
        lse_ref[:, columns] = high + jnp.log(total)


def backward_kernel(
    far,
    bits,
    which,
    ids,
    lengths,
    slots,
    first_ref,
    second_ref,
    query_ref,
    grad_ref,
    out_ref,
    lse_ref,
    dq_ref,
    dfirst_ref,
    dsecond_ref,
    pad_ref,
    right_ref,
    delta_ref,
    left_ref,
    acc_ref,
):
    count, places = seen_blocks(bits, which, ids, lengths, slots)
    queries = query_ref[...]
    grads = grad_ref[...]
    product = grads.astype(f32) * out_ref[...]
    for head in range(HEADS):
        delta_ref[:, head * BLK : (head + 1) * BLK] = jnp.sum(
            product[head * HD : (head + 1) * HD, :], axis=0, keepdims=True
        )
    for unit in range(2 * KVH):
        padded = heads_t(queries if unit < KVH else grads, unit % KVH, unit)
        rows = slice(unit * GCOLS, (unit + 1) * GCOLS)
        pad_ref[:, rows] = padded
        right_ref[rows, :] = padded.T
    dfirst_ref[...] = jnp.zeros_like(dfirst_ref)
    dsecond_ref[...] = jnp.zeros_like(dsecond_ref)
    acc_ref[...] = jnp.zeros_like(acc_ref)

    @pl.loop(0, (count + 1) // 2)
    def _(pair):
        index = 2 * pair
        held = (places(index), places(index + 1))
        mask = pair_mask(far, count, index)
        for group in range(KVH):
            value_unit = KVH + group
            columns = slice(group * GCOLS, (group + 1) * GCOLS)
            value_columns = slice(value_unit * GCOLS, (value_unit + 1) * GCOLS)
            keys = key_tile(first_ref, second_ref, held, group)
            values = key_tile(first_ref, second_ref, held, value_unit)
            scores = dot(keys, pad_ref[:, columns], 1, 0) * SCALE
            probs = jnp.where(mask, jnp.exp(scores - lse_ref[:, columns]), 0.0)
            grad_probs = dot(values, pad_ref[:, value_columns], 1, 0)
            grad_scores = (probs * (grad_probs - delta_ref[:, columns])).astype(bf16)
            left_ref[:, columns] = grad_scores
            left_ref[:, value_columns] = probs.astype(bf16)
            keys_t = half_rows(keys.T, group)
            acc_ref[:, columns] += dot(keys_t, grad_scores, 1, 0)
        for tile in range(KVH):
            rows = slice(2 * tile * GCOLS, 2 * (tile + 1) * GCOLS)
            lanes = slice(tile * LANES, (tile + 1) * LANES)
            block = dot(left_ref[:, rows], right_ref[rows, :], 1, 0)
            lane = lax.broadcasted_iota(jnp.int32, (1, LANES), 1) + tile * LANES
            block = (block * jnp.where(lane < KVH * HD, SCALE, 1.0)).astype(bf16)
            first, second = held[0]
            dfirst_ref[first, :, lanes] = block[:HALF]
            dsecond_ref[second, :, lanes] = block[HALF:BLK]

            @pl.when(index + 1 < count)
            def _():
                first, second = held[1]
                dfirst_ref[first, :, lanes] = block[BLK : BLK + HALF]
                dsecond_ref[second, :, lanes] = block[BLK + HALF :]

    for head in range(HEADS):
        columns = slice(head * BLK, (head + 1) * BLK)
        dq_ref[head * HD : (head + 1) * HD, :] = (acc_ref[:, columns] * SCALE).astype(bf16)


def in_hbm(values):
    return [pltpu.with_memory_space_constraint(v, pltpu.HBM) for v in values]


VMEM_SPEC = pl.BlockSpec(memory_space=pltpu.VMEM)
SMEM_SPEC = pl.BlockSpec(memory_space=pltpu.SMEM)


def attention_forward(which, tables, first, second, queries_t):
    steps = first.shape[0]
    return pl.pallas_call(
        functools.partial(
            forward_kernel, steps > WINDOW // BLK, steps.bit_length() - 1, which
        ),
        out_shape=(
            jax.ShapeDtypeStruct((HEADS * HD, BLK), f32),
            jax.ShapeDtypeStruct((1, HEADS * BLK), f32),
        ),
        in_specs=[SMEM_SPEC] * 3 + [VMEM_SPEC] * 3,
        out_specs=(VMEM_SPEC,) * 2,
        scratch_shapes=[pltpu.VMEM((LANES, HEADS * BLK), bf16)],
        compiler_params=pltpu.CompilerParams(vmem_limit_bytes=8 << 20),
        cost_estimate=pl.CostEstimate(
            flops=4 * HEADS * HD * BLK * BLK * 8,
            bytes_accessed=first.size * 4,
            transcendentals=HEADS * BLK * BLK * 8,
        ),
        name="attention_forward",
    )(*tables, first, second, queries_t)


def attention_backward(which, tables, first, second, queries_t, grads_t, out_t, lse):
    steps = first.shape[0]
    return pl.pallas_call(
        functools.partial(
            backward_kernel, steps > WINDOW // BLK, steps.bit_length() - 1, which
        ),
        out_shape=(
            jax.ShapeDtypeStruct((HEADS * HD, BLK), bf16),
            jax.ShapeDtypeStruct(first.shape, bf16),
            jax.ShapeDtypeStruct(second.shape, bf16),
        ),
        in_specs=[SMEM_SPEC] * 3 + [VMEM_SPEC] * 6,
        out_specs=(VMEM_SPEC,) * 3,
        scratch_shapes=[
            pltpu.VMEM((LANES, 2 * KVH * GCOLS), bf16),
            pltpu.VMEM((2 * KVH * GCOLS, LANES), bf16),
            pltpu.VMEM((1, HEADS * BLK), f32),
            pltpu.VMEM((2 * BLK, 2 * KVH * GCOLS), bf16),
            pltpu.VMEM((HD, HEADS * BLK), f32),
        ],
        compiler_params=pltpu.CompilerParams(vmem_limit_bytes=16 << 20),
        cost_estimate=pl.CostEstimate(
            flops=10 * HEADS * HD * BLK * BLK,
            bytes_accessed=first.size,
            transcendentals=HEADS * BLK * BLK,
        ),
        name="attention_backward",
    )(*tables, first, second, queries_t, grads_t, out_t, lse)


def block_kernel(
    x_ref,
    cot_ref,
    att_ref,
    out_w_ref,
    gain_ref,
    gate_w_ref,
    up_w_ref,
    down_w_ref,
    hidden_ref,
    grads_ref,
    normed_ref,
    layer_ref,
    grad_mixed_ref,
    grad_low_ref,
    grad_att_ref,
    gain_grad_ref,
    mixed,
    normed,
    cot,
    grad_normed,
    layer,
):
    step = pl.program_id(0)

    @pl.when(step == 0)
    def _():
        cot[...] = cot_ref[...].T
        values = x_ref[...].astype(f32).T + dot(att_ref[...], out_w_ref[...], 0, 0)
        mixed[...] = values
        inverse = lax.rsqrt(jnp.mean(values * values, axis=-1, keepdims=True) + EPS)
        low = (values * inverse * gain_ref[...]).astype(bf16)
        normed[...] = low
        normed_ref[...] = low.T
        layer[...] = values
        grad_normed[...] = jnp.zeros_like(grad_normed)

    grad_hidden = dot(cot[...], down_w_ref[...], 1, 0)
    gate = dot(normed[...], gate_w_ref[...], 1, 0)
    up = dot(normed[...], up_w_ref[...], 1, 0)
    sigmoid = jax.nn.sigmoid(gate)
    silu = gate * sigmoid
    hidden = (silu * up).astype(bf16)
    grad_gate = (grad_hidden * up * sigmoid * (1.0 + gate * (1.0 - sigmoid))).astype(bf16)
    grad_up = (grad_hidden * silu).astype(bf16)
    hidden_ref[...] = hidden
    grads_ref[0] = grad_gate
    grads_ref[1] = grad_up
    layer[...] += dot(hidden, down_w_ref[...], 1, 1)
    grad_normed[...] += dot(grad_gate, gate_w_ref[...], 1, 1) + dot(
        grad_up, up_w_ref[...], 1, 1
    )

    @pl.when(step == pl.num_programs(0) - 1)
    def _():
        values = mixed[...]
        layer_ref[...] = layer[...].astype(bf16).T
        inverse = lax.rsqrt(jnp.mean(values * values, axis=-1, keepdims=True) + EPS)
        grads = grad_normed[...]
        gain_grad_ref[...] = jnp.sum(grads * values * inverse, axis=0, keepdims=True)
        scaled = grads * gain_ref[...]
        cubed = inverse * inverse * inverse
        back = inverse * scaled - values * cubed * jnp.mean(
            scaled * values, axis=-1, keepdims=True
        )
        grad_mixed = cot[...].astype(f32) + back
        low = grad_mixed.astype(bf16)
        grad_mixed_ref[...] = grad_mixed.T
        grad_low_ref[...] = low
        grad_att_ref[...] = dot(out_w_ref[...], low, 1, 1).astype(bf16)


def feed_forward(x_t, cot_t, attended_t, out_w, gain, gate_w, up_w, down_w_t):
    width, rows = x_t.shape
    inner = gate_w.shape[1]
    tile = 256

    def fixed(shape):
        return pl.BlockSpec(shape, lambda i: (0,) * len(shape))

    weight = pl.BlockSpec((width, tile), lambda i: (0, i))
    wide = (width, rows)
    return pl.pallas_call(
        block_kernel,
        grid=(inner // tile,),
        in_specs=[fixed(wide)] * 3
        + [fixed(out_w.shape), fixed((1, width)), weight, weight, weight],
        out_specs=(
            pl.BlockSpec((rows, tile), lambda i: (0, i)),
            pl.BlockSpec((2, rows, tile), lambda i: (0, 0, i)),
            fixed(wide),
            fixed(wide),
            fixed(wide),
            fixed((rows, width)),
            fixed(wide),
            fixed((1, width)),
        ),
        out_shape=(
            pltpu.HBM((rows, inner), bf16),
            pltpu.HBM((2, rows, inner), bf16),
            pltpu.HBM(wide, bf16),
            pltpu.HBM(wide, bf16),
            pltpu.HBM(wide, f32),
            pltpu.HBM((rows, width), bf16),
            pltpu.HBM(wide, bf16),
            pltpu.HBM((1, width), f32),
        ),
        scratch_shapes=[
            pltpu.VMEM((rows, width), f32),
            pltpu.VMEM((rows, width), bf16),
            pltpu.VMEM((rows, width), bf16),
            pltpu.VMEM((rows, width), f32),
            pltpu.VMEM((rows, width), f32),
        ],
        compiler_params=pltpu.CompilerParams(vmem_limit_bytes=24 << 20),
        cost_estimate=pl.CostEstimate(
            flops=12 * rows * width * inner,
            bytes_accessed=8 * width * inner,
            transcendentals=rows * inner,
        ),
        name="feed_forward",
    )(*in_hbm([x_t, cot_t, attended_t, out_w, gain, gate_w, up_w, down_w_t]))


def weight_grad_kernel(products, sides, ids, *refs):
    values = []
    for number, (by_shard, right_t) in enumerate(products):
        left, left_other, right, right_other = refs[4 * number : 4 * number + 4]
        rows = left_other.shape[0]
        start = pl.multiple_of(ids[1] * rows if by_shard else 0, 8)
        dim = 1 if right_t else 0
        values.append(
            dot(left[pl.ds(start, rows), :], right[...].reshape(right.shape[-2:]), 1, dim)
            + dot(left_other[...], right_other[...].reshape(right_other.shape[-2:]), 1, dim)
        )
    outs = refs[4 * len(products) :]
    for number, (product, first, rows, bit) in enumerate(sides):
        sent, kept = outs[2 * number : 2 * number + 2]
        half = rows // 2
        low = values[product][first : first + half].astype(bf16)
        high = values[product][first + half : first + rows].astype(bf16)
        own = (ids[0] >> bit) & 1

        @pl.when(own == 0)
        def _():
            kept[...] = low
            sent[...] = high

        @pl.when(own != 0)
        def _():
            kept[...] = high
            sent[...] = low


def weight_grad(name, ids, products, operands, right_specs, sides, tiles, columns):
    tile = columns // tiles
    specs = []
    for (left, left_other, _, _), rights in zip(operands, right_specs):
        specs += [
            pl.BlockSpec(left.shape, lambda i, ids: (0, 0)),
            pl.BlockSpec(left_other.shape, lambda i, ids: (0, 0)),
            *rights,
        ]
    shapes = [(side[2] // 2, columns) for side in sides for _ in range(2)]
    return pl.pallas_call(
        functools.partial(weight_grad_kernel, products, sides),
        grid_spec=pltpu.PrefetchScalarGridSpec(
            num_scalar_prefetch=1,
            grid=(tiles,),
            in_specs=specs,
            out_specs=[pl.BlockSpec((rows, tile), lambda i, ids: (0, i)) for rows, _ in shapes],
        ),
        out_shape=[pltpu.HBM(shape, bf16) for shape in shapes],
        compiler_params=pltpu.CompilerParams(vmem_limit_bytes=16 << 20),
        cost_estimate=pl.CostEstimate(
            flops=2 * sum(rows * width for rows, width in shapes) * 512,
            bytes_accessed=2 * sum(rows * width for rows, width in shapes),
            transcendentals=0,
        ),
        name=name,
    )(ids, *in_hbm([o for group in operands for o in group]))


def per_device(
    inputs,
    gain_attn,
    w_query,
    w_keyval,
    w_out,
    gain_mlp,
    w_gate,
    w_up,
    w_down,
    cotangent,
    seq_blocks,
    block_slots,
):
    micro = inputs.shape[0]
    shard = lax.axis_index("fsdp")
    is_low = shard == 0
    rounds = Rounds()

    def joined(part, other):
        return jnp.concatenate(
            [jnp.where(is_low, part, other), jnp.where(is_low, other, part)], axis=0
        )

    def whole(part):
        return lax.all_gather(part, "fsdp", axis=0, tiled=True)

    def theirs(value, dim):
        half = value.shape[dim] // 2
        return lax.dynamic_slice_in_dim(value, (1 - shard) * half, half, dim)

    def tokens_last(value):
        return jnp.concatenate([value[m, 0].T for m in range(micro)], axis=1)

    out_full = whole(w_out)
    gate_full = whole(w_gate)
    up_full = whole(w_up)
    down_full_t = whole(w_down).T

    attn_gain = joined(gain_attn, swap_fsdp(gain_attn)).astype(f32)[:, None]
    keyval_full = joined(w_keyval, swap_fsdp(w_keyval))
    x_t = tokens_last(inputs)
    in_t = x_t.astype(f32)
    inverse_attn = lax.rsqrt(jnp.mean(in_t * in_t, axis=0, keepdims=True) + EPS)
    normed_t = (in_t * inverse_attn * attn_gain).astype(bf16)
    keyvals = dot(normed_t, keyval_full, 0, 0).astype(bf16)
    gathers = [GatherBlocks(keyvals[m * BLK : (m + 1) * BLK]) for m in range(micro)]

    rounds.begin(gathers[0])
    (w_query, gain_mlp, cotangent, normed_t) = rounds.end(
        gathers[:1], w_query, gain_mlp, cotangent, normed_t
    )
    rounds.begin(*gathers)
    query_other, gain_other = swap_fsdp(w_query), swap_fsdp(gain_mlp)
    cot_t = tokens_last(cotangent)
    (query_other, gain_other, cot_t) = rounds.end(gathers, query_other, gain_other, cot_t)
    for step in range(len(gathers[0].stages)):
        rounds.begin(*[g for g in gathers if len(g.stages) > 2 or g is gathers[0]])
        if step == 0:
            query_full = joined(w_query, query_other)
            mlp_gain = joined(gain_mlp, gain_other).astype(f32)[None]
            queries_t = dot(query_full, normed_t, 0, 0).astype(bf16)
            normed_theirs = theirs(normed_t, 0)
            (queries_t, mlp_gain, normed_theirs) = rounds.end(
                list(rounds.flying), queries_t, mlp_gain, normed_theirs
            )
        elif step == 1:
            normed_other = swap_fsdp(normed_theirs)
            cot_other = swap_fsdp(cot_t)
            (normed_other, cot_other) = rounds.end(list(rounds.flying), normed_other, cot_other)
        else:
            rounds.end(list(rounds.flying))
    queries = [queries_t[:, m * BLK : (m + 1) * BLK] for m in range(micro)]
    ids = jnp.stack([lax.axis_index("ctx"), shard]).astype(jnp.int32)
    tables = (ids, seq_blocks, block_slots)

    rounds.begin(gathers[1])
    rounds.end(gathers[1:])
    rounds.begin(gathers[1])
    first = attention_forward(0, tables, *gathers[0].halves, queries[0])
    first = rounds.end(gathers[1:], *first)
    second = attention_forward(1, tables, *gathers[1].halves, queries[1])
    outs, lses = zip(first, second)
    attended_t = jnp.concatenate(outs, axis=1).astype(bf16)

    attended_other = swap_fsdp(theirs(attended_t, 0))
    (
        hidden,
        grad_inner,
        normed_mlp_t,
        layer_out_t,
        grad_mixed_t,
        grad_mixed_low,
        grad_attended_t,
        mlp_gain_grad,
    ) = feed_forward(
        x_t, cot_t, attended_t, out_full, mlp_gain, gate_full, up_full, down_full_t
    )
    hidden_other = swap_fsdp(theirs(hidden, 1))
    mlp_other = swap_fsdp(theirs(normed_mlp_t, 0))
    inner_other = swap_fsdp(grad_inner)

    part = hidden_other.shape[1]
    width = cot_t.shape[0]
    half = width // 2
    tokens, inner = hidden.shape
    near = pl.BlockSpec((tokens, part // 2), lambda i, ids: (0, ids[1] * 2 + i))
    far = pl.BlockSpec((tokens, part // 2), lambda i, ids: (0, i))
    down_job = Reduce(
        weight_grad(
            "down_grad",
            ids,
            ((False, False),),
            ((cot_t, cot_other, hidden, hidden_other),),
            ((near, far),),
            ((0, 0, half, 0), (0, half, half, 1)),
            2,
            part,
        ),
        (1, 0),
    )

    def inner_job(n):
        spec = pl.BlockSpec((1, tokens, inner // 5), lambda i, ids: (n, 0, i))
        return Reduce(
            weight_grad(
                "inner_grad",
                ids,
                ((True, False),),
                ((normed_mlp_t, mlp_other, grad_inner, inner_other),),
                ((spec, spec),),
                ((0, 0, half // 2, 0), (0, half // 2, half // 2, 1)),
                5,
                inner,
            ),
            (1, 1),
        )

    def attention_back(m):
        return attention_backward(
            m,
            tables,
            *gathers[m].halves,
            queries[m],
            grad_attended_t[:, m * BLK : (m + 1) * BLK],
            outs[m],
            lses[m],
        )

    gate_job = inner_job(0)
    rounds.prepare(down_job, gate_job)
    (grad_inner, grad_attended_t, grad_mixed_low) = rounds.end(
        [], grad_inner, grad_attended_t, grad_mixed_low
    )

    rounds.begin(down_job, gate_job)
    up_job = inner_job(1)
    rounds.prepare(up_job)
    (grad_attended_t, grad_mixed_low) = rounds.end([down_job], grad_attended_t, grad_mixed_low)

    rounds.begin(up_job)
    rounds.prepare(down_job)
    back_first = attention_back(0)
    (grad_attended_t, grad_mixed_low, *back_first) = rounds.end(
        [gate_job], grad_attended_t, grad_mixed_low, *back_first
    )

    rounds.begin(down_job)
    key_first = ScatterBlocks(*back_first[1:])
    rounds.prepare(gate_job, key_first)
    (grad_attended_t, grad_mixed_low) = rounds.end([up_job], grad_attended_t, grad_mixed_low)

    rounds.begin(gate_job, key_first)
    rounds.prepare(up_job)
    back_second = attention_back(1)
    mixed_other = swap_fsdp(grad_mixed_low)
    (mixed_other, *back_second) = rounds.end([down_job], mixed_other, *back_second)

    rounds.begin(up_job, down_job)
    key_second = ScatterBlocks(*back_second[1:])
    rounds.prepare(key_second)
    grad_queries_t = jnp.concatenate([back_first[0], back_second[0]], axis=1)
    (grad_queries_t,) = rounds.end([gate_job], grad_queries_t)

    rounds.begin(key_second, gate_job)
    queries_other = swap_fsdp(grad_queries_t)
    (queries_other,) = rounds.end([key_first, down_job], queries_other)

    rounds.begin(down_job)
    rounds.prepare(key_first)
    rounds.end([up_job, gate_job])
    rounds.begin(key_first, up_job, gate_job)
    flat = pl.BlockSpec((width, tokens), lambda i, ids: (0, 0))
    flat_half = pl.BlockSpec((tokens, width), lambda i, ids: (0, 0))
    query_job = Reduce(
        weight_grad(
            "query_grad",
            ids,
            ((True, True), (True, False)),
            (
                (normed_t, normed_other, grad_queries_t, queries_other),
                (attended_t, attended_other, grad_mixed_low, mixed_other),
            ),
            ((flat, flat), (flat_half, flat_half)),
            ((0, 0, half, 0), (1, 0, half, 1)),
            1,
            width,
        ),
        (0, 1),
    )
    rounds.prepare(query_job)
    rounds.end([key_second, down_job])
    rounds.run(down_job, 0)
    down_spread = Spread(down_job)

    rounds.begin(down_spread, query_job)
    rounds.prepare(key_second)
    (grad_queries_t,) = rounds.end([key_first, up_job, gate_job], grad_queries_t)
    rounds.run(gate_job, 0)
    gate_spread = Spread(gate_job)

    rounds.begin(key_second, key_first, up_job, gate_spread)
    grad_normed_t = dot(query_full, grad_queries_t, 1, 0)
    (grad_normed_t,) = rounds.end([down_spread, query_job], grad_normed_t)
    rounds.run(down_spread, 3)

    rounds.begin(down_spread, query_job)
    rounds.end([key_second, key_first, up_job, gate_spread])
    rounds.run(up_job, 0)
    up_spread = Spread(up_job)
    rounds.run(gate_spread, 3)

    rounds.begin(key_second, key_first, up_spread, gate_spread)
    rounds.end([down_spread, query_job])

    rounds.begin(down_spread)
    rounds.end([key_second, key_first, up_spread, gate_spread])
    rounds.run(key_first, 0)
    rounds.run(up_spread, 3)

    rounds.begin(key_second, gate_spread, up_spread, query_job)
    rounds.end([down_spread, key_second])
    rounds.run(key_second, 0)
    grad_keyvals = jnp.concatenate([key_first.held[0], key_second.held[0]], axis=0)

    rounds.begin(down_spread)
    keyvals_other = swap_fsdp(grad_keyvals)
    grad_normed_t = grad_normed_t + dot(keyval_full, grad_keyvals, 1, 1)
    (grad_normed_t, keyvals_other) = rounds.end(
        [gate_spread, up_spread, query_job], grad_normed_t, keyvals_other
    )

    rounds.begin(gate_spread, query_job)
    attn_gain_grad = jnp.sum(grad_normed_t * in_t * inverse_attn, axis=1)
    gains = jnp.stack([attn_gain_grad, mlp_gain_grad[0]], axis=1)
    gains_theirs = theirs(gains, 0)
    normed_mine = lax.dynamic_slice_in_dim(normed_t, shard * half, half, 0)
    keyval_grad = dot(normed_mine, grad_keyvals, 1, 0) + dot(normed_other, keyvals_other, 1, 0)
    gains_mine = lax.dynamic_slice_in_dim(gains, shard * half, half, 0) + swap_fsdp(gains_theirs)
    pad = jnp.zeros((half, LANES - 2), bf16)
    last = jnp.concatenate([keyval_grad.astype(bf16), gains_mine.astype(bf16), pad], axis=1)
    last_job = Solo(last)
    rounds.prepare(last_job)
    (grad_normed_t,) = rounds.end([down_spread, query_job], grad_normed_t)
    rounds.run(query_job, 0)
    query_spread = Spread(query_job)

    rounds.begin(last_job, up_spread, query_spread)
    down_sum = jnp.concatenate(down_spread.pair, axis=0)
    (down_sum,) = rounds.end([last_job, gate_spread, query_spread], down_sum)
    rounds.run(query_spread, 3)

    rounds.begin(last_job, query_spread)
    scaled = grad_normed_t * attn_gain
    cubed = inverse_attn * inverse_attn * inverse_attn
    input_grad_t = (
        grad_mixed_t
        + inverse_attn * scaled
        - in_t * cubed * jnp.mean(scaled * in_t, axis=0, keepdims=True)
    )
    (input_grad_t,) = rounds.end([last_job, up_spread, query_spread], input_grad_t)

    rounds.begin(last_job, up_spread, query_spread)
    gate_sum = jnp.concatenate(gate_spread.pair, axis=0)
    (gate_sum,) = rounds.end([last_job, query_spread], gate_sum)
    rounds.begin(last_job, query_spread)
    rounds.end([last_job])
    rounds.run(last_job, 2)
    rounds.begin(last_job)
    rounds.end([last_job, up_spread])
    rounds.begin(last_job)
    up_sum = jnp.concatenate(up_spread.pair, axis=0)
    (up_sum,) = rounds.end([last_job, query_spread], up_sum)

    def by_token(value_t):
        parts = [value_t[:, m * BLK : (m + 1) * BLK].T[None] for m in range(micro)]
        return jnp.stack(parts)

    columns = keyval_grad.shape[1]
    return (
        by_token(layer_out_t),
        by_token(input_grad_t),
        last_job.value[:, columns],
        query_spread.pair[0],
        last_job.value[:, :columns],
        query_spread.pair[1],
        last_job.value[:, columns + 1],
        gate_sum,
        up_sum,
        down_sum.T,
    )


def solution(mesh):
    tokens = P(None, "fsdp", "ctx", None)
    vector = P("fsdp")
    matrix = P("fsdp", None)
    return jax.shard_map(
        per_device,
        mesh=mesh,
        in_specs=(
            tokens,
            vector,
            matrix,
            matrix,
            matrix,
            vector,
            matrix,
            matrix,
            matrix,
            tokens,
            P(),
            P(),
        ),
        out_specs=(
            tokens,
            tokens,
            vector,
            matrix,
            matrix,
            matrix,
            vector,
            matrix,
            matrix,
            matrix,
        ),
        check_vma=False,
    )
```

```python
import functools

import jax
import jax.numpy as jnp
from jax import lax
from jax.experimental import pallas as pl
from jax.experimental.pallas import tpu as pltpu
from jax.sharding import PartitionSpec as P

HEADS = 15
KVH = 5
HD = 64
REP = HEADS // KVH
WINDOW = 2048
BLK = 128
HALF = BLK // 2
KVW = 2 * KVH * HD
EPS = 1e-05
NEG = -1e30
SCALE = HD ** (-0.5)
LANES = 128
GCOLS = REP * BLK

bf16 = jnp.bfloat16
f32 = jnp.float32


def dot(left, right, left_dim, right_dim):
    return lax.dot_general(
        left, right, (((left_dim,), (right_dim,)), ((), ())), preferred_element_type=f32
    )


def flip_ctx(value, bit):
    size = lax.axis_size("ctx")
    return lax.ppermute(value, "ctx", [(i, i ^ (1 << bit)) for i in range(size)])


def swap_fsdp(value):
    return lax.ppermute(value, "fsdp", [(0, 1), (1, 0)])


def tie(values):
    return lax.optimization_barrier(tuple(values))


def own_bit(bit):
    return (lax.axis_index("ctx") >> bit) & 1


def high_bits():
    return list(range(2, lax.axis_size("ctx").bit_length() - 1))


def add_low(kept, arrived):
    return (kept.astype(f32) + arrived.astype(f32)).astype(bf16)


def by_bit(bit, mine, arrived):
    low = own_bit(bit) == 0
    return jnp.where(low, mine, arrived), jnp.where(low, arrived, mine)


def in_order(bit, mine, arrived, dim):
    return jnp.concatenate(by_bit(bit, mine, arrived), axis=dim)


class GatherBlocks:
    def __init__(self, block):
        self.held = block[None]
        self.stages = high_bits()[::-1] + [None, None]
        self.halves = None

    def operands(self):
        if self.stages[0] is not None:
            return [self.held], [self.stages[0]]
        if self.halves is None:
            self.halves = [self.held[:, :HALF], self.held[:, HALF:]]
            self.bits = (1, 0)
        return self.halves, self.bits

    def absorb(self, arrived):
        if self.stages.pop(0) is not None:
            self.held = jnp.concatenate([self.held, arrived[0]], axis=0)
        else:
            self.halves = [
                jnp.concatenate([h, a], axis=0) for h, a in zip(self.halves, arrived)
            ]
            self.bits = (0, 1)


class ScatterBlocks:
    def __init__(self, first, second):
        self.halves = [first, second]
        self.bits = (0, 1)
        self.stages = [None, None]

    def operands(self):
        count = self.halves[0].shape[0] // 2
        return [half[count:] for half in self.halves], self.bits

    def absorb(self, arrived):
        self.stages.pop(0)
        count = self.halves[0].shape[0] // 2
        self.halves = [add_low(half[:count], a) for half, a in zip(self.halves, arrived)]
        self.bits = (1, 0)


def cut(value, bit, dim):
    half = value.shape[dim] // 2
    own = own_bit(bit)
    sent = lax.dynamic_slice_in_dim(value, (1 - own) * half, half, dim)
    return lax.dynamic_slice_in_dim(value, own * half, half, dim), sent


class Reduce:
    def __init__(self, parts, dims):
        self.first = [parts[0], parts[2]]
        self.kept = [parts[1], parts[3]]
        self.dims = dims
        self.stages = [(0, 1), (1, 0)] + high_bits()

    def operands(self):
        stage = self.stages[0]
        if self.first is not None:
            sent, self.first = self.first, None
        elif isinstance(stage, tuple):
            parts = [cut(v, b, self.dims[0]) for v, b in zip(self.pair, stage)]
            self.kept = [p[0] for p in parts]
            sent = [p[1] for p in parts]
        else:
            if self.pair is not None:
                kept, out = by_bit(stage, *self.pair)
                self.pair = None
            else:
                kept, out = cut(self.held, stage, self.dims[1])
            self.kept, sent, stage = [kept], [out], [stage]
        return sent, stage

    def absorb(self, arrived):
        sums = [add_low(k, a) for k, a in zip(self.kept, arrived)]
        if isinstance(self.stages.pop(0), tuple):
            self.pair = sums
        else:
            self.held = sums[0]


class Spread:
    def __init__(self, job):
        self.held = job.held
        self.dims = job.dims
        self.stages = high_bits()[::-1] + [(1, 0), (0, 1)]
        self.pair = None

    def operands(self):
        stage = self.stages[0]
        if isinstance(stage, tuple):
            return self.pair, stage
        return [self.held], [stage]

    def absorb(self, arrived):
        stage = self.stages.pop(0)
        if isinstance(stage, tuple):
            parts = [by_bit(b, v, a) for v, a, b in zip(self.pair, arrived, stage)]
            if self.stages:
                self.pair = [jnp.concatenate(p, axis=self.dims[0]) for p in parts]
            else:
                self.quarters = [q for p in parts for q in p]
        elif stage == 2:
            self.pair = list(by_bit(stage, self.held, arrived[0]))
        else:
            self.held = in_order(stage, self.held, arrived[0], self.dims[1])


class GatherHigh:
    def __init__(self, value):
        self.held = value[None]
        self.stages = high_bits()[::-1]

    def operands(self):
        return [self.held], [self.stages[0]]

    def absorb(self, arrived):
        self.stages.pop(0)
        self.held = jnp.concatenate([self.held, arrived[0]], axis=0)


class ScatterHigh:
    def __init__(self, held):
        self.held = held
        self.stages = high_bits()

    def operands(self):
        return [self.held[self.held.shape[0] // 2 :]], [self.stages[0]]

    def absorb(self, arrived):
        self.stages.pop(0)
        self.held = add_low(self.held[: self.held.shape[0] // 2], arrived[0])


class SumVector:
    def __init__(self, value):
        self.value = value
        self.stages = list(range(lax.axis_size("ctx").bit_length() - 1))

    def operands(self):
        return [self.value], [self.stages[0]]

    def absorb(self, arrived):
        self.stages.pop(0)
        self.value = self.value + arrived[0]


def rows_of(quarters, columns=slice(None)):
    return jnp.concatenate([q[:, columns] for q in quarters], axis=0).astype(f32)


class Solo:
    def __init__(self, value):
        self.value = value
        high = [(bit, None) for bit in high_bits()]
        self.stages = [(0, True), (1, True)] + high + [(1, False), (0, False)]

    def operands(self):
        bit, cuts = self.stages[0]
        if not cuts:
            return [self.value], [bit]
        self.value, sent = cut(self.value, bit, 0)
        return [sent], [bit]

    def absorb(self, arrived):
        bit, cuts = self.stages.pop(0)
        if cuts is not False:
            self.value = add_low(self.value, arrived[0])
        else:
            kind = bf16 if self.stages else f32
            self.value = in_order(bit, self.value.astype(kind), arrived[0].astype(kind), 0)


class Rounds:
    def __init__(self):
        self.flying = {}
        self.ready = {}
        self.fresh = []

    def begin(self, *jobs):
        for job in jobs:
            arrays, bits = self.ready.pop(job, None) or job.operands()
            self.flying[job] = [flip_ctx(v, b) for v, b in zip(arrays, bits)]

    def prepare(self, *jobs):
        for job in jobs:
            self.ready[job] = job.operands()
            self.fresh.append(job)

    def end(self, jobs, *values):
        ahead = [job for job in self.fresh if job in self.ready]
        self.fresh = []
        arrays = [a for job in jobs for a in self.flying[job]]
        sent = [a for job in ahead for a in self.ready[job][0]]
        rest = list(tie([*values, *arrays, *sent]))
        values, rest = rest[: len(values)], rest[len(values) :]
        for job in jobs:
            count = len(self.flying.pop(job))
            job.absorb(rest[:count])
            rest = rest[count:]
        for job in ahead:
            count = len(self.ready[job][0])
            self.ready[job] = (rest[:count], self.ready[job][1])
            rest = rest[count:]
        return values

    def run(self, job, left):
        while len(job.stages) > left:
            self.begin(job)
            self.end([job])


def key_tile(first_ref, second_ref, places, unit):
    lanes = pl.ds(pl.multiple_of((unit // 2) * LANES, LANES), LANES)
    parts = []
    for first, second in places:
        parts += [first_ref[first, :, lanes], second_ref[second, :, lanes]]
    return jnp.concatenate(parts, axis=0)


def heads_t(rows_t, group, unit):
    parts = [
        rows_t[(group * REP + r) * HD : (group * REP + r + 1) * HD, :] for r in range(REP)
    ]
    block = jnp.concatenate(parts, axis=1)
    zero = jnp.zeros_like(block)
    return jnp.concatenate([zero, block] if unit % 2 else [block, zero], axis=0)


def half_rows(tile_t, unit):
    return tile_t[(unit % 2) * HD : (unit % 2 + 1) * HD, :]


def seen_blocks(bits, which, ids, lengths, slots):
    me, shard = ids[0], ids[1]

    def look(j, own):
        return jnp.where(slots[which, shard, j] == me, j, own)

    own = lax.fori_loop(0, slots.shape[2], look, jnp.int32(0))
    end = jnp.int32(0)
    start = jnp.int32(0)
    for i in range(lengths.shape[2]):
        end = end + lengths[which, shard, i]
        start = jnp.where(end <= own, end, start)
    lowest = jnp.maximum(start, own - WINDOW // BLK)

    def places(index):
        relative = slots[which, shard, jnp.maximum(own - index, 0)] ^ me
        high = jnp.int32(0)
        for position, bit in enumerate(range(bits - 1, 1, -1)):
            high = high | (((relative >> bit) & 1) << position)
        one = (relative & 1) << (bits - 1)
        two = ((relative >> 1) & 1) << (bits - 2)
        swapped = ((relative & 1) << (bits - 2)) | (((relative >> 1) & 1) << (bits - 1))
        return high | one | two, high | swapped

    return own - lowest + 1, places


def pair_mask(far, count, index):
    key = lax.broadcasted_iota(jnp.int32, (BLK, GCOLS), 0)
    query = lax.broadcasted_iota(jnp.int32, (BLK, GCOLS), 1) & (BLK - 1)
    ahead = key - query
    masks = []
    for i in (index, index + 1):
        most = jnp.where(i < count, i * BLK, -2 * BLK)
        mask = ahead <= most
        if far:
            mask = mask & (ahead > i * BLK - WINDOW)
        masks.append(mask)
    return jnp.concatenate(masks, axis=0)


def lanes_at(start, size=LANES):
    return pl.ds(pl.multiple_of(start, LANES), size)


def spread_heads(source_ref, pad_ref, unit, group):
    parts = [
        source_ref[pl.ds(pl.multiple_of((group * REP + r) * HD, HD), HD), :] for r in range(REP)
    ]
    row = pl.multiple_of((unit % 2) * HD, HD)
    pad_ref[pl.ds(row, HD), lanes_at(unit * GCOLS, GCOLS)] = jnp.concatenate(parts, axis=1)


def forward_kernel(
    far, bits, which, ids, lengths, slots, first_ref, second_ref, query_ref, out_ref, lse_ref, pad_ref, half_ref
):
    count, places = seen_blocks(bits, which, ids, lengths, slots)
    pad_ref[...] = jnp.zeros_like(pad_ref)

    @pl.loop(0, KVH)
    def _(group):
        spread_heads(query_ref, pad_ref, group, group)
        columns = lanes_at(group * GCOLS, GCOLS)
        value_unit = KVH + group

        def step(pair, carried):
            high, total, acc = carried
            index = 2 * pair
            held = (places(index), places(index + 1))
            keys = key_tile(first_ref, second_ref, held, group)
            values = key_tile(first_ref, second_ref, held, value_unit)
            scores = dot(keys, pad_ref[:, columns], 1, 0) * SCALE
            scores = jnp.where(pair_mask(far, count, index), scores, NEG)
            new_high = jnp.maximum(high, jnp.max(scores, axis=0, keepdims=True))
            weights = jnp.exp(scores - new_high)
            fade = jnp.exp(high - new_high)
            total = total * fade + jnp.sum(weights, axis=0, keepdims=True)
            acc = acc * fade + dot(values.T, weights.astype(bf16), 1, 0)
            return (new_high, total, acc)

        start = (
            jnp.full((1, GCOLS), NEG, f32),
            jnp.zeros((1, GCOLS), f32),
            jnp.zeros((LANES, GCOLS), f32),
        )
        high, total, acc = lax.fori_loop(0, (count + 1) // 2, step, start)
        half_ref[...] = acc / total
        row = pl.multiple_of((value_unit % 2) * HD, HD)
        for r in range(REP):
            head_rows = pl.ds(pl.multiple_of((group * REP + r) * HD, HD), HD)
            out_ref[head_rows, :] = half_ref[pl.ds(row, HD), r * BLK : (r + 1) * BLK]
        lse_ref[:, columns] = high + jnp.log(total)


def backward_kernel(
    far,
    bits,
    which,
    ids,
    lengths,
    slots,
    first_ref,
    second_ref,
    query_ref,
    grad_ref,
    out_ref,
    lse_ref,
    dq_ref,
    dfirst_ref,
    dsecond_ref,
    pad_ref,
    right_ref,
    delta_ref,
    left_ref,
    acc_ref,
):
    count, places = seen_blocks(bits, which, ids, lengths, slots)
    queries = query_ref[...]
    grads = grad_ref[...]
    product = grads.astype(f32) * out_ref[...]
    for head in range(HEADS):
        delta_ref[:, head * BLK : (head + 1) * BLK] = jnp.sum(
            product[head * HD : (head + 1) * HD, :], axis=0, keepdims=True
        )
    for unit in range(2 * KVH):
        padded = heads_t(queries if unit < KVH else grads, unit % KVH, unit)
        rows = slice(unit * GCOLS, (unit + 1) * GCOLS)
        pad_ref[:, rows] = padded
        right_ref[rows, :] = padded.T
    dfirst_ref[...] = jnp.zeros_like(dfirst_ref)
    dsecond_ref[...] = jnp.zeros_like(dsecond_ref)
    acc_ref[...] = jnp.zeros_like(acc_ref)

    @pl.loop(0, (count + 1) // 2)
    def _(pair):
        index = 2 * pair
        held = (places(index), places(index + 1))
        mask = pair_mask(far, count, index)
        for group in range(KVH):
            value_unit = KVH + group
            columns = slice(group * GCOLS, (group + 1) * GCOLS)
            value_columns = slice(value_unit * GCOLS, (value_unit + 1) * GCOLS)
            keys = key_tile(first_ref, second_ref, held, group)
            values = key_tile(first_ref, second_ref, held, value_unit)
            scores = dot(keys, pad_ref[:, columns], 1, 0) * SCALE
            probs = jnp.where(mask, jnp.exp(scores - lse_ref[:, columns]), 0.0)
            grad_probs = dot(values, pad_ref[:, value_columns], 1, 0)
            grad_scores = (probs * (grad_probs - delta_ref[:, columns])).astype(bf16)
            left_ref[:, columns] = grad_scores
            left_ref[:, value_columns] = probs.astype(bf16)
            keys_t = half_rows(keys.T, group)
            acc_ref[:, columns] += dot(keys_t, grad_scores, 1, 0)
        for tile in range(KVH):
            rows = slice(2 * tile * GCOLS, 2 * (tile + 1) * GCOLS)
            lanes = slice(tile * LANES, (tile + 1) * LANES)
            block = dot(left_ref[:, rows], right_ref[rows, :], 1, 0)
            lane = lax.broadcasted_iota(jnp.int32, (1, LANES), 1) + tile * LANES
            block = (block * jnp.where(lane < KVH * HD, SCALE, 1.0)).astype(bf16)
            first, second = held[0]
            dfirst_ref[first, :, lanes] = block[:HALF]
            dsecond_ref[second, :, lanes] = block[HALF:BLK]

            @pl.when(index + 1 < count)
            def _():
                first, second = held[1]
                dfirst_ref[first, :, lanes] = block[BLK : BLK + HALF]
                dsecond_ref[second, :, lanes] = block[BLK + HALF :]

    for head in range(HEADS):
        columns = slice(head * BLK, (head + 1) * BLK)
        dq_ref[head * HD : (head + 1) * HD, :] = (acc_ref[:, columns] * SCALE).astype(bf16)


def in_hbm(values):
    return [pltpu.with_memory_space_constraint(v, pltpu.HBM) for v in values]


VMEM_SPEC = pl.BlockSpec(memory_space=pltpu.VMEM)
SMEM_SPEC = pl.BlockSpec(memory_space=pltpu.SMEM)


def attention_forward(which, tables, first, second, queries_t):
    steps = first.shape[0]
    return pl.pallas_call(
        functools.partial(
            forward_kernel, steps > WINDOW // BLK, steps.bit_length() - 1, which
        ),
        out_shape=(
            jax.ShapeDtypeStruct((HEADS * HD, BLK), f32),
            jax.ShapeDtypeStruct((1, HEADS * BLK), f32),
        ),
        in_specs=[SMEM_SPEC] * 3 + [VMEM_SPEC] * 3,
        out_specs=(VMEM_SPEC,) * 2,
        scratch_shapes=[pltpu.VMEM((LANES, HEADS * BLK), bf16), pltpu.VMEM((LANES, GCOLS), f32)],
        compiler_params=pltpu.CompilerParams(vmem_limit_bytes=8 << 20),
        cost_estimate=pl.CostEstimate(
            flops=4 * HEADS * HD * BLK * BLK * 8,
            bytes_accessed=first.size * 4,
            transcendentals=HEADS * BLK * BLK * 8,
        ),
        name="attention_forward",
    )(*tables, first, second, queries_t)


def attention_backward(which, tables, first, second, queries_t, grads_t, out_t, lse):
    steps = first.shape[0]
    return pl.pallas_call(
        functools.partial(
            backward_kernel, steps > WINDOW // BLK, steps.bit_length() - 1, which
        ),
        out_shape=(
            jax.ShapeDtypeStruct((HEADS * HD, BLK), bf16),
            jax.ShapeDtypeStruct(first.shape, bf16),
            jax.ShapeDtypeStruct(second.shape, bf16),
        ),
        in_specs=[SMEM_SPEC] * 3 + [VMEM_SPEC] * 6,
        out_specs=(VMEM_SPEC,) * 3,
        scratch_shapes=[
            pltpu.VMEM((LANES, 2 * KVH * GCOLS), bf16),
            pltpu.VMEM((2 * KVH * GCOLS, LANES), bf16),
            pltpu.VMEM((1, HEADS * BLK), f32),
            pltpu.VMEM((2 * BLK, 2 * KVH * GCOLS), bf16),
            pltpu.VMEM((HD, HEADS * BLK), f32),
        ],
        compiler_params=pltpu.CompilerParams(vmem_limit_bytes=16 << 20),
        cost_estimate=pl.CostEstimate(
            flops=10 * HEADS * HD * BLK * BLK,
            bytes_accessed=first.size,
            transcendentals=HEADS * BLK * BLK,
        ),
        name="attention_backward",
    )(*tables, first, second, queries_t, grads_t, out_t, lse)


def block_kernel(
    x_ref,
    cot_ref,
    att_ref,
    out_w_ref,
    gain_ref,
    gate_w_ref,
    up_w_ref,
    down_w_ref,
    hidden_ref,
    grads_ref,
    normed_ref,
    layer_ref,
    grad_mixed_ref,
    grad_low_ref,
    grad_att_ref,
    gain_grad_ref,
    mixed,
    normed,
    cot,
    grad_normed,
    layer,
):
    step = pl.program_id(0)

    @pl.when(step == 0)
    def _():
        cot[...] = cot_ref[...].T
        values = x_ref[...].astype(f32).T + dot(att_ref[...], out_w_ref[...], 0, 0)
        mixed[...] = values
        inverse = lax.rsqrt(jnp.mean(values * values, axis=-1, keepdims=True) + EPS)
        low = (values * inverse * gain_ref[...]).astype(bf16)
        normed[...] = low
        normed_ref[...] = low.T
        layer[...] = values
        grad_normed[...] = jnp.zeros_like(grad_normed)

    grad_hidden = dot(cot[...], down_w_ref[...], 1, 0)
    gate = dot(normed[...], gate_w_ref[...], 1, 0)
    up = dot(normed[...], up_w_ref[...], 1, 0)
    sigmoid = jax.nn.sigmoid(gate)
    silu = gate * sigmoid
    hidden = (silu * up).astype(bf16)
    grad_gate = (grad_hidden * up * sigmoid * (1.0 + gate * (1.0 - sigmoid))).astype(bf16)
    grad_up = (grad_hidden * silu).astype(bf16)
    hidden_ref[...] = hidden
    grads_ref[0] = grad_gate
    grads_ref[1] = grad_up
    layer[...] += dot(hidden, down_w_ref[...], 1, 1)
    grad_normed[...] += dot(grad_gate, gate_w_ref[...], 1, 1) + dot(
        grad_up, up_w_ref[...], 1, 1
    )

    @pl.when(step == pl.num_programs(0) - 1)
    def _():
        values = mixed[...]
        layer_ref[...] = layer[...].astype(bf16).T
        inverse = lax.rsqrt(jnp.mean(values * values, axis=-1, keepdims=True) + EPS)
        grads = grad_normed[...]
        gain_grad_ref[...] = jnp.sum(grads * values * inverse, axis=0, keepdims=True)
        scaled = grads * gain_ref[...]
        cubed = inverse * inverse * inverse
        back = inverse * scaled - values * cubed * jnp.mean(
            scaled * values, axis=-1, keepdims=True
        )
        grad_mixed = cot[...].astype(f32) + back
        low = grad_mixed.astype(bf16)
        grad_mixed_ref[...] = grad_mixed.T
        grad_low_ref[...] = low
        grad_att_ref[...] = dot(out_w_ref[...], low, 1, 1).astype(bf16)


def feed_forward(x_t, cot_t, attended_t, out_w, gain, gate_w, up_w, down_w_t):
    width, rows = x_t.shape
    inner = gate_w.shape[1]
    tile = 512

    def fixed(shape):
        return pl.BlockSpec(shape, lambda i: (0,) * len(shape))

    weight = pl.BlockSpec((width, tile), lambda i: (0, i))
    wide = (width, rows)
    return pl.pallas_call(
        block_kernel,
        grid=(inner // tile,),
        in_specs=[fixed(wide)] * 3
        + [fixed(out_w.shape), fixed((1, width)), weight, weight, weight],
        out_specs=(
            pl.BlockSpec((rows, tile), lambda i: (0, i)),
            pl.BlockSpec((2, rows, tile), lambda i: (0, 0, i)),
            fixed(wide),
            fixed(wide),
            fixed(wide),
            fixed((rows, width)),
            fixed(wide),
            fixed((1, width)),
        ),
        out_shape=(
            pltpu.HBM((rows, inner), bf16),
            pltpu.HBM((2, rows, inner), bf16),
            pltpu.HBM(wide, bf16),
            pltpu.HBM(wide, bf16),
            pltpu.HBM(wide, f32),
            pltpu.HBM((rows, width), bf16),
            pltpu.HBM(wide, bf16),
            pltpu.HBM((1, width), f32),
        ),
        scratch_shapes=[
            pltpu.VMEM((rows, width), f32),
            pltpu.VMEM((rows, width), bf16),
            pltpu.VMEM((rows, width), bf16),
            pltpu.VMEM((rows, width), f32),
            pltpu.VMEM((rows, width), f32),
        ],
        compiler_params=pltpu.CompilerParams(vmem_limit_bytes=32 << 20),
        cost_estimate=pl.CostEstimate(
            flops=12 * rows * width * inner,
            bytes_accessed=8 * width * inner,
            transcendentals=rows * inner,
        ),
        name="feed_forward",
    )(*in_hbm([x_t, cot_t, attended_t, out_w, gain, gate_w, up_w, down_w_t]))


def weight_grad_kernel(products, sides, ids, *refs):
    values = []
    for number, (by_shard, right_t) in enumerate(products):
        left, left_other, right, right_other = refs[4 * number : 4 * number + 4]
        rows = left_other.shape[0]
        start = pl.multiple_of(ids[1] * rows if by_shard else 0, 8)
        dim = 1 if right_t else 0
        values.append(
            dot(left[pl.ds(start, rows), :], right[...].reshape(right.shape[-2:]), 1, dim)
            + dot(left_other[...], right_other[...].reshape(right_other.shape[-2:]), 1, dim)
        )
    outs = refs[4 * len(products) :]
    for number, (product, first, rows, bit) in enumerate(sides):
        sent, kept = outs[2 * number : 2 * number + 2]
        half = rows // 2
        low = values[product][first : first + half].astype(bf16)
        high = values[product][first + half : first + rows].astype(bf16)
        own = (ids[0] >> bit) & 1

        @pl.when(own == 0)
        def _():
            kept[...] = low
            sent[...] = high

        @pl.when(own != 0)
        def _():
            kept[...] = high
            sent[...] = low


def weight_grad(name, ids, products, operands, right_specs, sides, tiles, columns):
    tile = columns // tiles
    specs = []
    for (left, left_other, _, _), rights in zip(operands, right_specs):
        specs += [
            pl.BlockSpec(left.shape, lambda i, ids: (0, 0)),
            pl.BlockSpec(left_other.shape, lambda i, ids: (0, 0)),
            *rights,
        ]
    shapes = [(side[2] // 2, columns) for side in sides for _ in range(2)]
    return pl.pallas_call(
        functools.partial(weight_grad_kernel, products, sides),
        grid_spec=pltpu.PrefetchScalarGridSpec(
            num_scalar_prefetch=1,
            grid=(tiles,),
            in_specs=specs,
            out_specs=[pl.BlockSpec((rows, tile), lambda i, ids: (0, i)) for rows, _ in shapes],
        ),
        out_shape=[pltpu.HBM(shape, bf16) for shape in shapes],
        compiler_params=pltpu.CompilerParams(vmem_limit_bytes=16 << 20),
        cost_estimate=pl.CostEstimate(
            flops=2 * sum(rows * width for rows, width in shapes) * 512,
            bytes_accessed=2 * sum(rows * width for rows, width in shapes),
            transcendentals=0,
        ),
        name=name,
    )(ids, *in_hbm([o for group in operands for o in group]))


def keyval_grad_kernel(left, own, other, out, total):
    step = pl.program_id(0)
    tokens = own.shape[1]
    value = dot(left[0, :, :tokens], own[0], 1, 0) + dot(left[0, :, tokens:], other[0], 1, 0)

    @pl.when(step == 0)
    def _():
        total[...] = value

    @pl.when(step != 0)
    def _():
        total[...] += value

    @pl.when(step == pl.num_programs(0) - 1)
    def _():
        out[...] = total[...].astype(bf16)


def keyval_grad(left, own, other):
    count, rows, _ = left.shape
    columns = own.shape[2]

    def block(value):
        return pl.BlockSpec((1,) + value.shape[1:], lambda i: (i, 0, 0))

    return pl.pallas_call(
        keyval_grad_kernel,
        grid=(count,),
        in_specs=[block(left), block(own), block(other)],
        out_specs=pl.BlockSpec((rows, columns), lambda i: (0, 0)),
        out_shape=jax.ShapeDtypeStruct((rows, columns), bf16),
        scratch_shapes=[pltpu.VMEM((rows, columns), f32)],
        compiler_params=pltpu.CompilerParams(vmem_limit_bytes=12 << 20),
        cost_estimate=pl.CostEstimate(
            flops=2 * left.size * columns,
            bytes_accessed=2 * (left.size + 2 * own.size),
            transcendentals=0,
        ),
        name="keyval_grad",
    )(left, own, other)


def per_device(
    inputs,
    gain_attn,
    w_query,
    w_keyval,
    w_out,
    gain_mlp,
    w_gate,
    w_up,
    w_down,
    cotangent,
    seq_blocks,
    block_slots,
):
    micro = inputs.shape[0]
    shard = lax.axis_index("fsdp")
    is_low = shard == 0
    ids = jnp.stack([lax.axis_index("ctx"), shard]).astype(jnp.int32)
    rounds = Rounds()

    def joined(part, other):
        return jnp.concatenate(
            [jnp.where(is_low, part, other), jnp.where(is_low, other, part)], axis=0
        )

    def whole(part):
        return lax.all_gather(part, "fsdp", axis=0, tiled=True)

    def theirs(value, dim):
        half = value.shape[dim] // 2
        return lax.dynamic_slice_in_dim(value, (1 - shard) * half, half, dim)

    def tokens_last(value):
        return jnp.concatenate([value[m, 0].T for m in range(micro)], axis=1)

    out_full = whole(w_out)
    gate_full = whole(w_gate)
    up_full = whole(w_up)
    down_full_t = whole(w_down).T

    attn_gain = joined(gain_attn, swap_fsdp(gain_attn)).astype(f32)[:, None]
    keyval_full = joined(w_keyval, swap_fsdp(w_keyval))
    x_t = tokens_last(inputs)
    in_t = x_t.astype(f32)
    inverse_attn = lax.rsqrt(jnp.mean(in_t * in_t, axis=0, keepdims=True) + EPS)
    normed_t = (in_t * inverse_attn * attn_gain).astype(bf16)
    keyvals = dot(normed_t, keyval_full, 0, 0).astype(bf16)
    gathers = [GatherBlocks(keyvals[m * BLK : (m + 1) * BLK]) for m in range(micro)]

    rounds.begin(gathers[0])
    (w_query, gain_mlp, cotangent, normed_t) = rounds.end(
        gathers[:1], w_query, gain_mlp, cotangent, normed_t
    )
    rounds.begin(*gathers)
    query_other, gain_other = swap_fsdp(w_query), swap_fsdp(gain_mlp)
    cot_t = tokens_last(cotangent)
    (query_other, gain_other, cot_t) = rounds.end(gathers, query_other, gain_other, cot_t)
    half = normed_t.shape[0] // 2
    normed_mine = lax.dynamic_slice_in_dim(normed_t, shard * half, half, 0)
    for step in range(len(gathers[0].stages)):
        rounds.begin(*[g for g in gathers if len(g.stages) > 2 or g is gathers[0]])
        if step == 0:
            normed_other = swap_fsdp(theirs(normed_t, 0))
            query_full = joined(w_query, query_other)
            mlp_gain = joined(gain_mlp, gain_other).astype(f32)[None]
            (normed_other, mlp_gain) = rounds.end(list(rounds.flying), normed_other, mlp_gain)
        elif step == 1:
            column = GatherHigh(jnp.concatenate([normed_mine, normed_other], axis=1))
            rounds.begin(column)
            cot_other = swap_fsdp(cot_t)
            queries_t = dot(query_full, normed_t, 0, 0).astype(bf16)
            (cot_other, queries_t) = rounds.end(
                [j for j in rounds.flying if j is not column], cot_other, queries_t
            )
        else:
            rounds.end([j for j in rounds.flying if j is not column])
    queries = [queries_t[:, m * BLK : (m + 1) * BLK] for m in range(micro)]
    tables = (ids, seq_blocks, block_slots)

    rounds.begin(gathers[1])
    rounds.end([gathers[1], column])
    rounds.begin(gathers[1], column)
    first = attention_forward(0, tables, *gathers[0].halves, queries[0])
    first = rounds.end(gathers[1:], *first)
    second = attention_forward(1, tables, *gathers[1].halves, queries[1])
    second = rounds.end([column], *second)
    rounds.run(column, 0)
    outs, lses = zip(first, second)
    attended_t = jnp.concatenate(outs, axis=1).astype(bf16)

    attended_other = swap_fsdp(theirs(attended_t, 0))
    (
        hidden,
        grad_inner,
        normed_mlp_t,
        layer_out_t,
        grad_mixed_t,
        grad_mixed_low,
        grad_attended_t,
        mlp_gain_grad,
    ) = feed_forward(
        x_t, cot_t, attended_t, out_full, mlp_gain, gate_full, up_full, down_full_t
    )
    hidden_other = swap_fsdp(theirs(hidden, 1))
    mlp_other = swap_fsdp(theirs(normed_mlp_t, 0))
    inner_other = swap_fsdp(grad_inner)

    part = hidden_other.shape[1]
    width = cot_t.shape[0]
    tokens, inner = hidden.shape
    near = pl.BlockSpec((tokens, part // 2), lambda i, ids: (0, ids[1] * 2 + i))
    far = pl.BlockSpec((tokens, part // 2), lambda i, ids: (0, i))
    down_job = Reduce(
        weight_grad(
            "down_grad",
            ids,
            ((False, False),),
            ((cot_t, cot_other, hidden, hidden_other),),
            ((near, far),),
            ((0, 0, half, 0), (0, half, half, 1)),
            2,
            part,
        ),
        (1, 0),
    )

    def attention_back(m):
        return attention_backward(
            m,
            tables,
            *gathers[m].halves,
            queries[m],
            grad_attended_t[:, m * BLK : (m + 1) * BLK],
            outs[m],
            lses[m],
        )

    rounds.prepare(down_job)
    (grad_inner, inner_other, grad_attended_t, grad_mixed_low, normed_mlp_t, mlp_other) = rounds.end(
        [], grad_inner, inner_other, grad_attended_t, grad_mixed_low, normed_mlp_t, mlp_other
    )

    rounds.begin(down_job)
    spec = pl.BlockSpec((1, tokens, inner // 5), lambda i, ids: (i // 5, 0, i % 5))
    inner_job = Reduce(
        weight_grad(
            "inner_grad",
            ids,
            ((True, False),),
            ((normed_mlp_t, mlp_other, grad_inner, inner_other),),
            ((spec, spec),),
            ((0, 0, half // 2, 0), (0, half // 2, half // 2, 1)),
            10,
            2 * inner,
        ),
        (1, 1),
    )
    rounds.prepare(inner_job)
    (grad_attended_t, grad_mixed_low) = rounds.end([], grad_attended_t, grad_mixed_low)

    rounds.begin(inner_job)
    (grad_attended_t, grad_mixed_low) = rounds.end([down_job], grad_attended_t, grad_mixed_low)

    back_first = attention_back(0)
    key_first = ScatterBlocks(*back_first[1:])
    rounds.prepare(down_job, key_first)
    (grad_attended_t, grad_mixed_low, *back_first) = rounds.end(
        [inner_job], grad_attended_t, grad_mixed_low, *back_first
    )
    key_first.halves = back_first[1:]

    rounds.begin(down_job, key_first)
    rounds.prepare(inner_job)
    back_second = attention_back(1)
    key_second = ScatterBlocks(*back_second[1:])
    rounds.prepare(key_second)
    mixed_other = swap_fsdp(grad_mixed_low)
    (mixed_other, *back_second) = rounds.end([down_job, key_first], mixed_other, *back_second)
    key_second.halves = back_second[1:]

    rounds.begin(inner_job, key_second, down_job)
    rounds.prepare(key_first)
    grad_queries_t = jnp.concatenate([back_first[0], back_second[0]], axis=1)
    queries_other = swap_fsdp(grad_queries_t)
    (queries_other, grad_queries_t) = rounds.end(
        [inner_job, down_job], queries_other, grad_queries_t
    )

    rounds.begin(down_job, inner_job, key_first)
    flat = pl.BlockSpec((width, tokens), lambda i, ids: (0, 0))
    flat_half = pl.BlockSpec((tokens, width), lambda i, ids: (0, 0))
    query_job = Reduce(
        weight_grad(
            "query_grad",
            ids,
            ((True, True), (True, False)),
            (
                (normed_t, normed_other, grad_queries_t, queries_other),
                (attended_t, attended_other, grad_mixed_low, mixed_other),
            ),
            ((flat, flat), (flat_half, flat_half)),
            ((0, 0, half, 0), (1, 0, half, 1)),
            1,
            width,
        ),
        (0, 1),
    )
    rounds.prepare(query_job)
    (grad_queries_t,) = rounds.end([key_second, down_job], grad_queries_t)
    rounds.run(down_job, 0)
    down_spread = Spread(down_job)

    rounds.begin(query_job, down_spread)
    rounds.prepare(key_second)
    rounds.end([key_first, down_spread, inner_job])
    rounds.run(down_spread, 3)

    rounds.begin(key_second, down_spread, inner_job)
    grad_normed_t = dot(query_full, grad_queries_t, 1, 0)
    (grad_normed_t,) = rounds.end(
        [key_second, query_job, down_spread, inner_job], grad_normed_t
    )
    rounds.run(inner_job, 0)
    inner_spread = Spread(inner_job)

    rounds.begin(down_spread, query_job, inner_spread)
    parts = [part for job in (key_first, key_second) for part in job.halves]
    key_column = jnp.concatenate(parts, axis=1)
    key_other = swap_fsdp(key_column)
    last_job = Solo(keyval_grad(column.held, key_column, key_other))
    rounds.prepare(last_job)
    (key_column,) = rounds.end([down_spread, query_job, inner_spread], key_column)
    rounds.run(inner_spread, 3)
    key_job = ScatterHigh(key_column)

    rounds.begin(last_job, down_spread, inner_spread, query_job)
    rounds.end([last_job, down_spread, inner_spread, query_job])

    rounds.begin(last_job, inner_spread, key_job, query_job)
    down_sum = rows_of(down_spread.quarters)
    (down_sum,) = rounds.end([last_job, inner_spread, key_job, query_job], down_sum)
    rounds.run(query_job, 0)
    rounds.run(key_job, 1)
    query_spread = Spread(query_job)

    rounds.begin(inner_spread, last_job, key_job, query_spread)
    rounds.end([last_job, key_job, query_spread])
    rounds.run(last_job, 3)
    rounds.run(query_spread, 3)

    rounds.begin(last_job, query_spread)
    grad_keyvals = key_job.held[0]
    grad_normed_t = grad_normed_t + dot(keyval_full, grad_keyvals, 1, 1)
    attn_gain_grad = jnp.sum(grad_normed_t * in_t * inverse_attn, axis=1)
    gains = jnp.stack([attn_gain_grad, mlp_gain_grad[0]])
    gains_other = swap_fsdp(theirs(gains, 1))
    gains_mine = lax.dynamic_slice_in_dim(gains, shard * half, half, 1)
    (grad_normed_t, gains_mine, gains_other) = rounds.end(
        [last_job, query_spread], grad_normed_t, gains_mine, gains_other
    )
    gain_job = SumVector((gains_mine + gains_other).reshape(-1))

    rounds.begin(last_job, query_spread, gain_job)
    scaled = grad_normed_t * attn_gain
    cubed = inverse_attn * inverse_attn * inverse_attn
    input_grad_t = (
        grad_mixed_t
        + inverse_attn * scaled
        - in_t * cubed * jnp.mean(scaled * in_t, axis=0, keepdims=True)
    )
    (input_grad_t,) = rounds.end(
        [inner_spread, last_job, query_spread, gain_job], input_grad_t
    )

    rounds.begin(last_job, query_spread, gain_job)
    gate_sum = rows_of(inner_spread.quarters, slice(0, inner))
    (gate_sum,) = rounds.end([gain_job], gate_sum)
    rounds.begin(gain_job)
    up_sum = rows_of(inner_spread.quarters, slice(inner, None))
    (up_sum,) = rounds.end([last_job, gain_job], up_sum)
    rounds.begin(gain_job)
    rounds.end([query_spread, gain_job])
    rounds.run(gain_job, 0)

    def by_token(value_t):
        parts = [value_t[:, m * BLK : (m + 1) * BLK].T[None] for m in range(micro)]
        return jnp.stack(parts)

    return (
        by_token(layer_out_t),
        by_token(input_grad_t),
        gain_job.value[:half],
        rows_of(query_spread.quarters[:2]),
        last_job.value,
        rows_of(query_spread.quarters[2:]),
        gain_job.value[half:],
        gate_sum,
        up_sum,
        down_sum.T,
    )


def solution(mesh):
    tokens = P(None, "fsdp", "ctx", None)
    vector = P("fsdp")
    matrix = P("fsdp", None)
    return jax.shard_map(
        per_device,
        mesh=mesh,
        in_specs=(
            tokens,
            vector,
            matrix,
            matrix,
            matrix,
            vector,
            matrix,
            matrix,
            matrix,
            tokens,
            P(),
            P(),
        ),
        out_specs=(
            tokens,
            tokens,
            vector,
            matrix,
            matrix,
            matrix,
            vector,
            matrix,
            matrix,
            matrix,
        ),
        check_vma=False,
    )
```

```python
import functools

import jax
import jax.numpy as jnp
from jax import lax
from jax.experimental import pallas as pl
from jax.experimental.pallas import tpu as pltpu
from jax.sharding import PartitionSpec as P

HEADS = 15
KVH = 5
HD = 64
REP = HEADS // KVH
WINDOW = 2048
BLK = 128
HALF = BLK // 2
KVW = 2 * KVH * HD
EPS = 1e-05
NEG = -1e30
SCALE = HD ** (-0.5)
LANES = 128
GCOLS = REP * BLK

bf16 = jnp.bfloat16
f32 = jnp.float32


def dot(left, right, left_dim, right_dim):
    return lax.dot_general(
        left, right, (((left_dim,), (right_dim,)), ((), ())), preferred_element_type=f32
    )


def flip_ctx(value, bit):
    size = lax.axis_size("ctx")
    return lax.ppermute(value, "ctx", [(i, i ^ (1 << bit)) for i in range(size)])


def swap_fsdp(value):
    return lax.ppermute(value, "fsdp", [(0, 1), (1, 0)])


def tie(values):
    return lax.optimization_barrier(tuple(values))


def own_bit(bit):
    return (lax.axis_index("ctx") >> bit) & 1


def high_bits():
    return list(range(2, lax.axis_size("ctx").bit_length() - 1))


def add_low(kept, arrived):
    return (kept.astype(f32) + arrived.astype(f32)).astype(bf16)


def by_bit(bit, mine, arrived):
    low = own_bit(bit) == 0
    return jnp.where(low, mine, arrived), jnp.where(low, arrived, mine)


def in_order(bit, mine, arrived, dim):
    return jnp.concatenate(by_bit(bit, mine, arrived), axis=dim)


class GatherBlocks:
    def __init__(self, block):
        self.held = block[None]
        self.stages = high_bits()[::-1] + [None, None]
        self.halves = None

    def operands(self):
        if self.stages[0] is not None:
            return [self.held], [self.stages[0]]
        if self.halves is None:
            self.halves = [self.held[:, :HALF], self.held[:, HALF:]]
            self.bits = (1, 0)
        return self.halves, self.bits

    def absorb(self, arrived):
        if self.stages.pop(0) is not None:
            self.held = jnp.concatenate([self.held, arrived[0]], axis=0)
        else:
            self.halves = [
                jnp.concatenate([h, a], axis=0) for h, a in zip(self.halves, arrived)
            ]
            self.bits = (0, 1)


class ScatterBlocks:
    def __init__(self, first, second):
        self.halves = [first, second]
        self.bits = (0, 1)
        self.stages = [None, None]

    def operands(self):
        count = self.halves[0].shape[0] // 2
        return [half[count:] for half in self.halves], self.bits

    def absorb(self, arrived):
        self.stages.pop(0)
        count = self.halves[0].shape[0] // 2
        self.halves = [add_low(half[:count], a) for half, a in zip(self.halves, arrived)]
        self.bits = (1, 0)


def cut(value, bit, dim):
    half = value.shape[dim] // 2
    own = own_bit(bit)
    sent = lax.dynamic_slice_in_dim(value, (1 - own) * half, half, dim)
    return lax.dynamic_slice_in_dim(value, own * half, half, dim), sent


class Reduce:
    def __init__(self, parts, dims):
        self.first = [parts[0], parts[2]]
        self.kept = [parts[1], parts[3]]
        self.dims = dims
        self.stages = [(0, 1), (1, 0)] + high_bits()

    def operands(self):
        stage = self.stages[0]
        if self.first is not None:
            sent, self.first = self.first, None
        elif isinstance(stage, tuple):
            parts = [cut(v, b, self.dims[0]) for v, b in zip(self.pair, stage)]
            self.kept = [p[0] for p in parts]
            sent = [p[1] for p in parts]
        else:
            if self.pair is not None:
                kept, out = by_bit(stage, *self.pair)
                self.pair = None
            else:
                kept, out = cut(self.held, stage, self.dims[1])
            self.kept, sent, stage = [kept], [out], [stage]
        return sent, stage

    def absorb(self, arrived):
        sums = [add_low(k, a) for k, a in zip(self.kept, arrived)]
        if isinstance(self.stages.pop(0), tuple):
            self.pair = sums
        else:
            self.held = sums[0]


class Spread:
    def __init__(self, job):
        self.held = job.held
        self.dims = job.dims
        self.stages = high_bits()[::-1] + [(1, 0), (0, 1)]
        self.pair = None

    def operands(self):
        stage = self.stages[0]
        if isinstance(stage, tuple):
            return self.pair, stage
        return [self.held], [stage]

    def absorb(self, arrived):
        stage = self.stages.pop(0)
        if isinstance(stage, tuple):
            parts = [by_bit(b, v, a) for v, a, b in zip(self.pair, arrived, stage)]
            if self.stages:
                self.pair = [jnp.concatenate(p, axis=self.dims[0]) for p in parts]
            else:
                self.quarters = [q for p in parts for q in p]
        elif stage == 2:
            self.pair = list(by_bit(stage, self.held, arrived[0]))
        else:
            self.held = in_order(stage, self.held, arrived[0], self.dims[1])


class GatherHigh:
    def __init__(self, value):
        self.held = value[None]
        self.stages = high_bits()[::-1]

    def operands(self):
        return [self.held], [self.stages[0]]

    def absorb(self, arrived):
        self.stages.pop(0)
        self.held = jnp.concatenate([self.held, arrived[0]], axis=0)


class ScatterHigh:
    def __init__(self, held):
        self.held = held
        self.stages = high_bits()

    def operands(self):
        return [self.held[self.held.shape[0] // 2 :]], [self.stages[0]]

    def absorb(self, arrived):
        self.stages.pop(0)
        self.held = add_low(self.held[: self.held.shape[0] // 2], arrived[0])


class Exchange:
    def __init__(self, arrays, bits):
        self.arrays, self.bits = arrays, bits
        self.stages = [None]

    def operands(self):
        return self.arrays, self.bits

    def absorb(self, arrived):
        self.stages.pop()
        self.came = arrived


def four_rows(own, first, second, last, dim):
    rows = []
    for n, (low, high) in enumerate(((1, 0), (0, 1))):
        mine = in_order(low, own[n], first[n], dim)
        rows += by_bit(high, mine, in_order(low, second[n], last[n], dim))
    return rows


class SumVector:
    def __init__(self, value):
        self.value = value
        self.stages = high_bits() + [0, 1]

    def operands(self):
        return [self.value], [self.stages[0]]

    def absorb(self, arrived):
        self.stages.pop(0)
        self.value = self.value + arrived[0]


def rows_of(quarters, columns=slice(None)):
    return jnp.concatenate([q[:, columns] for q in quarters], axis=0).astype(f32)


class Solo:
    def __init__(self, value):
        self.value = value
        high = [(bit, None) for bit in high_bits()]
        self.stages = [(0, True), (1, True)] + high + [(1, False), (0, False)]

    def operands(self):
        bit, cuts = self.stages[0]
        if not cuts:
            return [self.value], [bit]
        self.value, sent = cut(self.value, bit, 0)
        return [sent], [bit]

    def absorb(self, arrived):
        bit, cuts = self.stages.pop(0)
        if cuts is not False:
            self.value = add_low(self.value, arrived[0])
        else:
            kind = bf16 if self.stages else f32
            self.value = in_order(bit, self.value.astype(kind), arrived[0].astype(kind), 0)


class Rounds:
    def __init__(self):
        self.flying = {}
        self.ready = {}
        self.fresh = []

    def begin(self, *jobs):
        for job in jobs:
            arrays, bits = self.ready.pop(job, None) or job.operands()
            self.flying[job] = [flip_ctx(v, b) for v, b in zip(arrays, bits)]

    def prepare(self, *jobs):
        for job in jobs:
            self.ready[job] = job.operands()
            self.fresh.append(job)

    def end(self, jobs, *values):
        ahead = [job for job in self.fresh if job in self.ready]
        self.fresh = []
        arrays = [a for job in jobs for a in self.flying[job]]
        sent = [a for job in ahead for a in self.ready[job][0]]
        rest = list(tie([*values, *arrays, *sent]))
        values, rest = rest[: len(values)], rest[len(values) :]
        for job in jobs:
            count = len(self.flying.pop(job))
            job.absorb(rest[:count])
            rest = rest[count:]
        for job in ahead:
            count = len(self.ready[job][0])
            self.ready[job] = (rest[:count], self.ready[job][1])
            rest = rest[count:]
        return values

    def run(self, job, left):
        while len(job.stages) > left:
            self.begin(job)
            self.end([job])


def key_tile(first_ref, second_ref, places, unit):
    lanes = pl.ds(pl.multiple_of((unit // 2) * LANES, LANES), LANES)
    parts = []
    for first, second in places:
        parts += [first_ref[first, :, lanes], second_ref[second, :, lanes]]
    return jnp.concatenate(parts, axis=0)


def heads_t(rows_t, group, unit):
    parts = [
        rows_t[(group * REP + r) * HD : (group * REP + r + 1) * HD, :] for r in range(REP)
    ]
    block = jnp.concatenate(parts, axis=1)
    zero = jnp.zeros_like(block)
    return jnp.concatenate([zero, block] if unit % 2 else [block, zero], axis=0)


def half_rows(tile_t, unit):
    return tile_t[(unit % 2) * HD : (unit % 2 + 1) * HD, :]


def seen_blocks(bits, which, ids, lengths, slots):
    me, shard = ids[0], ids[1]

    def look(j, own):
        return jnp.where(slots[which, shard, j] == me, j, own)

    own = lax.fori_loop(0, slots.shape[2], look, jnp.int32(0))
    end = jnp.int32(0)
    start = jnp.int32(0)
    for i in range(lengths.shape[2]):
        end = end + lengths[which, shard, i]
        start = jnp.where(end <= own, end, start)
    lowest = jnp.maximum(start, own - WINDOW // BLK)

    def places(index):
        relative = slots[which, shard, jnp.maximum(own - index, 0)] ^ me
        high = jnp.int32(0)
        for position, bit in enumerate(range(bits - 1, 1, -1)):
            high = high | (((relative >> bit) & 1) << position)
        one = (relative & 1) << (bits - 1)
        two = ((relative >> 1) & 1) << (bits - 2)
        swapped = ((relative & 1) << (bits - 2)) | (((relative >> 1) & 1) << (bits - 1))
        return high | one | two, high | swapped

    return own - lowest + 1, places


def pair_mask(far, count, index):
    key = lax.broadcasted_iota(jnp.int32, (BLK, GCOLS), 0)
    query = lax.broadcasted_iota(jnp.int32, (BLK, GCOLS), 1) & (BLK - 1)
    ahead = key - query
    masks = []
    for i in (index, index + 1):
        most = jnp.where(i < count, i * BLK, -2 * BLK)
        mask = ahead <= most
        if far:
            mask = mask & (ahead > i * BLK - WINDOW)
        masks.append(mask)
    return jnp.concatenate(masks, axis=0)


def lanes_at(start, size=LANES):
    return pl.ds(pl.multiple_of(start, LANES), size)


def spread_heads(source_ref, pad_ref, unit, group):
    parts = [
        source_ref[pl.ds(pl.multiple_of((group * REP + r) * HD, HD), HD), :] for r in range(REP)
    ]
    row = pl.multiple_of((unit % 2) * HD, HD)
    pad_ref[pl.ds(row, HD), lanes_at(unit * GCOLS, GCOLS)] = jnp.concatenate(parts, axis=1)


def forward_kernel(
    far, bits, which, ids, lengths, slots, first_ref, second_ref, query_ref, out_ref, lse_ref, pad_ref, half_ref
):
    count, places = seen_blocks(bits, which, ids, lengths, slots)
    pad_ref[...] = jnp.zeros_like(pad_ref)

    @pl.loop(0, KVH)
    def _(group):
        spread_heads(query_ref, pad_ref, group, group)
        columns = lanes_at(group * GCOLS, GCOLS)
        value_unit = KVH + group

        def step(pair, carried):
            high, total, acc = carried
            index = 2 * pair
            held = (places(index), places(index + 1))
            keys = key_tile(first_ref, second_ref, held, group)
            values = key_tile(first_ref, second_ref, held, value_unit)
            scores = dot(keys, pad_ref[:, columns], 1, 0) * SCALE
            scores = jnp.where(pair_mask(far, count, index), scores, NEG)
            new_high = jnp.maximum(high, jnp.max(scores, axis=0, keepdims=True))
            weights = jnp.exp(scores - new_high)
            fade = jnp.exp(high - new_high)
            total = total * fade + jnp.sum(weights, axis=0, keepdims=True)
            acc = acc * fade + dot(values.T, weights.astype(bf16), 1, 0)
            return (new_high, total, acc)

        start = (
            jnp.full((1, GCOLS), NEG, f32),
            jnp.zeros((1, GCOLS), f32),
            jnp.zeros((LANES, GCOLS), f32),
        )
        high, total, acc = lax.fori_loop(0, (count + 1) // 2, step, start)
        half_ref[...] = acc / total
        row = pl.multiple_of((value_unit % 2) * HD, HD)
        for r in range(REP):
            head_rows = pl.ds(pl.multiple_of((group * REP + r) * HD, HD), HD)
            out_ref[head_rows, :] = half_ref[pl.ds(row, HD), r * BLK : (r + 1) * BLK]
        lse_ref[:, columns] = high + jnp.log(total)


def backward_kernel(
    far,
    bits,
    which,
    ids,
    lengths,
    slots,
    first_ref,
    second_ref,
    query_ref,
    grad_ref,
    out_ref,
    lse_ref,
    dq_ref,
    dfirst_ref,
    dsecond_ref,
    pad_ref,
    right_ref,
    delta_ref,
    left_ref,
    acc_ref,
):
    count, places = seen_blocks(bits, which, ids, lengths, slots)
    queries = query_ref[...]
    grads = grad_ref[...]
    product = grads.astype(f32) * out_ref[...]
    for head in range(HEADS):
        delta_ref[:, head * BLK : (head + 1) * BLK] = jnp.sum(
            product[head * HD : (head + 1) * HD, :], axis=0, keepdims=True
        )
    for unit in range(2 * KVH):
        padded = heads_t(queries if unit < KVH else grads, unit % KVH, unit)
        rows = slice(unit * GCOLS, (unit + 1) * GCOLS)
        pad_ref[:, rows] = padded
        right_ref[rows, :] = padded.T
    dfirst_ref[...] = jnp.zeros_like(dfirst_ref)
    dsecond_ref[...] = jnp.zeros_like(dsecond_ref)
    acc_ref[...] = jnp.zeros_like(acc_ref)

    @pl.loop(0, (count + 1) // 2)
    def _(pair):
        index = 2 * pair
        held = (places(index), places(index + 1))
        mask = pair_mask(far, count, index)
        for group in range(KVH):
            value_unit = KVH + group
            columns = slice(group * GCOLS, (group + 1) * GCOLS)
            value_columns = slice(value_unit * GCOLS, (value_unit + 1) * GCOLS)
            keys = key_tile(first_ref, second_ref, held, group)
            values = key_tile(first_ref, second_ref, held, value_unit)
            scores = dot(keys, pad_ref[:, columns], 1, 0) * SCALE
            probs = jnp.where(mask, jnp.exp(scores - lse_ref[:, columns]), 0.0)
            grad_probs = dot(values, pad_ref[:, value_columns], 1, 0)
            grad_scores = (probs * (grad_probs - delta_ref[:, columns])).astype(bf16)
            left_ref[:, columns] = grad_scores
            left_ref[:, value_columns] = probs.astype(bf16)
            keys_t = half_rows(keys.T, group)
            acc_ref[:, columns] += dot(keys_t, grad_scores, 1, 0)
        for tile in range(KVH):
            rows = slice(2 * tile * GCOLS, 2 * (tile + 1) * GCOLS)
            lanes = slice(tile * LANES, (tile + 1) * LANES)
            block = dot(left_ref[:, rows], right_ref[rows, :], 1, 0)
            lane = lax.broadcasted_iota(jnp.int32, (1, LANES), 1) + tile * LANES
            block = (block * jnp.where(lane < KVH * HD, SCALE, 1.0)).astype(bf16)
            first, second = held[0]
            dfirst_ref[first, :, lanes] = block[:HALF]
            dsecond_ref[second, :, lanes] = block[HALF:BLK]

            @pl.when(index + 1 < count)
            def _():
                first, second = held[1]
                dfirst_ref[first, :, lanes] = block[BLK : BLK + HALF]
                dsecond_ref[second, :, lanes] = block[BLK + HALF :]

    for head in range(HEADS):
        columns = slice(head * BLK, (head + 1) * BLK)
        dq_ref[head * HD : (head + 1) * HD, :] = (acc_ref[:, columns] * SCALE).astype(bf16)


def in_hbm(values):
    return [pltpu.with_memory_space_constraint(v, pltpu.HBM) for v in values]


VMEM_SPEC = pl.BlockSpec(memory_space=pltpu.VMEM)
SMEM_SPEC = pl.BlockSpec(memory_space=pltpu.SMEM)


def attention_forward(which, tables, first, second, queries_t):
    steps = first.shape[0]
    return pl.pallas_call(
        functools.partial(
            forward_kernel, steps > WINDOW // BLK, steps.bit_length() - 1, which
        ),
        out_shape=(
            jax.ShapeDtypeStruct((HEADS * HD, BLK), f32),
            jax.ShapeDtypeStruct((1, HEADS * BLK), f32),
        ),
        in_specs=[SMEM_SPEC] * 3 + [VMEM_SPEC] * 3,
        out_specs=(VMEM_SPEC,) * 2,
        scratch_shapes=[pltpu.VMEM((LANES, HEADS * BLK), bf16), pltpu.VMEM((LANES, GCOLS), f32)],
        compiler_params=pltpu.CompilerParams(vmem_limit_bytes=8 << 20),
        cost_estimate=pl.CostEstimate(
            flops=4 * HEADS * HD * BLK * BLK * 8,
            bytes_accessed=first.size * 4,
            transcendentals=HEADS * BLK * BLK * 8,
        ),
        name="attention_forward",
    )(*tables, first, second, queries_t)


def attention_backward(which, tables, first, second, queries_t, grads_t, out_t, lse):
    steps = first.shape[0]
    return pl.pallas_call(
        functools.partial(
            backward_kernel, steps > WINDOW // BLK, steps.bit_length() - 1, which
        ),
        out_shape=(
            jax.ShapeDtypeStruct((HEADS * HD, BLK), bf16),
            jax.ShapeDtypeStruct(first.shape, bf16),
            jax.ShapeDtypeStruct(second.shape, bf16),
        ),
        in_specs=[SMEM_SPEC] * 3 + [VMEM_SPEC] * 6,
        out_specs=(VMEM_SPEC,) * 3,
        scratch_shapes=[
            pltpu.VMEM((LANES, 2 * KVH * GCOLS), bf16),
            pltpu.VMEM((2 * KVH * GCOLS, LANES), bf16),
            pltpu.VMEM((1, HEADS * BLK), f32),
            pltpu.VMEM((2 * BLK, 2 * KVH * GCOLS), bf16),
            pltpu.VMEM((HD, HEADS * BLK), f32),
        ],
        compiler_params=pltpu.CompilerParams(vmem_limit_bytes=16 << 20),
        cost_estimate=pl.CostEstimate(
            flops=10 * HEADS * HD * BLK * BLK,
            bytes_accessed=first.size,
            transcendentals=HEADS * BLK * BLK,
        ),
        name="attention_backward",
    )(*tables, first, second, queries_t, grads_t, out_t, lse)


def block_kernel(
    x_ref,
    cot_ref,
    att_ref,
    out_w_ref,
    gain_ref,
    gate_w_ref,
    up_w_ref,
    down_w_ref,
    hidden_ref,
    grads_ref,
    normed_ref,
    layer_ref,
    grad_mixed_ref,
    grad_low_ref,
    grad_att_ref,
    gain_grad_ref,
    mixed,
    normed,
    cot,
    grad_normed,
    layer,
):
    step = pl.program_id(0)

    @pl.when(step == 0)
    def _():
        cot[...] = cot_ref[...].T
        values = x_ref[...].astype(f32).T + dot(att_ref[...], out_w_ref[...], 0, 0)
        mixed[...] = values
        inverse = lax.rsqrt(jnp.mean(values * values, axis=-1, keepdims=True) + EPS)
        low = (values * inverse * gain_ref[...]).astype(bf16)
        normed[...] = low
        normed_ref[...] = low.T
        layer[...] = values
        grad_normed[...] = jnp.zeros_like(grad_normed)

    grad_hidden = dot(cot[...], down_w_ref[...], 1, 0)
    gate = dot(normed[...], gate_w_ref[...], 1, 0)
    up = dot(normed[...], up_w_ref[...], 1, 0)
    sigmoid = jax.nn.sigmoid(gate)
    silu = gate * sigmoid
    hidden = (silu * up).astype(bf16)
    grad_gate = (grad_hidden * up * sigmoid * (1.0 + gate * (1.0 - sigmoid))).astype(bf16)
    grad_up = (grad_hidden * silu).astype(bf16)
    hidden_ref[...] = hidden
    grads_ref[0] = grad_gate
    grads_ref[1] = grad_up
    layer[...] += dot(hidden, down_w_ref[...], 1, 1)
    grad_normed[...] += dot(grad_gate, gate_w_ref[...], 1, 1) + dot(
        grad_up, up_w_ref[...], 1, 1
    )

    @pl.when(step == pl.num_programs(0) - 1)
    def _():
        values = mixed[...]
        layer_ref[...] = layer[...].astype(bf16).T
        inverse = lax.rsqrt(jnp.mean(values * values, axis=-1, keepdims=True) + EPS)
        grads = grad_normed[...]
        gain_grad_ref[...] = jnp.sum(grads * values * inverse, axis=0, keepdims=True)
        scaled = grads * gain_ref[...]
        cubed = inverse * inverse * inverse
        back = inverse * scaled - values * cubed * jnp.mean(
            scaled * values, axis=-1, keepdims=True
        )
        grad_mixed = cot[...].astype(f32) + back
        low = grad_mixed.astype(bf16)
        grad_mixed_ref[...] = grad_mixed.T
        grad_low_ref[...] = low
        grad_att_ref[...] = dot(out_w_ref[...], low, 1, 1).astype(bf16)


def feed_forward(x_t, cot_t, attended_t, out_w, gain, gate_w, up_w, down_w_t):
    width, rows = x_t.shape
    inner = gate_w.shape[1]
    tile = 512

    def fixed(shape):
        return pl.BlockSpec(shape, lambda i: (0,) * len(shape))

    weight = pl.BlockSpec((width, tile), lambda i: (0, i))
    wide = (width, rows)
    return pl.pallas_call(
        block_kernel,
        grid=(inner // tile,),
        in_specs=[fixed(wide)] * 3
        + [fixed(out_w.shape), fixed((1, width)), weight, weight, weight],
        out_specs=(
            pl.BlockSpec((rows, tile), lambda i: (0, i)),
            pl.BlockSpec((2, rows, tile), lambda i: (0, 0, i)),
            fixed(wide),
            fixed(wide),
            fixed(wide),
            fixed((rows, width)),
            fixed(wide),
            fixed((1, width)),
        ),
        out_shape=(
            pltpu.HBM((rows, inner), bf16),
            pltpu.HBM((2, rows, inner), bf16),
            pltpu.HBM(wide, bf16),
            pltpu.HBM(wide, bf16),
            pltpu.HBM(wide, f32),
            pltpu.HBM((rows, width), bf16),
            pltpu.HBM(wide, bf16),
            pltpu.HBM((1, width), f32),
        ),
        scratch_shapes=[
            pltpu.VMEM((rows, width), f32),
            pltpu.VMEM((rows, width), bf16),
            pltpu.VMEM((rows, width), bf16),
            pltpu.VMEM((rows, width), f32),
            pltpu.VMEM((rows, width), f32),
        ],
        compiler_params=pltpu.CompilerParams(vmem_limit_bytes=32 << 20),
        cost_estimate=pl.CostEstimate(
            flops=12 * rows * width * inner,
            bytes_accessed=8 * width * inner,
            transcendentals=rows * inner,
        ),
        name="feed_forward",
    )(*in_hbm([x_t, cot_t, attended_t, out_w, gain, gate_w, up_w, down_w_t]))


def weight_grad_kernel(products, sides, ids, *refs):
    values = []
    for number, (by_shard, right_t) in enumerate(products):
        left, left_other, right, right_other = refs[4 * number : 4 * number + 4]
        rows = left_other.shape[0]
        start = pl.multiple_of(ids[1] * rows if by_shard else 0, 8)
        dim = 1 if right_t else 0
        values.append(
            dot(left[pl.ds(start, rows), :], right[...].reshape(right.shape[-2:]), 1, dim)
            + dot(left_other[...], right_other[...].reshape(right_other.shape[-2:]), 1, dim)
        )
    outs = refs[4 * len(products) :]
    for number, (product, first, rows, bit) in enumerate(sides):
        sent, kept = outs[2 * number : 2 * number + 2]
        half = rows // 2
        low = values[product][first : first + half].astype(bf16)
        high = values[product][first + half : first + rows].astype(bf16)
        own = (ids[0] >> bit) & 1

        @pl.when(own == 0)
        def _():
            kept[...] = low
            sent[...] = high

        @pl.when(own != 0)
        def _():
            kept[...] = high
            sent[...] = low


def weight_grad(name, ids, products, operands, right_specs, sides, tiles, columns):
    tile = columns // tiles
    specs = []
    for (left, left_other, _, _), rights in zip(operands, right_specs):
        specs += [
            pl.BlockSpec(left.shape, lambda i, ids: (0, 0)),
            pl.BlockSpec(left_other.shape, lambda i, ids: (0, 0)),
            *rights,
        ]
    shapes = [(side[2] // 2, columns) for side in sides for _ in range(2)]
    return pl.pallas_call(
        functools.partial(weight_grad_kernel, products, sides),
        grid_spec=pltpu.PrefetchScalarGridSpec(
            num_scalar_prefetch=1,
            grid=(tiles,),
            in_specs=specs,
            out_specs=[pl.BlockSpec((rows, tile), lambda i, ids: (0, i)) for rows, _ in shapes],
        ),
        out_shape=[pltpu.HBM(shape, bf16) for shape in shapes],
        compiler_params=pltpu.CompilerParams(vmem_limit_bytes=16 << 20),
        cost_estimate=pl.CostEstimate(
            flops=2 * sum(rows * width for rows, width in shapes) * 512,
            bytes_accessed=2 * sum(rows * width for rows, width in shapes),
            transcendentals=0,
        ),
        name=name,
    )(ids, *in_hbm([o for group in operands for o in group]))


def keyval_grad_kernel(left, own, other, out, total):
    step = pl.program_id(0)
    tokens = own.shape[1]
    value = dot(left[0, :, :tokens], own[0], 1, 0) + dot(left[0, :, tokens:], other[0], 1, 0)

    @pl.when(step == 0)
    def _():
        total[...] = value

    @pl.when(step != 0)
    def _():
        total[...] += value

    @pl.when(step == pl.num_programs(0) - 1)
    def _():
        out[...] = total[...].astype(bf16)


def keyval_grad(left, own, other):
    count, rows, _ = left.shape
    columns = own.shape[2]

    def block(value):
        return pl.BlockSpec((1,) + value.shape[1:], lambda i: (i, 0, 0))

    return pl.pallas_call(
        keyval_grad_kernel,
        grid=(count,),
        in_specs=[block(left), block(own), block(other)],
        out_specs=pl.BlockSpec((rows, columns), lambda i: (0, 0)),
        out_shape=jax.ShapeDtypeStruct((rows, columns), bf16),
        scratch_shapes=[pltpu.VMEM((rows, columns), f32)],
        compiler_params=pltpu.CompilerParams(vmem_limit_bytes=12 << 20),
        cost_estimate=pl.CostEstimate(
            flops=2 * left.size * columns,
            bytes_accessed=2 * (left.size + 2 * own.size),
            transcendentals=0,
        ),
        name="keyval_grad",
    )(left, own, other)


def per_device(
    inputs,
    gain_attn,
    w_query,
    w_keyval,
    w_out,
    gain_mlp,
    w_gate,
    w_up,
    w_down,
    cotangent,
    seq_blocks,
    block_slots,
):
    micro = inputs.shape[0]
    shard = lax.axis_index("fsdp")
    is_low = shard == 0
    ids = jnp.stack([lax.axis_index("ctx"), shard]).astype(jnp.int32)
    rounds = Rounds()

    def joined(part, other):
        return jnp.concatenate(
            [jnp.where(is_low, part, other), jnp.where(is_low, other, part)], axis=0
        )

    def whole(part):
        return lax.all_gather(part, "fsdp", axis=0, tiled=True)

    def theirs(value, dim):
        half = value.shape[dim] // 2
        return lax.dynamic_slice_in_dim(value, (1 - shard) * half, half, dim)

    def tokens_last(value):
        return jnp.concatenate([value[m, 0].T for m in range(micro)], axis=1)

    out_full = whole(w_out)
    gate_full = whole(w_gate)
    up_full = whole(w_up)
    down_full_t = whole(w_down).T

    attn_gain = joined(gain_attn, swap_fsdp(gain_attn)).astype(f32)[:, None]
    keyval_full = joined(w_keyval, swap_fsdp(w_keyval))
    x_t = tokens_last(inputs)
    in_t = x_t.astype(f32)
    inverse_attn = lax.rsqrt(jnp.mean(in_t * in_t, axis=0, keepdims=True) + EPS)
    normed_t = (in_t * inverse_attn * attn_gain).astype(bf16)
    keyvals = dot(normed_t, keyval_full, 0, 0).astype(bf16)
    gathers = [GatherBlocks(keyvals[m * BLK : (m + 1) * BLK]) for m in range(micro)]

    rounds.begin(gathers[0])
    (w_query, gain_mlp, cotangent, normed_t) = rounds.end(
        gathers[:1], w_query, gain_mlp, cotangent, normed_t
    )
    rounds.begin(*gathers)
    query_other, gain_other = swap_fsdp(w_query), swap_fsdp(gain_mlp)
    cot_t = tokens_last(cotangent)
    (query_other, gain_other, cot_t) = rounds.end(gathers, query_other, gain_other, cot_t)
    half = normed_t.shape[0] // 2
    normed_mine = lax.dynamic_slice_in_dim(normed_t, shard * half, half, 0)
    for step in range(len(gathers[0].stages)):
        rounds.begin(*[g for g in gathers if len(g.stages) > 2 or g is gathers[0]])
        if step == 0:
            normed_other = swap_fsdp(theirs(normed_t, 0))
            query_full = joined(w_query, query_other)
            mlp_gain = joined(gain_mlp, gain_other).astype(f32)[None]
            (normed_other, mlp_gain) = rounds.end(list(rounds.flying), normed_other, mlp_gain)
        elif step == 1:
            column = GatherHigh(jnp.concatenate([normed_mine, normed_other], axis=1))
            rounds.begin(column)
            cot_other = swap_fsdp(cot_t)
            queries_t = dot(query_full, normed_t, 0, 0).astype(bf16)
            (cot_other, queries_t) = rounds.end(
                [j for j in rounds.flying if j is not column], cot_other, queries_t
            )
        else:
            rounds.end([j for j in rounds.flying if j is not column])
    queries = [queries_t[:, m * BLK : (m + 1) * BLK] for m in range(micro)]
    tables = (ids, seq_blocks, block_slots)

    rounds.begin(gathers[1])
    rounds.end([gathers[1], column])
    rounds.begin(gathers[1], column)
    first = attention_forward(0, tables, *gathers[0].halves, queries[0])
    first = rounds.end(gathers[1:], *first)
    second = attention_forward(1, tables, *gathers[1].halves, queries[1])
    second = rounds.end([column], *second)
    rounds.run(column, 0)
    outs, lses = zip(first, second)
    attended_t = jnp.concatenate(outs, axis=1).astype(bf16)

    attended_other = swap_fsdp(theirs(attended_t, 0))
    (
        hidden,
        grad_inner,
        normed_mlp_t,
        layer_out_t,
        grad_mixed_t,
        grad_mixed_low,
        grad_attended_t,
        mlp_gain_grad,
    ) = feed_forward(
        x_t, cot_t, attended_t, out_full, mlp_gain, gate_full, up_full, down_full_t
    )
    hidden_other = swap_fsdp(theirs(hidden, 1))
    mlp_other = swap_fsdp(theirs(normed_mlp_t, 0))
    inner_other = swap_fsdp(grad_inner)

    part = hidden_other.shape[1]
    width = cot_t.shape[0]
    tokens, inner = hidden.shape
    near = pl.BlockSpec((tokens, part // 2), lambda i, ids: (0, ids[1] * 2 + i))
    far = pl.BlockSpec((tokens, part // 2), lambda i, ids: (0, i))
    down_job = Reduce(
        weight_grad(
            "down_grad",
            ids,
            ((False, False),),
            ((cot_t, cot_other, hidden, hidden_other),),
            ((near, far),),
            ((0, 0, half, 0), (0, half, half, 1)),
            2,
            part,
        ),
        (1, 0),
    )

    def attention_back(m):
        return attention_backward(
            m,
            tables,
            *gathers[m].halves,
            queries[m],
            grad_attended_t[:, m * BLK : (m + 1) * BLK],
            outs[m],
            lses[m],
        )

    rounds.prepare(down_job)
    (grad_inner, inner_other, grad_attended_t, grad_mixed_low, normed_mlp_t, mlp_other) = rounds.end(
        [], grad_inner, inner_other, grad_attended_t, grad_mixed_low, normed_mlp_t, mlp_other
    )

    rounds.begin(down_job)
    spec = pl.BlockSpec((1, tokens, inner // 5), lambda i, ids: (i // 5, 0, i % 5))
    inner_job = Reduce(
        weight_grad(
            "inner_grad",
            ids,
            ((True, False),),
            ((normed_mlp_t, mlp_other, grad_inner, inner_other),),
            ((spec, spec),),
            ((0, 0, half // 2, 0), (0, half // 2, half // 2, 1)),
            10,
            2 * inner,
        ),
        (1, 1),
    )
    rounds.prepare(inner_job)
    (grad_attended_t, grad_mixed_low) = rounds.end([], grad_attended_t, grad_mixed_low)

    rounds.begin(inner_job)
    (grad_attended_t, grad_mixed_low) = rounds.end([down_job], grad_attended_t, grad_mixed_low)

    back_first = attention_back(0)
    key_first = ScatterBlocks(*back_first[1:])
    rounds.prepare(down_job, key_first)
    (grad_attended_t, grad_mixed_low, *back_first) = rounds.end(
        [inner_job], grad_attended_t, grad_mixed_low, *back_first
    )
    key_first.halves = back_first[1:]

    rounds.begin(down_job, key_first)
    rounds.prepare(inner_job)
    back_second = attention_back(1)
    key_second = ScatterBlocks(*back_second[1:])
    rounds.prepare(key_second)
    mixed_other = swap_fsdp(grad_mixed_low)
    (mixed_other, *back_second) = rounds.end([down_job, key_first], mixed_other, *back_second)
    key_second.halves = back_second[1:]

    rounds.begin(inner_job, key_second, down_job)
    rounds.prepare(key_first)
    grad_queries_t = jnp.concatenate([back_first[0], back_second[0]], axis=1)
    queries_other = swap_fsdp(grad_queries_t)
    (queries_other, grad_queries_t) = rounds.end(
        [inner_job, down_job], queries_other, grad_queries_t
    )

    rounds.begin(down_job, inner_job, key_first)
    flat = pl.BlockSpec((width, tokens), lambda i, ids: (0, 0))
    flat_half = pl.BlockSpec((tokens, width), lambda i, ids: (0, 0))
    query_job = Reduce(
        weight_grad(
            "query_grad",
            ids,
            ((True, True), (True, False)),
            (
                (normed_t, normed_other, grad_queries_t, queries_other),
                (attended_t, attended_other, grad_mixed_low, mixed_other),
            ),
            ((flat, flat), (flat_half, flat_half)),
            ((0, 0, half, 0), (1, 0, half, 1)),
            1,
            width,
        ),
        (0, 1),
    )
    rounds.prepare(query_job)
    (grad_queries_t,) = rounds.end([key_second, down_job, inner_job], grad_queries_t)
    rounds.run(down_job, 0)
    rounds.run(inner_job, 1)
    down_spread = Spread(down_job)

    rounds.begin(query_job, down_spread, inner_job)
    rounds.prepare(key_second)
    rounds.end([key_first, down_spread, inner_job])
    rounds.run(down_spread, 3)
    inner_spread = Spread(inner_job)

    rounds.begin(key_second, down_spread, inner_spread)
    grad_normed_t = dot(query_full, grad_queries_t, 1, 0)
    (grad_normed_t,) = rounds.end(
        [key_second, query_job, down_spread, inner_spread], grad_normed_t
    )
    rounds.run(inner_spread, 3)

    parts = [part for job in (key_first, key_second) for part in job.halves]
    key_column = jnp.concatenate(parts, axis=1)
    rounds.begin(down_spread, query_job, inner_spread)
    key_other = swap_fsdp(key_column)
    last_job = Solo(keyval_grad(column.held, key_column, key_other))
    rounds.prepare(last_job)
    (key_column,) = rounds.end([down_spread, query_job, inner_spread], key_column)
    key_job = ScatterHigh(key_column)

    own = inner_spread.pair
    first = Exchange(own, (1, 0))
    second = Exchange(own, (0, 1))
    rounds.begin(last_job, query_job, key_job, first, down_spread, second)
    rounds.end([last_job, query_job, key_job])
    rounds.run(key_job, 1)
    rounds.begin(last_job, query_job, key_job)
    rounds.end([first, down_spread, last_job, key_job, query_job])
    rounds.run(query_job, 0)
    query_spread = Spread(query_job)

    third = Exchange(first.came, (0, 1))
    rounds.begin(third, last_job, query_spread)
    grad_keyvals = key_job.held[0]
    grad_normed_t = grad_normed_t + dot(keyval_full, grad_keyvals, 1, 1)
    attn_gain_grad = jnp.sum(grad_normed_t * in_t * inverse_attn, axis=1)
    gains = jnp.stack([attn_gain_grad, mlp_gain_grad[0]])
    gains_other = swap_fsdp(theirs(gains, 1))
    gains_mine = lax.dynamic_slice_in_dim(gains, shard * half, half, 1)
    (grad_normed_t, gains_mine, gains_other) = rounds.end(
        [last_job, query_spread, second], grad_normed_t, gains_mine, gains_other
    )
    rounds.run(query_spread, 3)
    rounds.run(last_job, 3)
    gain_job = SumVector((gains_mine + gains_other).reshape(-1))

    rounds.begin(last_job, query_spread, gain_job)
    down_sum = rows_of(down_spread.quarters)
    (down_sum,) = rounds.end([last_job, query_spread, gain_job, third], down_sum)
    rounds.run(gain_job, 3)

    rounds.begin(last_job, query_spread, gain_job)
    scaled = grad_normed_t * attn_gain
    cubed = inverse_attn * inverse_attn * inverse_attn
    input_grad_t = (
        grad_mixed_t
        + inverse_attn * scaled
        - in_t * cubed * jnp.mean(scaled * in_t, axis=0, keepdims=True)
    )
    tied = rounds.end(
        [last_job, query_spread, gain_job],
        input_grad_t,
        *own,
        *first.came,
        *second.came,
        *third.came,
    )
    input_grad_t = tied[0]
    quarters = four_rows(*[tied[i : i + 2] for i in (1, 3, 5, 7)], 1)

    rounds.begin(last_job, query_spread, gain_job)
    gate_sum = rows_of(quarters, slice(0, inner))
    up_sum = rows_of(quarters, slice(inner, None))
    (gate_sum, up_sum) = rounds.end([last_job, query_spread, gain_job], gate_sum, up_sum)
    rounds.begin(gain_job)
    rounds.end([gain_job])
    rounds.run(gain_job, 0)

    def by_token(value_t):
        parts = [value_t[:, m * BLK : (m + 1) * BLK].T[None] for m in range(micro)]
        return jnp.stack(parts)

    return (
        by_token(layer_out_t),
        by_token(input_grad_t),
        gain_job.value[:half],
        rows_of(query_spread.quarters[:2]),
        last_job.value,
        rows_of(query_spread.quarters[2:]),
        gain_job.value[half:],
        gate_sum,
        up_sum,
        down_sum.T,
    )


def solution(mesh):
    tokens = P(None, "fsdp", "ctx", None)
    vector = P("fsdp")
    matrix = P("fsdp", None)
    return jax.shard_map(
        per_device,
        mesh=mesh,
        in_specs=(
            tokens,
            vector,
            matrix,
            matrix,
            matrix,
            vector,
            matrix,
            matrix,
            matrix,
            tokens,
            P(),
            P(),
        ),
        out_specs=(
            tokens,
            tokens,
            vector,
            matrix,
            matrix,
            matrix,
            vector,
            matrix,
            matrix,
            matrix,
        ),
        check_vma=False,
    )
```

```python
import functools

import jax
import jax.numpy as jnp
from jax import lax
from jax.experimental import pallas as pl
from jax.experimental.pallas import tpu as pltpu
from jax.sharding import PartitionSpec as P

HEADS = 15
KVH = 5
HD = 64
REP = HEADS // KVH
WINDOW = 2048
BLK = 128
HALF = BLK // 2
KVW = 2 * KVH * HD
EPS = 1e-05
NEG = -1e30
SCALE = HD ** (-0.5)
LANES = 128
GCOLS = REP * BLK

bf16 = jnp.bfloat16
f32 = jnp.float32


def dot(left, right, left_dim, right_dim):
    return lax.dot_general(
        left, right, (((left_dim,), (right_dim,)), ((), ())), preferred_element_type=f32
    )


def flip_ctx(value, bit):
    size = lax.axis_size("ctx")
    mask = sum(1 << b for b in bit) if isinstance(bit, tuple) else 1 << bit
    return lax.ppermute(value, "ctx", [(i, i ^ mask) for i in range(size)])


def swap_fsdp(value):
    return lax.ppermute(value, "fsdp", [(0, 1), (1, 0)])


def tie(values):
    return lax.optimization_barrier(tuple(values))


def own_bit(bit):
    return (lax.axis_index("ctx") >> bit) & 1


def high_bits():
    return list(range(2, lax.axis_size("ctx").bit_length() - 1))


def add_low(kept, arrived):
    return (kept.astype(f32) + arrived.astype(f32)).astype(bf16)


def by_bit(bit, mine, arrived):
    low = own_bit(bit) == 0
    return jnp.where(low, mine, arrived), jnp.where(low, arrived, mine)


def in_order(bit, mine, arrived, dim):
    return jnp.concatenate(by_bit(bit, mine, arrived), axis=dim)


class GatherBlocks:
    def __init__(self, block):
        self.held = block[None]
        bits = high_bits()[::-1]
        self.stages = [tuple(bits[i : i + 2]) for i in range(0, len(bits), 2)] + [None, None]
        self.halves = None

    def operands(self):
        stage = self.stages[0]
        if stage is not None:
            hops = list(stage) + ([stage] if len(stage) == 2 else [])
            return [self.held] * len(hops), hops
        if self.halves is None:
            self.halves = [self.held[:, :HALF], self.held[:, HALF:]]
            self.bits = (1, 0)
        return self.halves, self.bits

    def absorb(self, arrived):
        if self.stages.pop(0) is not None:
            self.held = jnp.concatenate([self.held, *arrived], axis=0)
        else:
            self.halves = [
                jnp.concatenate([h, a], axis=0) for h, a in zip(self.halves, arrived)
            ]
            self.bits = (0, 1)


class ScatterBlocks:
    def __init__(self, first, second):
        self.halves = [first, second]
        self.bits = (0, 1)
        self.stages = [None, None]

    def operands(self):
        count = self.halves[0].shape[0] // 2
        return [half[count:] for half in self.halves], self.bits

    def absorb(self, arrived):
        self.stages.pop(0)
        count = self.halves[0].shape[0] // 2
        self.halves = [add_low(half[:count], a) for half, a in zip(self.halves, arrived)]
        self.bits = (1, 0)


def cut(value, bit, dim):
    half = value.shape[dim] // 2
    own = own_bit(bit)
    sent = lax.dynamic_slice_in_dim(value, (1 - own) * half, half, dim)
    return lax.dynamic_slice_in_dim(value, own * half, half, dim), sent


class Reduce:
    def __init__(self, parts, dims):
        self.first = [parts[0], parts[2]]
        self.kept = [parts[1], parts[3]]
        self.dims = dims
        self.stages = [(0, 1), (1, 0)] + high_bits()

    def operands(self):
        stage = self.stages[0]
        if self.first is not None:
            sent, self.first = self.first, None
        elif isinstance(stage, tuple):
            parts = [cut(v, b, self.dims[0]) for v, b in zip(self.pair, stage)]
            self.kept = [p[0] for p in parts]
            sent = [p[1] for p in parts]
        else:
            if self.pair is not None:
                kept, out = by_bit(stage, *self.pair)
                self.pair = None
            else:
                kept, out = cut(self.held, stage, self.dims[1])
            self.kept, sent, stage = [kept], [out], [stage]
        return sent, stage

    def absorb(self, arrived):
        sums = [add_low(k, a) for k, a in zip(self.kept, arrived)]
        if isinstance(self.stages.pop(0), tuple):
            self.pair = sums
        else:
            self.held = sums[0]


class Spread:
    def __init__(self, job):
        self.held = job.held
        self.dims = job.dims
        self.stages = high_bits()[::-1] + [(1, 0), (0, 1)]
        self.pair = None

    def operands(self):
        stage = self.stages[0]
        if isinstance(stage, tuple):
            return self.pair, stage
        return [self.held], [stage]

    def absorb(self, arrived):
        stage = self.stages.pop(0)
        if isinstance(stage, tuple):
            parts = [by_bit(b, v, a) for v, a, b in zip(self.pair, arrived, stage)]
            if self.stages:
                self.pair = [jnp.concatenate(p, axis=self.dims[0]) for p in parts]
            else:
                self.quarters = [q for p in parts for q in p]
        elif stage == 2:
            self.pair = list(by_bit(stage, self.held, arrived[0]))
        else:
            self.held = in_order(stage, self.held, arrived[0], self.dims[1])


class GatherHigh:
    def __init__(self, value):
        self.held = value[None]
        self.stages = high_bits()[::-1]

    def operands(self):
        return [self.held], [self.stages[0]]

    def absorb(self, arrived):
        self.stages.pop(0)
        self.held = jnp.concatenate([self.held, arrived[0]], axis=0)


class ScatterHigh:
    def __init__(self, held):
        self.held = held
        self.stages = high_bits()

    def operands(self):
        return [self.held[self.held.shape[0] // 2 :]], [self.stages[0]]

    def absorb(self, arrived):
        self.stages.pop(0)
        self.held = add_low(self.held[: self.held.shape[0] // 2], arrived[0])


class Exchange:
    def __init__(self, arrays, bits):
        self.arrays, self.bits = arrays, bits
        self.stages = [None]

    def operands(self):
        return self.arrays, self.bits

    def absorb(self, arrived):
        self.stages.pop()
        self.came = arrived


def four_rows(own, first, second, last, dim):
    rows = []
    for n, (low, high) in enumerate(((1, 0), (0, 1))):
        mine = in_order(low, own[n], first[n], dim)
        rows += by_bit(high, mine, in_order(low, second[n], last[n], dim))
    return rows


class SumVector:
    def __init__(self, value):
        self.value = value
        self.stages = high_bits() + [0, 1]

    def operands(self):
        return [self.value], [self.stages[0]]

    def absorb(self, arrived):
        self.stages.pop(0)
        self.value = self.value + arrived[0]


def rows_of(quarters, columns=slice(None)):
    return jnp.concatenate([q[:, columns] for q in quarters], axis=0).astype(f32)


class Solo:
    def __init__(self, value):
        self.value = value
        high = [(bit, None) for bit in high_bits()]
        self.stages = [(0, True), (1, True)] + high + [(1, False), (0, False)]

    def operands(self):
        bit, cuts = self.stages[0]
        if not cuts:
            return [self.value], [bit]
        self.value, sent = cut(self.value, bit, 0)
        return [sent], [bit]

    def absorb(self, arrived):
        bit, cuts = self.stages.pop(0)
        if cuts is not False:
            self.value = add_low(self.value, arrived[0])
        else:
            kind = bf16 if self.stages else f32
            self.value = in_order(bit, self.value.astype(kind), arrived[0].astype(kind), 0)


class Rounds:
    def __init__(self):
        self.flying = {}
        self.ready = {}
        self.fresh = []

    def begin(self, *jobs):
        for job in jobs:
            arrays, bits = self.ready.pop(job, None) or job.operands()
            self.flying[job] = [flip_ctx(v, b) for v, b in zip(arrays, bits)]

    def prepare(self, *jobs):
        for job in jobs:
            self.ready[job] = job.operands()
            self.fresh.append(job)

    def end(self, jobs, *values):
        ahead = [job for job in self.fresh if job in self.ready]
        self.fresh = []
        arrays = [a for job in jobs for a in self.flying[job]]
        sent = [a for job in ahead for a in self.ready[job][0]]
        rest = list(tie([*values, *arrays, *sent]))
        values, rest = rest[: len(values)], rest[len(values) :]
        for job in jobs:
            count = len(self.flying.pop(job))
            job.absorb(rest[:count])
            rest = rest[count:]
        for job in ahead:
            count = len(self.ready[job][0])
            self.ready[job] = (rest[:count], self.ready[job][1])
            rest = rest[count:]
        return values

    def run(self, job, left):
        while len(job.stages) > left:
            self.begin(job)
            self.end([job])


def key_tile(first_ref, second_ref, places, unit):
    lanes = pl.ds(pl.multiple_of((unit // 2) * LANES, LANES), LANES)
    parts = []
    for first, second in places:
        parts += [first_ref[first, :, lanes], second_ref[second, :, lanes]]
    return jnp.concatenate(parts, axis=0)


def heads_t(rows_t, group, unit):
    parts = [
        rows_t[(group * REP + r) * HD : (group * REP + r + 1) * HD, :] for r in range(REP)
    ]
    block = jnp.concatenate(parts, axis=1)
    zero = jnp.zeros_like(block)
    return jnp.concatenate([zero, block] if unit % 2 else [block, zero], axis=0)


def half_rows(tile_t, unit):
    return tile_t[(unit % 2) * HD : (unit % 2 + 1) * HD, :]


def seen_blocks(bits, which, ids, lengths, slots):
    me, shard = ids[0], ids[1]

    def look(j, own):
        return jnp.where(slots[which, shard, j] == me, j, own)

    own = lax.fori_loop(0, slots.shape[2], look, jnp.int32(0))
    end = jnp.int32(0)
    start = jnp.int32(0)
    for i in range(lengths.shape[2]):
        end = end + lengths[which, shard, i]
        start = jnp.where(end <= own, end, start)
    lowest = jnp.maximum(start, own - WINDOW // BLK)

    def places(index):
        relative = slots[which, shard, jnp.maximum(own - index, 0)] ^ me
        high = jnp.int32(0)
        for position, bit in enumerate(range(bits - 1, 1, -1)):
            high = high | (((relative >> bit) & 1) << position)
        one = (relative & 1) << (bits - 1)
        two = ((relative >> 1) & 1) << (bits - 2)
        swapped = ((relative & 1) << (bits - 2)) | (((relative >> 1) & 1) << (bits - 1))
        return high | one | two, high | swapped

    return own - lowest + 1, places


def pair_mask(far, count, index):
    key = lax.broadcasted_iota(jnp.int32, (BLK, GCOLS), 0)
    query = lax.broadcasted_iota(jnp.int32, (BLK, GCOLS), 1) & (BLK - 1)
    ahead = key - query
    masks = []
    for i in (index, index + 1):
        most = jnp.where(i < count, i * BLK, -2 * BLK)
        mask = ahead <= most
        if far:
            mask = mask & (ahead > i * BLK - WINDOW)
        masks.append(mask)
    return jnp.concatenate(masks, axis=0)


def lanes_at(start, size=LANES):
    return pl.ds(pl.multiple_of(start, LANES), size)


def spread_heads(source_ref, pad_ref, unit, group):
    parts = [
        source_ref[pl.ds(pl.multiple_of((group * REP + r) * HD, HD), HD), :] for r in range(REP)
    ]
    row = pl.multiple_of((unit % 2) * HD, HD)
    pad_ref[pl.ds(row, HD), lanes_at(unit * GCOLS, GCOLS)] = jnp.concatenate(parts, axis=1)


def forward_kernel(
    far, bits, which, ids, lengths, slots, first_ref, second_ref, query_ref, out_ref, lse_ref, pad_ref, half_ref
):
    count, places = seen_blocks(bits, which, ids, lengths, slots)
    pad_ref[...] = jnp.zeros_like(pad_ref)

    @pl.loop(0, KVH)
    def _(group):
        spread_heads(query_ref, pad_ref, group, group)
        columns = lanes_at(group * GCOLS, GCOLS)
        value_unit = KVH + group

        def step(pair, carried):
            high, total, acc = carried
            index = 2 * pair
            held = (places(index), places(index + 1))
            keys = key_tile(first_ref, second_ref, held, group)
            values = key_tile(first_ref, second_ref, held, value_unit)
            scores = dot(keys, pad_ref[:, columns], 1, 0) * SCALE
            scores = jnp.where(pair_mask(far, count, index), scores, NEG)
            new_high = jnp.maximum(high, jnp.max(scores, axis=0, keepdims=True))
            weights = jnp.exp(scores - new_high)
            fade = jnp.exp(high - new_high)
            total = total * fade + jnp.sum(weights, axis=0, keepdims=True)
            acc = acc * fade + dot(values.T, weights.astype(bf16), 1, 0)
            return (new_high, total, acc)

        start = (
            jnp.full((1, GCOLS), NEG, f32),
            jnp.zeros((1, GCOLS), f32),
            jnp.zeros((LANES, GCOLS), f32),
        )
        high, total, acc = lax.fori_loop(0, (count + 1) // 2, step, start)
        half_ref[...] = acc / total
        row = pl.multiple_of((value_unit % 2) * HD, HD)
        for r in range(REP):
            head_rows = pl.ds(pl.multiple_of((group * REP + r) * HD, HD), HD)
            out_ref[head_rows, :] = half_ref[pl.ds(row, HD), r * BLK : (r + 1) * BLK]
        lse_ref[:, columns] = high + jnp.log(total)


def backward_kernel(
    far,
    bits,
    which,
    ids,
    lengths,
    slots,
    first_ref,
    second_ref,
    query_ref,
    grad_ref,
    out_ref,
    lse_ref,
    dq_ref,
    dfirst_ref,
    dsecond_ref,
    pad_ref,
    right_ref,
    delta_ref,
    left_ref,
    acc_ref,
):
    count, places = seen_blocks(bits, which, ids, lengths, slots)
    queries = query_ref[...]
    grads = grad_ref[...]
    product = grads.astype(f32) * out_ref[...]
    for head in range(HEADS):
        delta_ref[:, head * BLK : (head + 1) * BLK] = jnp.sum(
            product[head * HD : (head + 1) * HD, :], axis=0, keepdims=True
        )
    for unit in range(2 * KVH):
        padded = heads_t(queries if unit < KVH else grads, unit % KVH, unit)
        rows = slice(unit * GCOLS, (unit + 1) * GCOLS)
        pad_ref[:, rows] = padded
        right_ref[rows, :] = padded.T
    dfirst_ref[...] = jnp.zeros_like(dfirst_ref)
    dsecond_ref[...] = jnp.zeros_like(dsecond_ref)
    acc_ref[...] = jnp.zeros_like(acc_ref)

    @pl.loop(0, (count + 1) // 2)
    def _(pair):
        index = 2 * pair
        held = (places(index), places(index + 1))
        mask = pair_mask(far, count, index)
        for group in range(KVH):
            value_unit = KVH + group
            columns = slice(group * GCOLS, (group + 1) * GCOLS)
            value_columns = slice(value_unit * GCOLS, (value_unit + 1) * GCOLS)
            keys = key_tile(first_ref, second_ref, held, group)
            values = key_tile(first_ref, second_ref, held, value_unit)
            scores = dot(keys, pad_ref[:, columns], 1, 0) * SCALE
            probs = jnp.where(mask, jnp.exp(scores - lse_ref[:, columns]), 0.0)
            grad_probs = dot(values, pad_ref[:, value_columns], 1, 0)
            grad_scores = (probs * (grad_probs - delta_ref[:, columns])).astype(bf16)
            left_ref[:, columns] = grad_scores
            left_ref[:, value_columns] = probs.astype(bf16)
            keys_t = half_rows(keys.T, group)
            acc_ref[:, columns] += dot(keys_t, grad_scores, 1, 0)
        for tile in range(KVH):
            rows = slice(2 * tile * GCOLS, 2 * (tile + 1) * GCOLS)
            lanes = slice(tile * LANES, (tile + 1) * LANES)
            block = dot(left_ref[:, rows], right_ref[rows, :], 1, 0)
            lane = lax.broadcasted_iota(jnp.int32, (1, LANES), 1) + tile * LANES
            block = (block * jnp.where(lane < KVH * HD, SCALE, 1.0)).astype(bf16)
            first, second = held[0]
            dfirst_ref[first, :, lanes] = block[:HALF]
            dsecond_ref[second, :, lanes] = block[HALF:BLK]

            @pl.when(index + 1 < count)
            def _():
                first, second = held[1]
                dfirst_ref[first, :, lanes] = block[BLK : BLK + HALF]
                dsecond_ref[second, :, lanes] = block[BLK + HALF :]

    for head in range(HEADS):
        columns = slice(head * BLK, (head + 1) * BLK)
        dq_ref[head * HD : (head + 1) * HD, :] = (acc_ref[:, columns] * SCALE).astype(bf16)


def in_hbm(values):
    return [pltpu.with_memory_space_constraint(v, pltpu.HBM) for v in values]


VMEM_SPEC = pl.BlockSpec(memory_space=pltpu.VMEM)
SMEM_SPEC = pl.BlockSpec(memory_space=pltpu.SMEM)


def attention_forward(which, tables, first, second, queries_t):
    steps = first.shape[0]
    return pl.pallas_call(
        functools.partial(
            forward_kernel, steps > WINDOW // BLK, steps.bit_length() - 1, which
        ),
        out_shape=(
            jax.ShapeDtypeStruct((HEADS * HD, BLK), f32),
            jax.ShapeDtypeStruct((1, HEADS * BLK), f32),
        ),
        in_specs=[SMEM_SPEC] * 3 + [VMEM_SPEC] * 3,
        out_specs=(VMEM_SPEC,) * 2,
        scratch_shapes=[pltpu.VMEM((LANES, HEADS * BLK), bf16), pltpu.VMEM((LANES, GCOLS), f32)],
        compiler_params=pltpu.CompilerParams(vmem_limit_bytes=4 << 20),
        cost_estimate=pl.CostEstimate(
            flops=4 * HEADS * HD * BLK * BLK * 8,
            bytes_accessed=first.size * 4,
            transcendentals=HEADS * BLK * BLK * 8,
        ),
        name="attention_forward",
    )(*tables, first, second, queries_t)


def attention_backward(which, tables, first, second, queries_t, grads_t, out_t, lse):
    steps = first.shape[0]
    return pl.pallas_call(
        functools.partial(
            backward_kernel, steps > WINDOW // BLK, steps.bit_length() - 1, which
        ),
        out_shape=(
            jax.ShapeDtypeStruct((HEADS * HD, BLK), bf16),
            jax.ShapeDtypeStruct(first.shape, bf16),
            jax.ShapeDtypeStruct(second.shape, bf16),
        ),
        in_specs=[SMEM_SPEC] * 3 + [VMEM_SPEC] * 6,
        out_specs=(VMEM_SPEC,) * 3,
        scratch_shapes=[
            pltpu.VMEM((LANES, 2 * KVH * GCOLS), bf16),
            pltpu.VMEM((2 * KVH * GCOLS, LANES), bf16),
            pltpu.VMEM((1, HEADS * BLK), f32),
            pltpu.VMEM((2 * BLK, 2 * KVH * GCOLS), bf16),
            pltpu.VMEM((HD, HEADS * BLK), f32),
        ],
        compiler_params=pltpu.CompilerParams(vmem_limit_bytes=8 << 20),
        cost_estimate=pl.CostEstimate(
            flops=10 * HEADS * HD * BLK * BLK,
            bytes_accessed=first.size,
            transcendentals=HEADS * BLK * BLK,
        ),
        name="attention_backward",
    )(*tables, first, second, queries_t, grads_t, out_t, lse)


def block_kernel(
    x_ref,
    cot_ref,
    att_ref,
    out_w_ref,
    gain_ref,
    gate_w_ref,
    up_w_ref,
    down_w_ref,
    hidden_ref,
    grads_ref,
    normed_ref,
    layer_ref,
    grad_mixed_ref,
    grad_low_ref,
    grad_att_ref,
    gain_grad_ref,
    mixed,
    normed,
    cot,
    grad_normed,
    layer,
):
    step = pl.program_id(0)

    @pl.when(step == 0)
    def _():
        cot[...] = cot_ref[...].T
        values = x_ref[...].astype(f32).T + dot(att_ref[...], out_w_ref[...], 0, 0)
        mixed[...] = values
        inverse = lax.rsqrt(jnp.mean(values * values, axis=-1, keepdims=True) + EPS)
        low = (values * inverse * gain_ref[...]).astype(bf16)
        normed[...] = low
        normed_ref[...] = low.T
        layer[...] = values
        grad_normed[...] = jnp.zeros_like(grad_normed)

    grad_hidden = dot(cot[...], down_w_ref[...], 1, 0)
    gate = dot(normed[...], gate_w_ref[...], 1, 0)
    up = dot(normed[...], up_w_ref[...], 1, 0)
    sigmoid = jax.nn.sigmoid(gate)
    silu = gate * sigmoid
    hidden = (silu * up).astype(bf16)
    grad_gate = (grad_hidden * up * sigmoid * (1.0 + gate * (1.0 - sigmoid))).astype(bf16)
    grad_up = (grad_hidden * silu).astype(bf16)
    hidden_ref[...] = hidden
    grads_ref[0] = grad_gate
    grads_ref[1] = grad_up
    layer[...] += dot(hidden, down_w_ref[...], 1, 1)
    grad_normed[...] += dot(grad_gate, gate_w_ref[...], 1, 1) + dot(
        grad_up, up_w_ref[...], 1, 1
    )

    @pl.when(step == pl.num_programs(0) - 1)
    def _():
        values = mixed[...]
        layer_ref[...] = layer[...].astype(bf16).T
        inverse = lax.rsqrt(jnp.mean(values * values, axis=-1, keepdims=True) + EPS)
        grads = grad_normed[...]
        gain_grad_ref[...] = jnp.sum(grads * values * inverse, axis=0, keepdims=True)
        scaled = grads * gain_ref[...]
        cubed = inverse * inverse * inverse
        back = inverse * scaled - values * cubed * jnp.mean(
            scaled * values, axis=-1, keepdims=True
        )
        grad_mixed = cot[...].astype(f32) + back
        low = grad_mixed.astype(bf16)
        grad_mixed_ref[...] = grad_mixed.T
        grad_low_ref[...] = low
        grad_att_ref[...] = dot(out_w_ref[...], low, 1, 1).astype(bf16)


def feed_forward(x_t, cot_t, attended_t, out_w, gain, gate_w, up_w, down_w_t):
    width, rows = x_t.shape
    inner = gate_w.shape[1]
    tile = 512

    def fixed(shape):
        return pl.BlockSpec(shape, lambda i: (0,) * len(shape))

    weight = pl.BlockSpec((width, tile), lambda i: (0, i))
    wide = (width, rows)
    return pl.pallas_call(
        block_kernel,
        grid=(inner // tile,),
        in_specs=[fixed(wide)] * 3
        + [fixed(out_w.shape), fixed((1, width)), weight, weight, weight],
        out_specs=(
            pl.BlockSpec((rows, tile), lambda i: (0, i)),
            pl.BlockSpec((2, rows, tile), lambda i: (0, 0, i)),
            fixed(wide),
            fixed(wide),
            fixed(wide),
            fixed((rows, width)),
            fixed(wide),
            fixed((1, width)),
        ),
        out_shape=(
            pltpu.HBM((rows, inner), bf16),
            pltpu.HBM((2, rows, inner), bf16),
            pltpu.HBM(wide, bf16),
            pltpu.HBM(wide, bf16),
            pltpu.HBM(wide, f32),
            pltpu.HBM((rows, width), bf16),
            pltpu.HBM(wide, bf16),
            pltpu.HBM((1, width), f32),
        ),
        scratch_shapes=[
            pltpu.VMEM((rows, width), f32),
            pltpu.VMEM((rows, width), bf16),
            pltpu.VMEM((rows, width), bf16),
            pltpu.VMEM((rows, width), f32),
            pltpu.VMEM((rows, width), f32),
        ],
        compiler_params=pltpu.CompilerParams(vmem_limit_bytes=26 << 20),
        cost_estimate=pl.CostEstimate(
            flops=12 * rows * width * inner,
            bytes_accessed=8 * width * inner,
            transcendentals=rows * inner,
        ),
        name="feed_forward",
    )(*in_hbm([x_t, cot_t, attended_t, out_w, gain, gate_w, up_w, down_w_t]))


def weight_grad_kernel(products, sides, ids, *refs):
    values = []
    for number, (by_shard, right_t) in enumerate(products):
        left, left_other, right, right_other = refs[4 * number : 4 * number + 4]
        rows = left_other.shape[0]
        start = pl.multiple_of(ids[1] * rows if by_shard else 0, 8)
        dim = 1 if right_t else 0
        values.append(
            dot(left[pl.ds(start, rows), :], right[...].reshape(right.shape[-2:]), 1, dim)
            + dot(left_other[...], right_other[...].reshape(right_other.shape[-2:]), 1, dim)
        )
    outs = refs[4 * len(products) :]
    for number, (product, first, rows, bit) in enumerate(sides):
        sent, kept = outs[2 * number : 2 * number + 2]
        half = rows // 2
        low = values[product][first : first + half].astype(bf16)
        high = values[product][first + half : first + rows].astype(bf16)
        own = (ids[0] >> bit) & 1

        @pl.when(own == 0)
        def _():
            kept[...] = low
            sent[...] = high

        @pl.when(own != 0)
        def _():
            kept[...] = high
            sent[...] = low


def weight_grad(name, ids, products, operands, right_specs, sides, tiles, columns):
    tile = columns // tiles
    specs = []
    for (left, left_other, _, _), rights in zip(operands, right_specs):
        specs += [
            pl.BlockSpec(left.shape, lambda i, ids: (0, 0)),
            pl.BlockSpec(left_other.shape, lambda i, ids: (0, 0)),
            *rights,
        ]
    shapes = [(side[2] // 2, columns) for side in sides for _ in range(2)]
    return pl.pallas_call(
        functools.partial(weight_grad_kernel, products, sides),
        grid_spec=pltpu.PrefetchScalarGridSpec(
            num_scalar_prefetch=1,
            grid=(tiles,),
            in_specs=specs,
            out_specs=[pl.BlockSpec((rows, tile), lambda i, ids: (0, i)) for rows, _ in shapes],
        ),
        out_shape=[pltpu.HBM(shape, bf16) for shape in shapes],
        compiler_params=pltpu.CompilerParams(vmem_limit_bytes=11 << 20),
        cost_estimate=pl.CostEstimate(
            flops=2 * sum(rows * width for rows, width in shapes) * 512,
            bytes_accessed=2 * sum(rows * width for rows, width in shapes),
            transcendentals=0,
        ),
        name=name,
    )(ids, *in_hbm([o for group in operands for o in group]))


def keyval_grad_kernel(left, own, other, out, total):
    step = pl.program_id(0)
    tokens = own.shape[1]
    value = dot(left[0, :, :tokens], own[0], 1, 0) + dot(left[0, :, tokens:], other[0], 1, 0)

    @pl.when(step == 0)
    def _():
        total[...] = value

    @pl.when(step != 0)
    def _():
        total[...] += value

    @pl.when(step == pl.num_programs(0) - 1)
    def _():
        out[...] = total[...].astype(bf16)


def keyval_grad(left, own, other):
    count, rows, _ = left.shape
    columns = own.shape[2]

    def block(value):
        return pl.BlockSpec((1,) + value.shape[1:], lambda i: (i, 0, 0))

    return pl.pallas_call(
        keyval_grad_kernel,
        grid=(count,),
        in_specs=[block(left), block(own), block(other)],
        out_specs=pl.BlockSpec((rows, columns), lambda i: (0, 0)),
        out_shape=jax.ShapeDtypeStruct((rows, columns), bf16),
        scratch_shapes=[pltpu.VMEM((rows, columns), f32)],
        compiler_params=pltpu.CompilerParams(vmem_limit_bytes=5 << 20),
        cost_estimate=pl.CostEstimate(
            flops=2 * left.size * columns,
            bytes_accessed=2 * (left.size + 2 * own.size),
            transcendentals=0,
        ),
        name="keyval_grad",
    )(left, own, other)


def per_device(
    inputs,
    gain_attn,
    w_query,
    w_keyval,
    w_out,
    gain_mlp,
    w_gate,
    w_up,
    w_down,
    cotangent,
    seq_blocks,
    block_slots,
):
    micro = inputs.shape[0]
    shard = lax.axis_index("fsdp")
    is_low = shard == 0
    ids = jnp.stack([lax.axis_index("ctx"), shard]).astype(jnp.int32)
    rounds = Rounds()

    def joined(part, other):
        return jnp.concatenate(
            [jnp.where(is_low, part, other), jnp.where(is_low, other, part)], axis=0
        )

    def whole(part):
        return lax.all_gather(part, "fsdp", axis=0, tiled=True)

    def theirs(value, dim):
        half = value.shape[dim] // 2
        return lax.dynamic_slice_in_dim(value, (1 - shard) * half, half, dim)

    def tokens_last(value):
        return jnp.concatenate([value[m, 0].T for m in range(micro)], axis=1)

    out_full = whole(w_out)
    gate_full = whole(w_gate)
    up_full = whole(w_up)
    down_full_t = whole(w_down).T

    attn_gain = joined(gain_attn, swap_fsdp(gain_attn)).astype(f32)[:, None]
    keyval_full = joined(w_keyval, swap_fsdp(w_keyval))
    x_t = tokens_last(inputs)
    in_t = x_t.astype(f32)
    inverse_attn = lax.rsqrt(jnp.mean(in_t * in_t, axis=0, keepdims=True) + EPS)
    normed_t = (in_t * inverse_attn * attn_gain).astype(bf16)
    keyvals = dot(normed_t, keyval_full, 0, 0).astype(bf16)
    gathers = [GatherBlocks(keyvals[m * BLK : (m + 1) * BLK]) for m in range(micro)]

    rounds.begin(*gathers)
    (w_query, gain_mlp, cotangent, normed_t) = rounds.end(
        gathers[:1], w_query, gain_mlp, cotangent, normed_t
    )
    while len(gathers[0].stages) > 2:
        rounds.end(gathers[1:])
        rounds.begin(*gathers)
        rounds.end(gathers[:1])

    half = normed_t.shape[0] // 2
    rounds.begin(gathers[0])
    query_other, gain_other = swap_fsdp(w_query), swap_fsdp(gain_mlp)
    normed_other = swap_fsdp(theirs(normed_t, 0))
    (query_other, gain_other, normed_other) = rounds.end(
        gathers[:1], query_other, gain_other, normed_other
    )
    rounds.begin(gathers[0])
    normed_mine = lax.dynamic_slice_in_dim(normed_t, shard * half, half, 0)
    column = GatherHigh(jnp.concatenate([normed_mine, normed_other], axis=1))
    rounds.begin(column)
    cot_t = tokens_last(cotangent)
    query_full = joined(w_query, query_other)
    mlp_gain = joined(gain_mlp, gain_other).astype(f32)[None]
    (cot_t, mlp_gain) = rounds.end(gathers, cot_t, mlp_gain)

    rounds.begin(gathers[1])
    cot_other = swap_fsdp(cot_t)
    queries_t = dot(query_full, normed_t, 0, 0).astype(bf16)
    (cot_other, queries_t) = rounds.end([gathers[1], column], cot_other, queries_t)
    queries = [queries_t[:, m * BLK : (m + 1) * BLK] for m in range(micro)]
    tables = (ids, seq_blocks, block_slots)

    rounds.begin(gathers[1], column)
    first = attention_forward(0, tables, *gathers[0].halves, queries[0])
    first = rounds.end(gathers[1:], *first)
    second = attention_forward(1, tables, *gathers[1].halves, queries[1])
    second = rounds.end([column], *second)
    rounds.run(column, 0)
    outs, lses = zip(first, second)
    attended_t = jnp.concatenate(outs, axis=1).astype(bf16)

    attended_other = swap_fsdp(theirs(attended_t, 0))
    (
        hidden,
        grad_inner,
        normed_mlp_t,
        layer_out_t,
        grad_mixed_t,
        grad_mixed_low,
        grad_attended_t,
        mlp_gain_grad,
    ) = feed_forward(
        x_t, cot_t, attended_t, out_full, mlp_gain, gate_full, up_full, down_full_t
    )
    hidden_other = swap_fsdp(theirs(hidden, 1))
    mlp_other = swap_fsdp(theirs(normed_mlp_t, 0))
    inner_other = swap_fsdp(grad_inner)

    part = hidden_other.shape[1]
    width = cot_t.shape[0]
    tokens, inner = hidden.shape
    near = pl.BlockSpec((tokens, part // 2), lambda i, ids: (0, ids[1] * 2 + i))
    far = pl.BlockSpec((tokens, part // 2), lambda i, ids: (0, i))
    down_job = Reduce(
        weight_grad(
            "down_grad",
            ids,
            ((False, False),),
            ((cot_t, cot_other, hidden, hidden_other),),
            ((near, far),),
            ((0, 0, half, 0), (0, half, half, 1)),
            2,
            part,
        ),
        (1, 0),
    )

    def attention_back(m):
        return attention_backward(
            m,
            tables,
            *gathers[m].halves,
            queries[m],
            grad_attended_t[:, m * BLK : (m + 1) * BLK],
            outs[m],
            lses[m],
        )

    rounds.prepare(down_job)
    (grad_inner, inner_other, grad_attended_t, grad_mixed_low, normed_mlp_t, mlp_other) = rounds.end(
        [], grad_inner, inner_other, grad_attended_t, grad_mixed_low, normed_mlp_t, mlp_other
    )

    rounds.begin(down_job)
    spec = pl.BlockSpec((1, tokens, inner // 5), lambda i, ids: (i // 5, 0, i % 5))
    inner_job = Reduce(
        weight_grad(
            "inner_grad",
            ids,
            ((True, False),),
            ((normed_mlp_t, mlp_other, grad_inner, inner_other),),
            ((spec, spec),),
            ((0, 0, half // 2, 0), (0, half // 2, half // 2, 1)),
            10,
            2 * inner,
        ),
        (1, 1),
    )
    rounds.prepare(inner_job)
    (grad_attended_t, grad_mixed_low) = rounds.end([], grad_attended_t, grad_mixed_low)

    rounds.begin(inner_job)
    (grad_attended_t, grad_mixed_low) = rounds.end([down_job], grad_attended_t, grad_mixed_low)

    back_first = attention_back(0)
    key_first = ScatterBlocks(*back_first[1:])
    rounds.prepare(down_job, key_first)
    (grad_attended_t, grad_mixed_low, *back_first) = rounds.end(
        [inner_job], grad_attended_t, grad_mixed_low, *back_first
    )
    key_first.halves = back_first[1:]

    rounds.begin(down_job, key_first)
    rounds.prepare(inner_job)
    back_second = attention_back(1)
    key_second = ScatterBlocks(*back_second[1:])
    rounds.prepare(key_second)
    mixed_other = swap_fsdp(grad_mixed_low)
    (mixed_other, *back_second) = rounds.end([down_job, key_first], mixed_other, *back_second)
    key_second.halves = back_second[1:]

    rounds.begin(inner_job, key_second, down_job)
    rounds.prepare(key_first)
    grad_queries_t = jnp.concatenate([back_first[0], back_second[0]], axis=1)
    queries_other = swap_fsdp(grad_queries_t)
    (queries_other, grad_queries_t) = rounds.end(
        [inner_job, down_job], queries_other, grad_queries_t
    )

    rounds.begin(down_job, inner_job, key_first)
    flat = pl.BlockSpec((width, tokens), lambda i, ids: (0, 0))
    flat_half = pl.BlockSpec((tokens, width), lambda i, ids: (0, 0))
    query_job = Reduce(
        weight_grad(
            "query_grad",
            ids,
            ((True, True), (True, False)),
            (
                (normed_t, normed_other, grad_queries_t, queries_other),
                (attended_t, attended_other, grad_mixed_low, mixed_other),
            ),
            ((flat, flat), (flat_half, flat_half)),
            ((0, 0, half, 0), (1, 0, half, 1)),
            1,
            width,
        ),
        (0, 1),
    )
    rounds.prepare(query_job)
    (grad_queries_t,) = rounds.end([key_second, down_job, inner_job], grad_queries_t)
    rounds.run(down_job, 0)
    rounds.run(inner_job, 1)
    down_spread = Spread(down_job)

    rounds.begin(query_job, down_spread, inner_job)
    rounds.prepare(key_second)
    rounds.end([key_first, down_spread, inner_job])
    rounds.run(down_spread, 3)
    inner_spread = Spread(inner_job)

    rounds.begin(key_second, down_spread, inner_spread)
    grad_normed_t = dot(query_full, grad_queries_t, 1, 0)
    (grad_normed_t,) = rounds.end(
        [key_second, query_job, down_spread, inner_spread], grad_normed_t
    )
    rounds.run(inner_spread, 3)

    parts = [part for job in (key_first, key_second) for part in job.halves]
    key_column = jnp.concatenate(parts, axis=1)
    rounds.begin(down_spread, query_job, inner_spread)
    key_other = swap_fsdp(key_column)
    last_job = Solo(keyval_grad(column.held, key_column, key_other))
    rounds.prepare(last_job)
    (key_column,) = rounds.end([down_spread, query_job, inner_spread], key_column)
    key_job = ScatterHigh(key_column)

    own = inner_spread.pair
    first = Exchange(own, (1, 0))
    second = Exchange(own, (0, 1))
    rounds.begin(last_job, query_job, key_job, first, down_spread, second)
    rounds.end([last_job, query_job, key_job])
    rounds.run(key_job, 1)
    rounds.begin(last_job, query_job, key_job)
    rounds.end([first, down_spread, last_job, key_job, query_job])
    rounds.run(query_job, 0)
    query_spread = Spread(query_job)

    third = Exchange(first.came, (0, 1))
    rounds.begin(third, last_job, query_spread)
    grad_keyvals = key_job.held[0]
    grad_normed_t = grad_normed_t + dot(keyval_full, grad_keyvals, 1, 1)
    attn_gain_grad = jnp.sum(grad_normed_t * in_t * inverse_attn, axis=1)
    gains = jnp.stack([attn_gain_grad, mlp_gain_grad[0]])
    gains_other = swap_fsdp(theirs(gains, 1))
    gains_mine = lax.dynamic_slice_in_dim(gains, shard * half, half, 1)
    (grad_normed_t, gains_mine, gains_other) = rounds.end(
        [last_job, query_spread, second], grad_normed_t, gains_mine, gains_other
    )
    rounds.run(query_spread, 3)
    rounds.run(last_job, 3)
    gain_job = SumVector((gains_mine + gains_other).reshape(-1))

    rounds.begin(last_job, query_spread, gain_job)
    down_sum = rows_of(down_spread.quarters)
    (down_sum,) = rounds.end([last_job, query_spread, gain_job, third], down_sum)
    rounds.run(gain_job, 3)

    rounds.begin(last_job, query_spread, gain_job)
    scaled = grad_normed_t * attn_gain
    cubed = inverse_attn * inverse_attn * inverse_attn
    input_grad_t = (
        grad_mixed_t
        + inverse_attn * scaled
        - in_t * cubed * jnp.mean(scaled * in_t, axis=0, keepdims=True)
    )
    tied = rounds.end(
        [last_job, query_spread, gain_job],
        input_grad_t,
        *own,
        *first.came,
        *second.came,
        *third.came,
    )
    input_grad_t = tied[0]
    quarters = four_rows(*[tied[i : i + 2] for i in (1, 3, 5, 7)], 1)

    rounds.begin(last_job, query_spread, gain_job)
    gate_sum = rows_of(quarters, slice(0, inner))
    up_sum = rows_of(quarters, slice(inner, None))
    (gate_sum, up_sum) = rounds.end([last_job, query_spread, gain_job], gate_sum, up_sum)
    rounds.begin(gain_job)
    rounds.end([gain_job])
    rounds.run(gain_job, 0)

    def by_token(value_t):
        parts = [value_t[:, m * BLK : (m + 1) * BLK].T[None] for m in range(micro)]
        return jnp.stack(parts)

    return (
        by_token(layer_out_t),
        by_token(input_grad_t),
        gain_job.value[:half],
        rows_of(query_spread.quarters[:2]),
        last_job.value,
        rows_of(query_spread.quarters[2:]),
        gain_job.value[half:],
        gate_sum,
        up_sum,
        down_sum.T,
    )


def solution(mesh):
    tokens = P(None, "fsdp", "ctx", None)
    vector = P("fsdp")
    matrix = P("fsdp", None)
    return jax.shard_map(
        per_device,
        mesh=mesh,
        in_specs=(
            tokens,
            vector,
            matrix,
            matrix,
            matrix,
            vector,
            matrix,
            matrix,
            matrix,
            tokens,
            P(),
            P(),
        ),
        out_specs=(
            tokens,
            tokens,
            vector,
            matrix,
            matrix,
            matrix,
            vector,
            matrix,
            matrix,
            matrix,
        ),
        check_vma=False,
    )
```

```python
import functools

import jax
import jax.numpy as jnp
from jax import lax
from jax.experimental import pallas as pl
from jax.experimental.pallas import tpu as pltpu
from jax.sharding import PartitionSpec as P

HEADS = 15
KVH = 5
HD = 64
REP = HEADS // KVH
WINDOW = 2048
BLK = 128
HALF = BLK // 2
KVW = 2 * KVH * HD
EPS = 1e-05
NEG = -1e30
SCALE = HD ** (-0.5)
LANES = 128
GCOLS = REP * BLK

bf16 = jnp.bfloat16
f32 = jnp.float32


def dot(left, right, left_dim, right_dim):
    return lax.dot_general(
        left, right, (((left_dim,), (right_dim,)), ((), ())), preferred_element_type=f32
    )


def flip_ctx(value, bit):
    size = lax.axis_size("ctx")
    mask = sum(1 << b for b in bit) if isinstance(bit, tuple) else 1 << bit
    return lax.ppermute(value, "ctx", [(i, i ^ mask) for i in range(size)])


def swap_fsdp(value):
    return lax.ppermute(value, "fsdp", [(0, 1), (1, 0)])


def tie(values):
    return lax.optimization_barrier(tuple(values))


def own_bit(bit):
    return (lax.axis_index("ctx") >> bit) & 1


def high_bits():
    return list(range(2, lax.axis_size("ctx").bit_length() - 1))


def add_low(kept, arrived):
    return (kept.astype(f32) + arrived.astype(f32)).astype(bf16)


def by_bit(bit, mine, arrived):
    low = own_bit(bit) == 0
    return jnp.where(low, mine, arrived), jnp.where(low, arrived, mine)


def in_order(bit, mine, arrived, dim):
    return jnp.concatenate(by_bit(bit, mine, arrived), axis=dim)


class GatherBlocks:
    def __init__(self, block):
        self.held = block[None]
        bits = high_bits()[::-1]
        self.stages = [tuple(bits[i : i + 2]) for i in range(0, len(bits), 2)] + [None, None]
        self.halves = None

    def operands(self):
        stage = self.stages[0]
        if stage is not None:
            hops = list(stage) + ([stage] if len(stage) == 2 else [])
            return [self.held] * len(hops), hops
        if self.halves is None:
            self.halves = [self.held[:, :HALF], self.held[:, HALF:]]
            self.bits = (1, 0)
        return self.halves, self.bits

    def absorb(self, arrived):
        if self.stages.pop(0) is not None:
            self.held = jnp.concatenate([self.held, *arrived], axis=0)
        else:
            self.halves = [
                jnp.concatenate([h, a], axis=0) for h, a in zip(self.halves, arrived)
            ]
            self.bits = (0, 1)


class ScatterBlocks:
    def __init__(self, first, second):
        self.halves = [first, second]
        self.bits = (0, 1)
        self.stages = [None, None]

    def operands(self):
        count = self.halves[0].shape[0] // 2
        return [half[count:] for half in self.halves], self.bits

    def absorb(self, arrived):
        self.stages.pop(0)
        count = self.halves[0].shape[0] // 2
        self.halves = [add_low(half[:count], a) for half, a in zip(self.halves, arrived)]
        self.bits = (1, 0)


def cut(value, bit, dim):
    half = value.shape[dim] // 2
    own = own_bit(bit)
    sent = lax.dynamic_slice_in_dim(value, (1 - own) * half, half, dim)
    return lax.dynamic_slice_in_dim(value, own * half, half, dim), sent


class Reduce:
    def __init__(self, parts, dims):
        self.first = [parts[0], parts[2]]
        self.kept = [parts[1], parts[3]]
        self.dims = dims
        self.stages = [(0, 1), (1, 0)] + high_bits()

    def operands(self):
        stage = self.stages[0]
        if self.first is not None:
            sent, self.first = self.first, None
        elif isinstance(stage, tuple):
            parts = [cut(v, b, self.dims[0]) for v, b in zip(self.pair, stage)]
            self.kept = [p[0] for p in parts]
            sent = [p[1] for p in parts]
        else:
            if self.pair is not None:
                kept, out = by_bit(stage, *self.pair)
                self.pair = None
            else:
                kept, out = cut(self.held, stage, self.dims[1])
            self.kept, sent, stage = [kept], [out], [stage]
        return sent, stage

    def absorb(self, arrived):
        sums = [add_low(k, a) for k, a in zip(self.kept, arrived)]
        if isinstance(self.stages.pop(0), tuple):
            self.pair = sums
        else:
            self.held = sums[0]


class Spread:
    def __init__(self, job):
        self.held = job.held
        self.dims = job.dims
        self.stages = high_bits()[::-1] + [(1, 0), (0, 1)]
        self.pair = None

    def operands(self):
        stage = self.stages[0]
        if isinstance(stage, tuple):
            return self.pair, stage
        return [self.held], [stage]

    def absorb(self, arrived):
        stage = self.stages.pop(0)
        if isinstance(stage, tuple):
            parts = [by_bit(b, v, a) for v, a, b in zip(self.pair, arrived, stage)]
            if self.stages:
                self.pair = [jnp.concatenate(p, axis=self.dims[0]) for p in parts]
            else:
                self.quarters = [q for p in parts for q in p]
        elif stage == 2:
            self.pair = list(by_bit(stage, self.held, arrived[0]))
        else:
            self.held = in_order(stage, self.held, arrived[0], self.dims[1])


class GatherHigh:
    def __init__(self, value):
        self.held = value[None]
        self.stages = high_bits()[::-1]

    def operands(self):
        return [self.held], [self.stages[0]]

    def absorb(self, arrived):
        self.stages.pop(0)
        self.held = jnp.concatenate([self.held, arrived[0]], axis=0)


class ScatterHigh:
    def __init__(self, held):
        self.held = held
        self.stages = high_bits()

    def operands(self):
        return [self.held[self.held.shape[0] // 2 :]], [self.stages[0]]

    def absorb(self, arrived):
        self.stages.pop(0)
        self.held = add_low(self.held[: self.held.shape[0] // 2], arrived[0])


class Exchange:
    def __init__(self, arrays, bits):
        self.arrays, self.bits = arrays, bits
        self.stages = [None]

    def operands(self):
        return self.arrays, self.bits

    def absorb(self, arrived):
        self.stages.pop()
        self.came = arrived


def four_rows(own, first, second, last, dim):
    rows = []
    for n, (low, high) in enumerate(((1, 0), (0, 1))):
        mine = in_order(low, own[n], first[n], dim)
        rows += by_bit(high, mine, in_order(low, second[n], last[n], dim))
    return rows


class SumVector:
    def __init__(self, value):
        self.value = value
        self.stages = high_bits() + [0, 1]

    def operands(self):
        return [self.value], [self.stages[0]]

    def absorb(self, arrived):
        self.stages.pop(0)
        self.value = self.value + arrived[0]


def rows_of(quarters, columns=slice(None)):
    return jnp.concatenate([q[:, columns] for q in quarters], axis=0).astype(f32)


class Solo:
    def __init__(self, value):
        self.value = value
        high = [(bit, None) for bit in high_bits()]
        self.stages = [(0, True), (1, True)] + high + [(1, False), (0, False)]

    def operands(self):
        bit, cuts = self.stages[0]
        if not cuts:
            return [self.value], [bit]
        self.value, sent = cut(self.value, bit, 0)
        return [sent], [bit]

    def absorb(self, arrived):
        bit, cuts = self.stages.pop(0)
        if cuts is not False:
            self.value = add_low(self.value, arrived[0])
        else:
            kind = bf16 if self.stages else f32
            self.value = in_order(bit, self.value.astype(kind), arrived[0].astype(kind), 0)


class Rounds:
    def __init__(self):
        self.flying = {}
        self.ready = {}
        self.fresh = []

    def begin(self, *jobs):
        for job in jobs:
            arrays, bits = self.ready.pop(job, None) or job.operands()
            self.flying[job] = [flip_ctx(v, b) for v, b in zip(arrays, bits)]

    def prepare(self, *jobs):
        for job in jobs:
            self.ready[job] = job.operands()
            self.fresh.append(job)

    def end(self, jobs, *values):
        ahead = [job for job in self.fresh if job in self.ready]
        self.fresh = []
        arrays = [a for job in jobs for a in self.flying[job]]
        sent = [a for job in ahead for a in self.ready[job][0]]
        rest = list(tie([*values, *arrays, *sent]))
        values, rest = rest[: len(values)], rest[len(values) :]
        for job in jobs:
            count = len(self.flying.pop(job))
            job.absorb(rest[:count])
            rest = rest[count:]
        for job in ahead:
            count = len(self.ready[job][0])
            self.ready[job] = (rest[:count], self.ready[job][1])
            rest = rest[count:]
        return values

    def run(self, job, left):
        while len(job.stages) > left:
            self.begin(job)
            self.end([job])


def key_tile(first_ref, second_ref, places, unit):
    lanes = pl.ds(pl.multiple_of((unit // 2) * LANES, LANES), LANES)
    parts = []
    for first, second in places:
        parts += [first_ref[first, :, lanes], second_ref[second, :, lanes]]
    return jnp.concatenate(parts, axis=0)


def heads_t(rows_t, group, unit):
    parts = [
        rows_t[(group * REP + r) * HD : (group * REP + r + 1) * HD, :] for r in range(REP)
    ]
    block = jnp.concatenate(parts, axis=1)
    zero = jnp.zeros_like(block)
    return jnp.concatenate([zero, block] if unit % 2 else [block, zero], axis=0)


def half_rows(tile_t, unit):
    return tile_t[(unit % 2) * HD : (unit % 2 + 1) * HD, :]


def seen_blocks(bits, which, ids, lengths, slots):
    me, shard = ids[0], ids[1]

    def look(j, own):
        return jnp.where(slots[which, shard, j] == me, j, own)

    own = lax.fori_loop(0, slots.shape[2], look, jnp.int32(0))
    end = jnp.int32(0)
    start = jnp.int32(0)
    for i in range(lengths.shape[2]):
        end = end + lengths[which, shard, i]
        start = jnp.where(end <= own, end, start)
    lowest = jnp.maximum(start, own - WINDOW // BLK)

    def places(index):
        relative = slots[which, shard, jnp.maximum(own - index, 0)] ^ me
        high = jnp.int32(0)
        for position, bit in enumerate(range(bits - 1, 1, -1)):
            high = high | (((relative >> bit) & 1) << position)
        one = (relative & 1) << (bits - 1)
        two = ((relative >> 1) & 1) << (bits - 2)
        swapped = ((relative & 1) << (bits - 2)) | (((relative >> 1) & 1) << (bits - 1))
        return high | one | two, high | swapped

    return own - lowest + 1, places


def pair_mask(far, count, index):
    key = lax.broadcasted_iota(jnp.int32, (BLK, GCOLS), 0)
    query = lax.broadcasted_iota(jnp.int32, (BLK, GCOLS), 1) & (BLK - 1)
    ahead = key - query
    masks = []
    for i in (index, index + 1):
        most = jnp.where(i < count, i * BLK, -2 * BLK)
        mask = ahead <= most
        if far:
            mask = mask & (ahead > i * BLK - WINDOW)
        masks.append(mask)
    return jnp.concatenate(masks, axis=0)


def lanes_at(start, size=LANES):
    return pl.ds(pl.multiple_of(start, LANES), size)


def spread_heads(source_ref, pad_ref, unit, group):
    parts = [
        source_ref[pl.ds(pl.multiple_of((group * REP + r) * HD, HD), HD), :] for r in range(REP)
    ]
    row = pl.multiple_of((unit % 2) * HD, HD)
    pad_ref[pl.ds(row, HD), lanes_at(unit * GCOLS, GCOLS)] = jnp.concatenate(parts, axis=1)


def forward_kernel(
    far, bits, which, ids, lengths, slots, first_ref, second_ref, query_ref, out_ref, lse_ref, pad_ref, half_ref
):
    count, places = seen_blocks(bits, which, ids, lengths, slots)
    pad_ref[...] = jnp.zeros_like(pad_ref)

    @pl.loop(0, KVH)
    def _(group):
        spread_heads(query_ref, pad_ref, group, group)
        columns = lanes_at(group * GCOLS, GCOLS)
        value_unit = KVH + group

        def step(pair, carried):
            high, total, acc = carried
            index = 2 * pair
            held = (places(index), places(index + 1))
            keys = key_tile(first_ref, second_ref, held, group)
            values = key_tile(first_ref, second_ref, held, value_unit)
            scores = dot(keys, pad_ref[:, columns], 1, 0) * SCALE
            scores = jnp.where(pair_mask(far, count, index), scores, NEG)
            new_high = jnp.maximum(high, jnp.max(scores, axis=0, keepdims=True))
            weights = jnp.exp(scores - new_high)
            fade = jnp.exp(high - new_high)
            total = total * fade + jnp.sum(weights, axis=0, keepdims=True)
            acc = acc * fade + dot(values.T, weights.astype(bf16), 1, 0)
            return (new_high, total, acc)

        start = (
            jnp.full((1, GCOLS), NEG, f32),
            jnp.zeros((1, GCOLS), f32),
            jnp.zeros((LANES, GCOLS), f32),
        )
        high, total, acc = lax.fori_loop(0, (count + 1) // 2, step, start)
        half_ref[...] = acc / total
        row = pl.multiple_of((value_unit % 2) * HD, HD)
        for r in range(REP):
            head_rows = pl.ds(pl.multiple_of((group * REP + r) * HD, HD), HD)
            out_ref[head_rows, :] = half_ref[pl.ds(row, HD), r * BLK : (r + 1) * BLK]
        lse_ref[:, columns] = high + jnp.log(total)


def backward_kernel(
    far,
    bits,
    which,
    ids,
    lengths,
    slots,
    first_ref,
    second_ref,
    query_ref,
    grad_ref,
    out_ref,
    lse_ref,
    dq_ref,
    dfirst_ref,
    dsecond_ref,
    pad_ref,
    right_ref,
    delta_ref,
    left_ref,
    acc_ref,
):
    count, places = seen_blocks(bits, which, ids, lengths, slots)
    queries = query_ref[...]
    grads = grad_ref[...]
    product = grads.astype(f32) * out_ref[...]
    for head in range(HEADS):
        delta_ref[:, head * BLK : (head + 1) * BLK] = jnp.sum(
            product[head * HD : (head + 1) * HD, :], axis=0, keepdims=True
        )
    for unit in range(2 * KVH):
        padded = heads_t(queries if unit < KVH else grads, unit % KVH, unit)
        rows = slice(unit * GCOLS, (unit + 1) * GCOLS)
        pad_ref[:, rows] = padded
        right_ref[rows, :] = padded.T
    dfirst_ref[...] = jnp.zeros_like(dfirst_ref)
    dsecond_ref[...] = jnp.zeros_like(dsecond_ref)
    acc_ref[...] = jnp.zeros_like(acc_ref)

    @pl.loop(0, (count + 1) // 2)
    def _(pair):
        index = 2 * pair
        held = (places(index), places(index + 1))
        mask = pair_mask(far, count, index)
        for group in range(KVH):
            value_unit = KVH + group
            columns = slice(group * GCOLS, (group + 1) * GCOLS)
            value_columns = slice(value_unit * GCOLS, (value_unit + 1) * GCOLS)
            keys = key_tile(first_ref, second_ref, held, group)
            values = key_tile(first_ref, second_ref, held, value_unit)
            scores = dot(keys, pad_ref[:, columns], 1, 0) * SCALE
            probs = jnp.where(mask, jnp.exp(scores - lse_ref[:, columns]), 0.0)
            grad_probs = dot(values, pad_ref[:, value_columns], 1, 0)
            grad_scores = (probs * (grad_probs - delta_ref[:, columns])).astype(bf16)
            left_ref[:, columns] = grad_scores
            left_ref[:, value_columns] = probs.astype(bf16)
            keys_t = half_rows(keys.T, group)
            acc_ref[:, columns] += dot(keys_t, grad_scores, 1, 0)
        for tile in range(KVH):
            rows = slice(2 * tile * GCOLS, 2 * (tile + 1) * GCOLS)
            lanes = slice(tile * LANES, (tile + 1) * LANES)
            block = dot(left_ref[:, rows], right_ref[rows, :], 1, 0)
            lane = lax.broadcasted_iota(jnp.int32, (1, LANES), 1) + tile * LANES
            block = (block * jnp.where(lane < KVH * HD, SCALE, 1.0)).astype(bf16)
            first, second = held[0]
            dfirst_ref[first, :, lanes] = block[:HALF]
            dsecond_ref[second, :, lanes] = block[HALF:BLK]

            @pl.when(index + 1 < count)
            def _():
                first, second = held[1]
                dfirst_ref[first, :, lanes] = block[BLK : BLK + HALF]
                dsecond_ref[second, :, lanes] = block[BLK + HALF :]

    for head in range(HEADS):
        columns = slice(head * BLK, (head + 1) * BLK)
        dq_ref[head * HD : (head + 1) * HD, :] = (acc_ref[:, columns] * SCALE).astype(bf16)


def in_hbm(values):
    return [pltpu.with_memory_space_constraint(v, pltpu.HBM) for v in values]


VMEM_SPEC = pl.BlockSpec(memory_space=pltpu.VMEM)
SMEM_SPEC = pl.BlockSpec(memory_space=pltpu.SMEM)


def attention_forward(which, tables, first, second, queries_t):
    steps = first.shape[0]
    return pl.pallas_call(
        functools.partial(
            forward_kernel, steps > WINDOW // BLK, steps.bit_length() - 1, which
        ),
        out_shape=(
            jax.ShapeDtypeStruct((HEADS * HD, BLK), f32),
            jax.ShapeDtypeStruct((1, HEADS * BLK), f32),
        ),
        in_specs=[SMEM_SPEC] * 3 + [VMEM_SPEC] * 3,
        out_specs=(VMEM_SPEC,) * 2,
        scratch_shapes=[pltpu.VMEM((LANES, HEADS * BLK), bf16), pltpu.VMEM((LANES, GCOLS), f32)],
        compiler_params=pltpu.CompilerParams(vmem_limit_bytes=4 << 20),
        cost_estimate=pl.CostEstimate(
            flops=256 * HEADS * HD * BLK * BLK,
            bytes_accessed=first.size * 4,
            transcendentals=HEADS * BLK * BLK * 8,
        ),
        name="attention_forward",
    )(*tables, first, second, queries_t)


def attention_backward(which, tables, first, second, queries_t, grads_t, out_t, lse):
    steps = first.shape[0]
    return pl.pallas_call(
        functools.partial(
            backward_kernel, steps > WINDOW // BLK, steps.bit_length() - 1, which
        ),
        out_shape=(
            jax.ShapeDtypeStruct((HEADS * HD, BLK), bf16),
            jax.ShapeDtypeStruct(first.shape, bf16),
            jax.ShapeDtypeStruct(second.shape, bf16),
        ),
        in_specs=[SMEM_SPEC] * 3 + [VMEM_SPEC] * 6,
        out_specs=(VMEM_SPEC,) * 3,
        scratch_shapes=[
            pltpu.VMEM((LANES, 2 * KVH * GCOLS), bf16),
            pltpu.VMEM((2 * KVH * GCOLS, LANES), bf16),
            pltpu.VMEM((1, HEADS * BLK), f32),
            pltpu.VMEM((2 * BLK, 2 * KVH * GCOLS), bf16),
            pltpu.VMEM((HD, HEADS * BLK), f32),
        ],
        compiler_params=pltpu.CompilerParams(vmem_limit_bytes=8 << 20),
        cost_estimate=pl.CostEstimate(
            flops=640 * HEADS * HD * BLK * BLK,
            bytes_accessed=first.size,
            transcendentals=HEADS * BLK * BLK,
        ),
        name="attention_backward",
    )(*tables, first, second, queries_t, grads_t, out_t, lse)


def block_kernel(
    x_ref,
    cot_ref,
    att_ref,
    out_w_ref,
    gain_ref,
    gate_w_ref,
    up_w_ref,
    down_w_ref,
    hidden_ref,
    grads_ref,
    normed_ref,
    layer_ref,
    grad_mixed_ref,
    grad_low_ref,
    grad_att_ref,
    gain_grad_ref,
    mixed,
    normed,
    cot,
    grad_normed,
    layer,
):
    step = pl.program_id(0)

    @pl.when(step == 0)
    def _():
        cot[...] = cot_ref[...].T
        values = x_ref[...].astype(f32).T + dot(att_ref[...], out_w_ref[...], 0, 0)
        mixed[...] = values
        inverse = lax.rsqrt(jnp.mean(values * values, axis=-1, keepdims=True) + EPS)
        low = (values * inverse * gain_ref[...]).astype(bf16)
        normed[...] = low
        normed_ref[...] = low.T
        layer[...] = values
        grad_normed[...] = jnp.zeros_like(grad_normed)

    grad_hidden = dot(cot[...], down_w_ref[...], 1, 0)
    gate = dot(normed[...], gate_w_ref[...], 1, 0)
    up = dot(normed[...], up_w_ref[...], 1, 0)
    sigmoid = jax.nn.sigmoid(gate)
    silu = gate * sigmoid
    hidden = (silu * up).astype(bf16)
    grad_gate = (grad_hidden * up * sigmoid * (1.0 + gate * (1.0 - sigmoid))).astype(bf16)
    grad_up = (grad_hidden * silu).astype(bf16)
    hidden_ref[...] = hidden
    grads_ref[0] = grad_gate
    grads_ref[1] = grad_up
    layer[...] += dot(hidden, down_w_ref[...], 1, 1)
    grad_normed[...] += dot(grad_gate, gate_w_ref[...], 1, 1) + dot(
        grad_up, up_w_ref[...], 1, 1
    )

    @pl.when(step == pl.num_programs(0) - 1)
    def _():
        values = mixed[...]
        layer_ref[...] = layer[...].astype(bf16).T
        inverse = lax.rsqrt(jnp.mean(values * values, axis=-1, keepdims=True) + EPS)
        grads = grad_normed[...]
        gain_grad_ref[...] = jnp.sum(grads * values * inverse, axis=0, keepdims=True)
        scaled = grads * gain_ref[...]
        cubed = inverse * inverse * inverse
        back = inverse * scaled - values * cubed * jnp.mean(
            scaled * values, axis=-1, keepdims=True
        )
        grad_mixed = cot[...].astype(f32) + back
        low = grad_mixed.astype(bf16)
        grad_mixed_ref[...] = grad_mixed.T
        grad_low_ref[...] = low
        grad_att_ref[...] = dot(out_w_ref[...], low, 1, 1).astype(bf16)


def feed_forward(x_t, cot_t, attended_t, out_w, gain, gate_w, up_w, down_w_t):
    width, rows = x_t.shape
    inner = gate_w.shape[1]
    tile = 512

    def fixed(shape):
        return pl.BlockSpec(shape, lambda i: (0,) * len(shape))

    weight = pl.BlockSpec((width, tile), lambda i: (0, i))
    wide = (width, rows)
    return pl.pallas_call(
        block_kernel,
        grid=(inner // tile,),
        in_specs=[fixed(wide)] * 3
        + [fixed(out_w.shape), fixed((1, width)), weight, weight, weight],
        out_specs=(
            pl.BlockSpec((rows, tile), lambda i: (0, i)),
            pl.BlockSpec((2, rows, tile), lambda i: (0, 0, i)),
            fixed(wide),
            fixed(wide),
            fixed(wide),
            fixed((rows, width)),
            fixed(wide),
            fixed((1, width)),
        ),
        out_shape=(
            pltpu.HBM((rows, inner), bf16),
            pltpu.HBM((2, rows, inner), bf16),
            pltpu.HBM(wide, bf16),
            pltpu.HBM(wide, bf16),
            pltpu.HBM(wide, f32),
            pltpu.HBM((rows, width), bf16),
            pltpu.HBM(wide, bf16),
            pltpu.HBM((1, width), f32),
        ),
        scratch_shapes=[
            pltpu.VMEM((rows, width), f32),
            pltpu.VMEM((rows, width), bf16),
            pltpu.VMEM((rows, width), bf16),
            pltpu.VMEM((rows, width), f32),
            pltpu.VMEM((rows, width), f32),
        ],
        compiler_params=pltpu.CompilerParams(vmem_limit_bytes=26 << 20),
        cost_estimate=pl.CostEstimate(
            flops=12 * rows * width * inner,
            bytes_accessed=8 * width * inner,
            transcendentals=rows * inner,
        ),
        name="feed_forward",
    )(*in_hbm([x_t, cot_t, attended_t, out_w, gain, gate_w, up_w, down_w_t]))


def weight_grad_kernel(products, sides, ids, *refs):
    values = []
    for number, (by_shard, right_t) in enumerate(products):
        left, left_other, right, right_other = refs[4 * number : 4 * number + 4]
        rows = left_other.shape[0]
        start = pl.multiple_of(ids[1] * rows if by_shard else 0, 8)
        dim = 1 if right_t else 0
        values.append(
            dot(left[pl.ds(start, rows), :], right[...].reshape(right.shape[-2:]), 1, dim)
            + dot(left_other[...], right_other[...].reshape(right_other.shape[-2:]), 1, dim)
        )
    outs = refs[4 * len(products) :]
    for number, (product, first, rows, bit) in enumerate(sides):
        sent, kept = outs[2 * number : 2 * number + 2]
        half = rows // 2
        low = values[product][first : first + half].astype(bf16)
        high = values[product][first + half : first + rows].astype(bf16)
        own = (ids[0] >> bit) & 1

        @pl.when(own == 0)
        def _():
            kept[...] = low
            sent[...] = high

        @pl.when(own != 0)
        def _():
            kept[...] = high
            sent[...] = low


def weight_grad(name, ids, products, operands, right_specs, sides, tiles, columns):
    tile = columns // tiles
    specs = []
    for (left, left_other, _, _), rights in zip(operands, right_specs):
        specs += [
            pl.BlockSpec(left.shape, lambda i, ids: (0, 0)),
            pl.BlockSpec(left_other.shape, lambda i, ids: (0, 0)),
            *rights,
        ]
    shapes = [(side[2] // 2, columns) for side in sides for _ in range(2)]
    return pl.pallas_call(
        functools.partial(weight_grad_kernel, products, sides),
        grid_spec=pltpu.PrefetchScalarGridSpec(
            num_scalar_prefetch=1,
            grid=(tiles,),
            in_specs=specs,
            out_specs=[pl.BlockSpec((rows, tile), lambda i, ids: (0, i)) for rows, _ in shapes],
        ),
        out_shape=[pltpu.HBM(shape, bf16) for shape in shapes],
        compiler_params=pltpu.CompilerParams(vmem_limit_bytes=11 << 20),
        cost_estimate=pl.CostEstimate(
            flops=16 * sum(rows * width for rows, width in shapes) * 512,
            bytes_accessed=2 * sum(rows * width for rows, width in shapes),
            transcendentals=0,
        ),
        name=name,
    )(ids, *in_hbm([o for group in operands for o in group]))


def keyval_grad_kernel(left, own, other, out, total):
    step = pl.program_id(0)
    tokens = own.shape[1]
    value = dot(left[0, :, :tokens], own[0], 1, 0) + dot(left[0, :, tokens:], other[0], 1, 0)

    @pl.when(step == 0)
    def _():
        total[...] = value

    @pl.when(step != 0)
    def _():
        total[...] += value

    @pl.when(step == pl.num_programs(0) - 1)
    def _():
        out[...] = total[...].astype(bf16)


def keyval_grad(left, own, other):
    count, rows, _ = left.shape
    columns = own.shape[2]

    def block(value):
        return pl.BlockSpec((1,) + value.shape[1:], lambda i: (i, 0, 0))

    return pl.pallas_call(
        keyval_grad_kernel,
        grid=(count,),
        in_specs=[block(left), block(own), block(other)],
        out_specs=pl.BlockSpec((rows, columns), lambda i: (0, 0)),
        out_shape=jax.ShapeDtypeStruct((rows, columns), bf16),
        scratch_shapes=[pltpu.VMEM((rows, columns), f32)],
        compiler_params=pltpu.CompilerParams(vmem_limit_bytes=5 << 20),
        cost_estimate=pl.CostEstimate(
            flops=2 * left.size * columns,
            bytes_accessed=2 * (left.size + 2 * own.size),
            transcendentals=0,
        ),
        name="keyval_grad",
    )(left, own, other)


def per_device(
    inputs,
    gain_attn,
    w_query,
    w_keyval,
    w_out,
    gain_mlp,
    w_gate,
    w_up,
    w_down,
    cotangent,
    seq_blocks,
    block_slots,
):
    micro = inputs.shape[0]
    shard = lax.axis_index("fsdp")
    is_low = shard == 0
    ids = jnp.stack([lax.axis_index("ctx"), shard]).astype(jnp.int32)
    rounds = Rounds()

    def joined(part, other):
        return jnp.concatenate(
            [jnp.where(is_low, part, other), jnp.where(is_low, other, part)], axis=0
        )

    def whole(part):
        return lax.all_gather(part, "fsdp", axis=0, tiled=True)

    def theirs(value, dim):
        half = value.shape[dim] // 2
        return lax.dynamic_slice_in_dim(value, (1 - shard) * half, half, dim)

    def tokens_last(value):
        return jnp.concatenate([value[m, 0].T for m in range(micro)], axis=1)

    out_full = whole(w_out)
    gate_full = whole(w_gate)
    up_full = whole(w_up)
    down_full_t = whole(w_down).T

    attn_gain = joined(gain_attn, swap_fsdp(gain_attn)).astype(f32)[:, None]
    keyval_full = joined(w_keyval, swap_fsdp(w_keyval))
    x_t = tokens_last(inputs)
    in_t = x_t.astype(f32)
    inverse_attn = lax.rsqrt(jnp.mean(in_t * in_t, axis=0, keepdims=True) + EPS)
    normed_t = (in_t * inverse_attn * attn_gain).astype(bf16)
    keyvals = dot(normed_t, keyval_full, 0, 0).astype(bf16)
    gathers = [GatherBlocks(keyvals[m * BLK : (m + 1) * BLK]) for m in range(micro)]

    rounds.begin(*gathers)
    (w_query, gain_mlp, cotangent, normed_t) = rounds.end(
        gathers[:1], w_query, gain_mlp, cotangent, normed_t
    )
    while len(gathers[0].stages) > 2:
        rounds.end(gathers[1:])
        rounds.begin(*gathers)
        rounds.end(gathers[:1])

    half = normed_t.shape[0] // 2
    rounds.begin(gathers[0])
    query_other, gain_other = swap_fsdp(w_query), swap_fsdp(gain_mlp)
    normed_other = swap_fsdp(theirs(normed_t, 0))
    (query_other, gain_other, normed_other) = rounds.end(
        gathers[:1], query_other, gain_other, normed_other
    )
    rounds.begin(gathers[0])
    normed_mine = lax.dynamic_slice_in_dim(normed_t, shard * half, half, 0)
    column = GatherHigh(jnp.concatenate([normed_mine, normed_other], axis=1))
    rounds.begin(column)
    cot_t = tokens_last(cotangent)
    query_full = joined(w_query, query_other)
    mlp_gain = joined(gain_mlp, gain_other).astype(f32)[None]
    (cot_t, mlp_gain) = rounds.end(gathers, cot_t, mlp_gain)

    rounds.begin(gathers[1])
    cot_other = swap_fsdp(cot_t)
    queries_t = dot(query_full, normed_t, 0, 0).astype(bf16)
    (cot_other, queries_t) = rounds.end([gathers[1], column], cot_other, queries_t)
    queries = [queries_t[:, m * BLK : (m + 1) * BLK] for m in range(micro)]
    tables = (ids, seq_blocks, block_slots)

    rounds.begin(gathers[1], column)
    first = attention_forward(0, tables, *gathers[0].halves, queries[0])
    first = rounds.end(gathers[1:], *first)
    second = attention_forward(1, tables, *gathers[1].halves, queries[1])
    second = rounds.end([column], *second)
    rounds.run(column, 0)
    outs, lses = zip(first, second)
    attended_t = jnp.concatenate(outs, axis=1).astype(bf16)

    attended_other = swap_fsdp(theirs(attended_t, 0))
    (
        hidden,
        grad_inner,
        normed_mlp_t,
        layer_out_t,
        grad_mixed_t,
        grad_mixed_low,
        grad_attended_t,
        mlp_gain_grad,
    ) = feed_forward(
        x_t, cot_t, attended_t, out_full, mlp_gain, gate_full, up_full, down_full_t
    )
    hidden_other = swap_fsdp(theirs(hidden, 1))
    mlp_other = swap_fsdp(theirs(normed_mlp_t, 0))
    inner_other = swap_fsdp(grad_inner)

    part = hidden_other.shape[1]
    width = cot_t.shape[0]
    tokens, inner = hidden.shape
    near = pl.BlockSpec((tokens, part // 2), lambda i, ids: (0, ids[1] * 2 + i))
    far = pl.BlockSpec((tokens, part // 2), lambda i, ids: (0, i))
    down_job = Reduce(
        weight_grad(
            "down_grad",
            ids,
            ((False, False),),
            ((cot_t, cot_other, hidden, hidden_other),),
            ((near, far),),
            ((0, 0, half, 0), (0, half, half, 1)),
            2,
            part,
        ),
        (1, 0),
    )

    def attention_back(m):
        return attention_backward(
            m,
            tables,
            *gathers[m].halves,
            queries[m],
            grad_attended_t[:, m * BLK : (m + 1) * BLK],
            outs[m],
            lses[m],
        )

    rounds.prepare(down_job)
    (grad_inner, inner_other, grad_attended_t, grad_mixed_low, normed_mlp_t, mlp_other) = rounds.end(
        [], grad_inner, inner_other, grad_attended_t, grad_mixed_low, normed_mlp_t, mlp_other
    )

    rounds.begin(down_job)
    spec = pl.BlockSpec((1, tokens, inner // 5), lambda i, ids: (i // 5, 0, i % 5))
    inner_job = Reduce(
        weight_grad(
            "inner_grad",
            ids,
            ((True, False),),
            ((normed_mlp_t, mlp_other, grad_inner, inner_other),),
            ((spec, spec),),
            ((0, 0, half // 2, 0), (0, half // 2, half // 2, 1)),
            10,
            2 * inner,
        ),
        (1, 1),
    )
    rounds.prepare(inner_job)
    (grad_attended_t, grad_mixed_low) = rounds.end([], grad_attended_t, grad_mixed_low)

    rounds.begin(inner_job)
    (grad_attended_t, grad_mixed_low) = rounds.end([down_job], grad_attended_t, grad_mixed_low)

    back_first = attention_back(0)
    key_first = ScatterBlocks(*back_first[1:])
    rounds.prepare(down_job, key_first)
    (grad_attended_t, grad_mixed_low, *back_first) = rounds.end(
        [inner_job], grad_attended_t, grad_mixed_low, *back_first
    )
    key_first.halves = back_first[1:]

    rounds.begin(down_job, key_first)
    rounds.prepare(inner_job)
    back_second = attention_back(1)
    key_second = ScatterBlocks(*back_second[1:])
    rounds.prepare(key_second)
    mixed_other = swap_fsdp(grad_mixed_low)
    (mixed_other, *back_second) = rounds.end([down_job, key_first], mixed_other, *back_second)
    key_second.halves = back_second[1:]

    rounds.begin(inner_job, key_second, down_job)
    rounds.prepare(key_first)
    grad_queries_t = jnp.concatenate([back_first[0], back_second[0]], axis=1)
    queries_other = swap_fsdp(grad_queries_t)
    (queries_other, grad_queries_t) = rounds.end(
        [inner_job, down_job], queries_other, grad_queries_t
    )

    rounds.begin(down_job, inner_job, key_first)
    flat = pl.BlockSpec((width, tokens), lambda i, ids: (0, 0))
    flat_half = pl.BlockSpec((tokens, width), lambda i, ids: (0, 0))
    query_job = Reduce(
        weight_grad(
            "query_grad",
            ids,
            ((True, True), (True, False)),
            (
                (normed_t, normed_other, grad_queries_t, queries_other),
                (attended_t, attended_other, grad_mixed_low, mixed_other),
            ),
            ((flat, flat), (flat_half, flat_half)),
            ((0, 0, half, 0), (1, 0, half, 1)),
            1,
            width,
        ),
        (0, 1),
    )
    rounds.prepare(query_job)
    (grad_queries_t,) = rounds.end([key_second, down_job, inner_job], grad_queries_t)
    rounds.run(down_job, 0)
    rounds.run(inner_job, 1)
    down_spread = Spread(down_job)

    rounds.begin(query_job, down_spread, inner_job)
    rounds.prepare(key_second)
    rounds.end([key_first, down_spread, inner_job])
    rounds.run(down_spread, 3)
    inner_spread = Spread(inner_job)

    rounds.begin(key_second, down_spread, inner_spread)
    grad_normed_t = dot(query_full, grad_queries_t, 1, 0)
    (grad_normed_t,) = rounds.end(
        [key_second, query_job, down_spread, inner_spread], grad_normed_t
    )
    rounds.run(inner_spread, 3)

    parts = [part for job in (key_first, key_second) for part in job.halves]
    key_column = jnp.concatenate(parts, axis=1)
    rounds.begin(down_spread, query_job, inner_spread)
    key_other = swap_fsdp(key_column)
    last_job = Solo(keyval_grad(column.held, key_column, key_other))
    rounds.prepare(last_job)
    (key_column,) = rounds.end([down_spread, query_job, inner_spread], key_column)
    key_job = ScatterHigh(key_column)

    own = inner_spread.pair
    first = Exchange(own, (1, 0))
    second = Exchange(own, (0, 1))
    rounds.begin(last_job, query_job, key_job, first, down_spread, second)
    rounds.end([last_job, query_job, key_job])
    rounds.run(key_job, 1)
    rounds.begin(last_job, query_job, key_job)
    rounds.end([first, down_spread, last_job, key_job, query_job])
    rounds.run(query_job, 0)
    query_spread = Spread(query_job)

    third = Exchange(first.came, (0, 1))
    rounds.begin(third, last_job, query_spread)
    grad_keyvals = key_job.held[0]
    grad_normed_t = grad_normed_t + dot(keyval_full, grad_keyvals, 1, 1)
    attn_gain_grad = jnp.sum(grad_normed_t * in_t * inverse_attn, axis=1)
    gains = jnp.stack([attn_gain_grad, mlp_gain_grad[0]])
    gains_other = swap_fsdp(theirs(gains, 1))
    gains_mine = lax.dynamic_slice_in_dim(gains, shard * half, half, 1)
    (grad_normed_t, gains_mine, gains_other) = rounds.end(
        [last_job, query_spread, second], grad_normed_t, gains_mine, gains_other
    )
    rounds.run(query_spread, 3)
    rounds.run(last_job, 3)
    gain_job = SumVector((gains_mine + gains_other).reshape(-1))

    rounds.begin(last_job, query_spread, gain_job)
    down_sum = rows_of(down_spread.quarters)
    (down_sum,) = rounds.end([last_job, query_spread, gain_job, third], down_sum)
    rounds.run(gain_job, 3)

    rounds.begin(last_job, query_spread, gain_job)
    scaled = grad_normed_t * attn_gain
    cubed = inverse_attn * inverse_attn * inverse_attn
    input_grad_t = (
        grad_mixed_t
        + inverse_attn * scaled
        - in_t * cubed * jnp.mean(scaled * in_t, axis=0, keepdims=True)
    )
    tied = rounds.end(
        [last_job, query_spread, gain_job],
        input_grad_t,
        *own,
        *first.came,
        *second.came,
        *third.came,
    )
    input_grad_t = tied[0]
    quarters = four_rows(*[tied[i : i + 2] for i in (1, 3, 5, 7)], 1)

    rounds.begin(last_job, query_spread, gain_job)
    gate_sum = rows_of(quarters, slice(0, inner))
    up_sum = rows_of(quarters, slice(inner, None))
    (gate_sum, up_sum) = rounds.end([last_job, query_spread, gain_job], gate_sum, up_sum)
    rounds.begin(gain_job)
    rounds.end([gain_job])
    rounds.run(gain_job, 0)

    def by_token(value_t):
        parts = [value_t[:, m * BLK : (m + 1) * BLK].T[None] for m in range(micro)]
        return jnp.stack(parts)

    return (
        by_token(layer_out_t),
        by_token(input_grad_t),
        gain_job.value[:half],
        rows_of(query_spread.quarters[:2]),
        last_job.value,
        rows_of(query_spread.quarters[2:]),
        gain_job.value[half:],
        gate_sum,
        up_sum,
        down_sum.T,
    )


def solution(mesh):
    tokens = P(None, "fsdp", "ctx", None)
    vector = P("fsdp")
    matrix = P("fsdp", None)
    return jax.shard_map(
        per_device,
        mesh=mesh,
        in_specs=(
            tokens,
            vector,
            matrix,
            matrix,
            matrix,
            vector,
            matrix,
            matrix,
            matrix,
            tokens,
            P(),
            P(),
        ),
        out_specs=(
            tokens,
            tokens,
            vector,
            matrix,
            matrix,
            matrix,
            vector,
            matrix,
            matrix,
            matrix,
        ),
        check_vma=False,
    )
```

```python
import functools

import jax
import jax.numpy as jnp
from jax import lax
from jax.experimental import pallas as pl
from jax.experimental.pallas import tpu as pltpu
from jax.sharding import PartitionSpec as P

HEADS = 15
KVH = 5
HD = 64
REP = HEADS // KVH
WINDOW = 2048
BLK = 128
HALF = BLK // 2
KVW = 2 * KVH * HD
EPS = 1e-05
NEG = -1e30
SCALE = HD ** (-0.5)
LANES = 128
GCOLS = REP * BLK

bf16 = jnp.bfloat16
f32 = jnp.float32


def dot(left, right, left_dim, right_dim):
    return lax.dot_general(
        left, right, (((left_dim,), (right_dim,)), ((), ())), preferred_element_type=f32
    )


def flip_ctx(value, bit):
    size = lax.axis_size("ctx")
    mask = sum(1 << b for b in bit) if isinstance(bit, tuple) else 1 << bit
    return lax.ppermute(value, "ctx", [(i, i ^ mask) for i in range(size)])


def swap_fsdp(value):
    return lax.ppermute(value, "fsdp", [(0, 1), (1, 0)])


def tie(values):
    return lax.optimization_barrier(tuple(values))


def own_bit(bit):
    return (lax.axis_index("ctx") >> bit) & 1


def high_bits():
    return list(range(2, lax.axis_size("ctx").bit_length() - 1))


def add_low(kept, arrived):
    return (kept.astype(f32) + arrived.astype(f32)).astype(bf16)


def by_bit(bit, mine, arrived):
    low = own_bit(bit) == 0
    return jnp.where(low, mine, arrived), jnp.where(low, arrived, mine)


def in_order(bit, mine, arrived, dim):
    return jnp.concatenate(by_bit(bit, mine, arrived), axis=dim)


class GatherBlocks:
    def __init__(self, block):
        self.held = block[None]
        bits = high_bits()[::-1]
        self.stages = [tuple(bits[i : i + 2]) for i in range(0, len(bits), 2)] + [None, None]
        self.halves = None

    def operands(self):
        stage = self.stages[0]
        if stage is not None:
            hops = list(stage) + ([stage] if len(stage) == 2 else [])
            return [self.held] * len(hops), hops
        if self.halves is None:
            self.halves = [self.held[:, :HALF], self.held[:, HALF:]]
            self.bits = (1, 0)
        return self.halves, self.bits

    def absorb(self, arrived):
        if self.stages.pop(0) is not None:
            self.held = jnp.concatenate([self.held, *arrived], axis=0)
        else:
            self.halves = [
                jnp.concatenate([h, a], axis=0) for h, a in zip(self.halves, arrived)
            ]
            self.bits = (0, 1)


class ScatterBlocks:
    def __init__(self, first, second):
        self.halves = [first, second]
        self.bits = (0, 1)
        self.stages = [None, None]

    def operands(self):
        count = self.halves[0].shape[0] // 2
        return [half[count:] for half in self.halves], self.bits

    def absorb(self, arrived):
        self.stages.pop(0)
        count = self.halves[0].shape[0] // 2
        self.halves = [add_low(half[:count], a) for half, a in zip(self.halves, arrived)]
        self.bits = (1, 0)


def cut(value, bit, dim):
    half = value.shape[dim] // 2
    own = own_bit(bit)
    sent = lax.dynamic_slice_in_dim(value, (1 - own) * half, half, dim)
    return lax.dynamic_slice_in_dim(value, own * half, half, dim), sent


class Reduce:
    def __init__(self, parts, dims):
        self.first = [parts[0], parts[2]]
        self.kept = [parts[1], parts[3]]
        self.dims = dims
        self.stages = [(0, 1), (1, 0)] + high_bits()

    def operands(self):
        stage = self.stages[0]
        if self.first is not None:
            sent, self.first = self.first, None
        elif isinstance(stage, tuple):
            parts = [cut(v, b, self.dims[0]) for v, b in zip(self.pair, stage)]
            self.kept = [p[0] for p in parts]
            sent = [p[1] for p in parts]
        else:
            if self.pair is not None:
                kept, out = by_bit(stage, *self.pair)
                self.pair = None
            else:
                kept, out = cut(self.held, stage, self.dims[1])
            self.kept, sent, stage = [kept], [out], [stage]
        return sent, stage

    def absorb(self, arrived):
        sums = [add_low(k, a) for k, a in zip(self.kept, arrived)]
        if isinstance(self.stages.pop(0), tuple):
            self.pair = sums
        else:
            self.held = sums[0]


class Spread:
    def __init__(self, job):
        self.held = job.held
        self.dims = job.dims
        self.stages = high_bits()[::-1] + [(1, 0), (0, 1)]
        self.pair = None

    def operands(self):
        stage = self.stages[0]
        if isinstance(stage, tuple):
            return self.pair, stage
        return [self.held], [stage]

    def absorb(self, arrived):
        stage = self.stages.pop(0)
        if isinstance(stage, tuple):
            parts = [by_bit(b, v, a) for v, a, b in zip(self.pair, arrived, stage)]
            if self.stages:
                self.pair = [jnp.concatenate(p, axis=self.dims[0]) for p in parts]
            else:
                self.quarters = [q for p in parts for q in p]
        elif stage == 2:
            self.pair = list(by_bit(stage, self.held, arrived[0]))
        else:
            self.held = in_order(stage, self.held, arrived[0], self.dims[1])


class GatherHigh:
    def __init__(self, value):
        self.held = value[None]
        self.stages = high_bits()[::-1]

    def operands(self):
        return [self.held], [self.stages[0]]

    def absorb(self, arrived):
        self.stages.pop(0)
        self.held = jnp.concatenate([self.held, arrived[0]], axis=0)


class ScatterHigh:
    def __init__(self, held):
        self.held = held
        self.stages = high_bits()

    def operands(self):
        return [self.held[self.held.shape[0] // 2 :]], [self.stages[0]]

    def absorb(self, arrived):
        self.stages.pop(0)
        self.held = add_low(self.held[: self.held.shape[0] // 2], arrived[0])


class Exchange:
    def __init__(self, arrays, bits):
        self.arrays, self.bits = arrays, bits
        self.stages = [None]

    def operands(self):
        return self.arrays, self.bits

    def absorb(self, arrived):
        self.stages.pop()
        self.came = arrived


def four_rows(own, first, second, last, dim):
    rows = []
    for n, (low, high) in enumerate(((1, 0), (0, 1))):
        mine = in_order(low, own[n], first[n], dim)
        rows += by_bit(high, mine, in_order(low, second[n], last[n], dim))
    return rows


class SumVector:
    def __init__(self, value):
        self.value = value
        self.stages = [0, 1] + high_bits()

    def operands(self):
        return [self.value], [self.stages[0]]

    def absorb(self, arrived):
        self.stages.pop(0)
        self.value = self.value + arrived[0]


def rows_of(quarters, columns=slice(None)):
    return jnp.concatenate([q[:, columns] for q in quarters], axis=0).astype(f32)


class Solo:
    def __init__(self, value):
        self.value = value
        high = [(bit, None) for bit in high_bits()]
        self.stages = [(0, True), (1, True)] + high + [(1, False), (0, False)]

    def operands(self):
        bit, cuts = self.stages[0]
        if not cuts:
            return [self.value], [bit]
        self.value, sent = cut(self.value, bit, 0)
        return [sent], [bit]

    def absorb(self, arrived):
        bit, cuts = self.stages.pop(0)
        if cuts is not False:
            self.value = add_low(self.value, arrived[0])
        else:
            kind = bf16 if self.stages else f32
            self.value = in_order(bit, self.value.astype(kind), arrived[0].astype(kind), 0)


class Rounds:
    def __init__(self):
        self.flying = {}
        self.ready = {}
        self.fresh = []

    def begin(self, *jobs):
        for job in jobs:
            arrays, bits = self.ready.pop(job, None) or job.operands()
            self.flying[job] = [flip_ctx(v, b) for v, b in zip(arrays, bits)]

    def prepare(self, *jobs):
        for job in jobs:
            self.ready[job] = job.operands()
            self.fresh.append(job)

    def end(self, jobs, *values):
        ahead = [job for job in self.fresh if job in self.ready]
        self.fresh = []
        arrays = [a for job in jobs for a in self.flying[job]]
        sent = [a for job in ahead for a in self.ready[job][0]]
        rest = list(tie([*values, *arrays, *sent]))
        values, rest = rest[: len(values)], rest[len(values) :]
        for job in jobs:
            count = len(self.flying.pop(job))
            job.absorb(rest[:count])
            rest = rest[count:]
        for job in ahead:
            count = len(self.ready[job][0])
            self.ready[job] = (rest[:count], self.ready[job][1])
            rest = rest[count:]
        return values

    def run(self, job, left):
        while len(job.stages) > left:
            self.begin(job)
            self.end([job])


def key_tile(first_ref, second_ref, places, unit):
    lanes = pl.ds(pl.multiple_of((unit // 2) * LANES, LANES), LANES)
    parts = []
    for first, second in places:
        parts += [first_ref[first, :, lanes], second_ref[second, :, lanes]]
    return jnp.concatenate(parts, axis=0)


def heads_t(rows_t, group, unit):
    parts = [
        rows_t[(group * REP + r) * HD : (group * REP + r + 1) * HD, :] for r in range(REP)
    ]
    block = jnp.concatenate(parts, axis=1)
    zero = jnp.zeros_like(block)
    return jnp.concatenate([zero, block] if unit % 2 else [block, zero], axis=0)


def half_rows(tile_t, unit):
    return tile_t[(unit % 2) * HD : (unit % 2 + 1) * HD, :]


def seen_blocks(bits, which, ids, lengths, slots):
    me, shard = ids[0], ids[1]

    def look(j, own):
        return jnp.where(slots[which, shard, j] == me, j, own)

    own = lax.fori_loop(0, slots.shape[2], look, jnp.int32(0))
    end = jnp.int32(0)
    start = jnp.int32(0)
    for i in range(lengths.shape[2]):
        end = end + lengths[which, shard, i]
        start = jnp.where(end <= own, end, start)
    lowest = jnp.maximum(start, own - WINDOW // BLK)

    def places(index):
        relative = slots[which, shard, jnp.maximum(own - index, 0)] ^ me
        high = jnp.int32(0)
        for position, bit in enumerate(range(bits - 1, 1, -1)):
            high = high | (((relative >> bit) & 1) << position)
        one = (relative & 1) << (bits - 1)
        two = ((relative >> 1) & 1) << (bits - 2)
        swapped = ((relative & 1) << (bits - 2)) | (((relative >> 1) & 1) << (bits - 1))
        return high | one | two, high | swapped

    return own - lowest + 1, places


def pair_mask(far, count, index):
    key = lax.broadcasted_iota(jnp.int32, (BLK, GCOLS), 0)
    query = lax.broadcasted_iota(jnp.int32, (BLK, GCOLS), 1) & (BLK - 1)
    ahead = key - query
    masks = []
    for i in (index, index + 1):
        most = jnp.where(i < count, i * BLK, -2 * BLK)
        mask = ahead <= most
        if far:
            mask = mask & (ahead > i * BLK - WINDOW)
        masks.append(mask)
    return jnp.concatenate(masks, axis=0)


def lanes_at(start, size=LANES):
    return pl.ds(pl.multiple_of(start, LANES), size)


def spread_heads(source_ref, pad_ref, unit, group):
    parts = [
        source_ref[pl.ds(pl.multiple_of((group * REP + r) * HD, HD), HD), :] for r in range(REP)
    ]
    row = pl.multiple_of((unit % 2) * HD, HD)
    pad_ref[pl.ds(row, HD), lanes_at(unit * GCOLS, GCOLS)] = jnp.concatenate(parts, axis=1)


def forward_kernel(
    far, bits, which, ids, lengths, slots, first_ref, second_ref, query_ref, out_ref, lse_ref, pad_ref, half_ref
):
    count, places = seen_blocks(bits, which, ids, lengths, slots)
    pad_ref[...] = jnp.zeros_like(pad_ref)

    @pl.loop(0, KVH)
    def _(group):
        spread_heads(query_ref, pad_ref, group, group)
        columns = lanes_at(group * GCOLS, GCOLS)
        value_unit = KVH + group

        def step(pair, carried):
            high, total, acc = carried
            index = 2 * pair
            held = (places(index), places(index + 1))
            keys = key_tile(first_ref, second_ref, held, group)
            values = key_tile(first_ref, second_ref, held, value_unit)
            scores = dot(keys, pad_ref[:, columns], 1, 0) * SCALE
            scores = jnp.where(pair_mask(far, count, index), scores, NEG)
            new_high = jnp.maximum(high, jnp.max(scores, axis=0, keepdims=True))
            weights = jnp.exp(scores - new_high)
            fade = jnp.exp(high - new_high)
            total = total * fade + jnp.sum(weights, axis=0, keepdims=True)
            acc = acc * fade + dot(values.T, weights.astype(bf16), 1, 0)
            return (new_high, total, acc)

        start = (
            jnp.full((1, GCOLS), NEG, f32),
            jnp.zeros((1, GCOLS), f32),
            jnp.zeros((LANES, GCOLS), f32),
        )
        high, total, acc = lax.fori_loop(0, (count + 1) // 2, step, start)
        half_ref[...] = acc / total
        row = pl.multiple_of((value_unit % 2) * HD, HD)
        for r in range(REP):
            head_rows = pl.ds(pl.multiple_of((group * REP + r) * HD, HD), HD)
            out_ref[head_rows, :] = half_ref[pl.ds(row, HD), r * BLK : (r + 1) * BLK]
        lse_ref[:, columns] = high + jnp.log(total)


def backward_kernel(
    far,
    bits,
    which,
    ids,
    lengths,
    slots,
    first_ref,
    second_ref,
    query_ref,
    grad_ref,
    out_ref,
    lse_ref,
    dq_ref,
    dfirst_ref,
    dsecond_ref,
    pad_ref,
    right_ref,
    delta_ref,
    left_ref,
    acc_ref,
):
    count, places = seen_blocks(bits, which, ids, lengths, slots)
    queries = query_ref[...]
    grads = grad_ref[...]
    product = grads.astype(f32) * out_ref[...]
    for head in range(HEADS):
        delta_ref[:, head * BLK : (head + 1) * BLK] = jnp.sum(
            product[head * HD : (head + 1) * HD, :], axis=0, keepdims=True
        )
    for unit in range(2 * KVH):
        padded = heads_t(queries if unit < KVH else grads, unit % KVH, unit)
        rows = slice(unit * GCOLS, (unit + 1) * GCOLS)
        pad_ref[:, rows] = padded
        right_ref[rows, :] = padded.T
    dfirst_ref[...] = jnp.zeros_like(dfirst_ref)
    dsecond_ref[...] = jnp.zeros_like(dsecond_ref)
    acc_ref[...] = jnp.zeros_like(acc_ref)

    @pl.loop(0, (count + 1) // 2)
    def _(pair):
        index = 2 * pair
        held = (places(index), places(index + 1))
        mask = pair_mask(far, count, index)
        for group in range(KVH):
            value_unit = KVH + group
            columns = slice(group * GCOLS, (group + 1) * GCOLS)
            value_columns = slice(value_unit * GCOLS, (value_unit + 1) * GCOLS)
            keys = key_tile(first_ref, second_ref, held, group)
            values = key_tile(first_ref, second_ref, held, value_unit)
            scores = dot(keys, pad_ref[:, columns], 1, 0) * SCALE
            probs = jnp.where(mask, jnp.exp(scores - lse_ref[:, columns]), 0.0)
            grad_probs = dot(values, pad_ref[:, value_columns], 1, 0)
            grad_scores = (probs * (grad_probs - delta_ref[:, columns])).astype(bf16)
            left_ref[:, columns] = grad_scores
            left_ref[:, value_columns] = probs.astype(bf16)
            keys_t = half_rows(keys.T, group)
            acc_ref[:, columns] += dot(keys_t, grad_scores, 1, 0)
        for tile in range(KVH):
            rows = slice(2 * tile * GCOLS, 2 * (tile + 1) * GCOLS)
            lanes = slice(tile * LANES, (tile + 1) * LANES)
            block = dot(left_ref[:, rows], right_ref[rows, :], 1, 0)
            lane = lax.broadcasted_iota(jnp.int32, (1, LANES), 1) + tile * LANES
            block = (block * jnp.where(lane < KVH * HD, SCALE, 1.0)).astype(bf16)
            first, second = held[0]
            dfirst_ref[first, :, lanes] = block[:HALF]
            dsecond_ref[second, :, lanes] = block[HALF:BLK]

            @pl.when(index + 1 < count)
            def _():
                first, second = held[1]
                dfirst_ref[first, :, lanes] = block[BLK : BLK + HALF]
                dsecond_ref[second, :, lanes] = block[BLK + HALF :]

    for head in range(HEADS):
        columns = slice(head * BLK, (head + 1) * BLK)
        dq_ref[head * HD : (head + 1) * HD, :] = (acc_ref[:, columns] * SCALE).astype(bf16)


def in_hbm(values):
    return [pltpu.with_memory_space_constraint(v, pltpu.HBM) for v in values]


VMEM_SPEC = pl.BlockSpec(memory_space=pltpu.VMEM)
SMEM_SPEC = pl.BlockSpec(memory_space=pltpu.SMEM)


def attention_forward(which, tables, first, second, queries_t):
    steps = first.shape[0]
    return pl.pallas_call(
        functools.partial(
            forward_kernel, steps > WINDOW // BLK, steps.bit_length() - 1, which
        ),
        out_shape=(
            jax.ShapeDtypeStruct((HEADS * HD, BLK), f32),
            jax.ShapeDtypeStruct((1, HEADS * BLK), f32),
        ),
        in_specs=[SMEM_SPEC] * 3 + [VMEM_SPEC] * 3,
        out_specs=(VMEM_SPEC,) * 2,
        scratch_shapes=[pltpu.VMEM((LANES, HEADS * BLK), bf16), pltpu.VMEM((LANES, GCOLS), f32)],
        compiler_params=pltpu.CompilerParams(vmem_limit_bytes=4 << 20),
        cost_estimate=pl.CostEstimate(
            flops=256 * HEADS * HD * BLK * BLK,
            bytes_accessed=first.size * 4,
            transcendentals=HEADS * BLK * BLK * 8,
        ),
        name="attention_forward",
    )(*tables, first, second, queries_t)


def attention_backward(which, tables, first, second, queries_t, grads_t, out_t, lse):
    steps = first.shape[0]
    return pl.pallas_call(
        functools.partial(
            backward_kernel, steps > WINDOW // BLK, steps.bit_length() - 1, which
        ),
        out_shape=(
            jax.ShapeDtypeStruct((HEADS * HD, BLK), bf16),
            jax.ShapeDtypeStruct(first.shape, bf16),
            jax.ShapeDtypeStruct(second.shape, bf16),
        ),
        in_specs=[SMEM_SPEC] * 3 + [VMEM_SPEC] * 6,
        out_specs=(VMEM_SPEC,) * 3,
        scratch_shapes=[
            pltpu.VMEM((LANES, 2 * KVH * GCOLS), bf16),
            pltpu.VMEM((2 * KVH * GCOLS, LANES), bf16),
            pltpu.VMEM((1, HEADS * BLK), f32),
            pltpu.VMEM((2 * BLK, 2 * KVH * GCOLS), bf16),
            pltpu.VMEM((HD, HEADS * BLK), f32),
        ],
        compiler_params=pltpu.CompilerParams(vmem_limit_bytes=8 << 20),
        cost_estimate=pl.CostEstimate(
            flops=640 * HEADS * HD * BLK * BLK,
            bytes_accessed=first.size,
            transcendentals=HEADS * BLK * BLK,
        ),
        name="attention_backward",
    )(*tables, first, second, queries_t, grads_t, out_t, lse)


def block_kernel(
    x_ref,
    cot_ref,
    att_ref,
    out_w_ref,
    gain_ref,
    gate_w_ref,
    up_w_ref,
    down_w_ref,
    hidden_ref,
    grads_ref,
    normed_ref,
    layer_ref,
    grad_mixed_ref,
    grad_low_ref,
    grad_att_ref,
    gain_grad_ref,
    mixed,
    normed,
    cot,
    grad_normed,
    layer,
):
    step = pl.program_id(0)

    @pl.when(step == 0)
    def _():
        cot[...] = cot_ref[...].T
        values = x_ref[...].astype(f32).T + dot(att_ref[...], out_w_ref[...], 0, 0)
        mixed[...] = values
        inverse = lax.rsqrt(jnp.mean(values * values, axis=-1, keepdims=True) + EPS)
        low = (values * inverse * gain_ref[...]).astype(bf16)
        normed[...] = low
        normed_ref[...] = low.T
        layer[...] = values
        grad_normed[...] = jnp.zeros_like(grad_normed)

    grad_hidden = dot(cot[...], down_w_ref[...], 1, 0)
    gate = dot(normed[...], gate_w_ref[...], 1, 0)
    up = dot(normed[...], up_w_ref[...], 1, 0)
    sigmoid = jax.nn.sigmoid(gate)
    silu = gate * sigmoid
    hidden = (silu * up).astype(bf16)
    grad_gate = (grad_hidden * up * sigmoid * (1.0 + gate * (1.0 - sigmoid))).astype(bf16)
    grad_up = (grad_hidden * silu).astype(bf16)
    hidden_ref[...] = hidden
    grads_ref[0] = grad_gate
    grads_ref[1] = grad_up
    layer[...] += dot(hidden, down_w_ref[...], 1, 1)
    grad_normed[...] += dot(grad_gate, gate_w_ref[...], 1, 1) + dot(
        grad_up, up_w_ref[...], 1, 1
    )

    @pl.when(step == pl.num_programs(0) - 1)
    def _():
        values = mixed[...]
        layer_ref[...] = layer[...].astype(bf16).T
        inverse = lax.rsqrt(jnp.mean(values * values, axis=-1, keepdims=True) + EPS)
        grads = grad_normed[...]
        gain_grad_ref[...] = jnp.sum(grads * values * inverse, axis=0, keepdims=True)
        scaled = grads * gain_ref[...]
        cubed = inverse * inverse * inverse
        back = inverse * scaled - values * cubed * jnp.mean(
            scaled * values, axis=-1, keepdims=True
        )
        grad_mixed = cot[...].astype(f32) + back
        low = grad_mixed.astype(bf16)
        grad_mixed_ref[...] = grad_mixed.T
        grad_low_ref[...] = low
        grad_att_ref[...] = dot(out_w_ref[...], low, 1, 1).astype(bf16)


def feed_forward(x_t, cot_t, attended_t, out_w, gain, gate_w, up_w, down_w_t):
    width, rows = x_t.shape
    inner = gate_w.shape[1]
    tile = 512

    def fixed(shape):
        return pl.BlockSpec(shape, lambda i: (0,) * len(shape))

    weight = pl.BlockSpec((width, tile), lambda i: (0, i))
    wide = (width, rows)
    return pl.pallas_call(
        block_kernel,
        grid=(inner // tile,),
        in_specs=[fixed(wide)] * 3
        + [fixed(out_w.shape), fixed((1, width)), weight, weight, weight],
        out_specs=(
            pl.BlockSpec((rows, tile), lambda i: (0, i)),
            pl.BlockSpec((2, rows, tile), lambda i: (0, 0, i)),
            fixed(wide),
            fixed(wide),
            fixed(wide),
            fixed((rows, width)),
            fixed(wide),
            fixed((1, width)),
        ),
        out_shape=(
            pltpu.HBM((rows, inner), bf16),
            pltpu.HBM((2, rows, inner), bf16),
            pltpu.HBM(wide, bf16),
            pltpu.HBM(wide, bf16),
            pltpu.HBM(wide, f32),
            pltpu.HBM((rows, width), bf16),
            pltpu.HBM(wide, bf16),
            pltpu.HBM((1, width), f32),
        ),
        scratch_shapes=[
            pltpu.VMEM((rows, width), f32),
            pltpu.VMEM((rows, width), bf16),
            pltpu.VMEM((rows, width), bf16),
            pltpu.VMEM((rows, width), f32),
            pltpu.VMEM((rows, width), f32),
        ],
        compiler_params=pltpu.CompilerParams(vmem_limit_bytes=26 << 20),
        cost_estimate=pl.CostEstimate(
            flops=12 * rows * width * inner,
            bytes_accessed=8 * width * inner,
            transcendentals=rows * inner,
        ),
        name="feed_forward",
    )(*in_hbm([x_t, cot_t, attended_t, out_w, gain, gate_w, up_w, down_w_t]))


def weight_grad_kernel(products, sides, ids, *refs):
    values = []
    for number, (by_shard, right_t) in enumerate(products):
        left, left_other, right, right_other = refs[4 * number : 4 * number + 4]
        rows = left_other.shape[0]
        start = pl.multiple_of(ids[1] * rows if by_shard else 0, 8)
        dim = 1 if right_t else 0
        values.append(
            dot(left[pl.ds(start, rows), :], right[...].reshape(right.shape[-2:]), 1, dim)
            + dot(left_other[...], right_other[...].reshape(right_other.shape[-2:]), 1, dim)
        )
    outs = refs[4 * len(products) :]
    for number, (product, first, rows, bit) in enumerate(sides):
        sent, kept = outs[2 * number : 2 * number + 2]
        half = rows // 2
        low = values[product][first : first + half].astype(bf16)
        high = values[product][first + half : first + rows].astype(bf16)
        own = (ids[0] >> bit) & 1

        @pl.when(own == 0)
        def _():
            kept[...] = low
            sent[...] = high

        @pl.when(own != 0)
        def _():
            kept[...] = high
            sent[...] = low


def weight_grad(name, ids, products, operands, right_specs, sides, tiles, columns):
    tile = columns // tiles
    specs = []
    for (left, left_other, _, _), rights in zip(operands, right_specs):
        specs += [
            pl.BlockSpec(left.shape, lambda i, ids: (0, 0)),
            pl.BlockSpec(left_other.shape, lambda i, ids: (0, 0)),
            *rights,
        ]
    shapes = [(side[2] // 2, columns) for side in sides for _ in range(2)]
    return pl.pallas_call(
        functools.partial(weight_grad_kernel, products, sides),
        grid_spec=pltpu.PrefetchScalarGridSpec(
            num_scalar_prefetch=1,
            grid=(tiles,),
            in_specs=specs,
            out_specs=[pl.BlockSpec((rows, tile), lambda i, ids: (0, i)) for rows, _ in shapes],
        ),
        out_shape=[pltpu.HBM(shape, bf16) for shape in shapes],
        compiler_params=pltpu.CompilerParams(vmem_limit_bytes=11 << 20),
        cost_estimate=pl.CostEstimate(
            flops=16 * sum(rows * width for rows, width in shapes) * 512,
            bytes_accessed=2 * sum(rows * width for rows, width in shapes),
            transcendentals=0,
        ),
        name=name,
    )(ids, *in_hbm([o for group in operands for o in group]))


def keyval_grad_kernel(left, own, other, out, total):
    step = pl.program_id(0)
    tokens = own.shape[1]
    value = dot(left[0, :, :tokens], own[0], 1, 0) + dot(left[0, :, tokens:], other[0], 1, 0)

    @pl.when(step == 0)
    def _():
        total[...] = value

    @pl.when(step != 0)
    def _():
        total[...] += value

    @pl.when(step == pl.num_programs(0) - 1)
    def _():
        out[...] = total[...].astype(bf16)


def keyval_grad(left, own, other):
    count, rows, _ = left.shape
    columns = own.shape[2]

    def block(value):
        return pl.BlockSpec((1,) + value.shape[1:], lambda i: (i, 0, 0))

    return pl.pallas_call(
        keyval_grad_kernel,
        grid=(count,),
        in_specs=[block(left), block(own), block(other)],
        out_specs=pl.BlockSpec((rows, columns), lambda i: (0, 0)),
        out_shape=jax.ShapeDtypeStruct((rows, columns), bf16),
        scratch_shapes=[pltpu.VMEM((rows, columns), f32)],
        compiler_params=pltpu.CompilerParams(vmem_limit_bytes=5 << 20),
        cost_estimate=pl.CostEstimate(
            flops=2 * left.size * columns,
            bytes_accessed=2 * (left.size + 2 * own.size),
            transcendentals=0,
        ),
        name="keyval_grad",
    )(left, own, other)


def per_device(
    inputs,
    gain_attn,
    w_query,
    w_keyval,
    w_out,
    gain_mlp,
    w_gate,
    w_up,
    w_down,
    cotangent,
    seq_blocks,
    block_slots,
):
    micro = inputs.shape[0]
    shard = lax.axis_index("fsdp")
    is_low = shard == 0
    ids = jnp.stack([lax.axis_index("ctx"), shard]).astype(jnp.int32)
    rounds = Rounds()

    def joined(part, other):
        return jnp.concatenate(
            [jnp.where(is_low, part, other), jnp.where(is_low, other, part)], axis=0
        )

    def whole(part):
        return lax.all_gather(part, "fsdp", axis=0, tiled=True)

    def theirs(value, dim):
        half = value.shape[dim] // 2
        return lax.dynamic_slice_in_dim(value, (1 - shard) * half, half, dim)

    def tokens_last(value):
        return jnp.concatenate([value[m, 0].T for m in range(micro)], axis=1)

    out_full = whole(w_out)
    gate_full = whole(w_gate)
    up_full = whole(w_up)
    down_full_t = whole(w_down).T

    attn_gain = joined(gain_attn, swap_fsdp(gain_attn)).astype(f32)[:, None]
    keyval_full = joined(w_keyval, swap_fsdp(w_keyval))
    x_t = tokens_last(inputs)
    in_t = x_t.astype(f32)
    inverse_attn = lax.rsqrt(jnp.mean(in_t * in_t, axis=0, keepdims=True) + EPS)
    normed_t = (in_t * inverse_attn * attn_gain).astype(bf16)
    keyvals = dot(normed_t, keyval_full, 0, 0).astype(bf16)
    gathers = [GatherBlocks(keyvals[m * BLK : (m + 1) * BLK]) for m in range(micro)]

    rounds.begin(*gathers)
    (w_query, gain_mlp, cotangent, normed_t) = rounds.end(
        gathers[:1], w_query, gain_mlp, cotangent, normed_t
    )
    while len(gathers[0].stages) > 2:
        rounds.end(gathers[1:])
        rounds.begin(*gathers)
        rounds.end(gathers[:1])

    half = normed_t.shape[0] // 2
    rounds.begin(gathers[0])
    query_other, gain_other = swap_fsdp(w_query), swap_fsdp(gain_mlp)
    normed_other = swap_fsdp(theirs(normed_t, 0))
    (query_other, gain_other, normed_other) = rounds.end(
        gathers[:1], query_other, gain_other, normed_other
    )
    rounds.begin(gathers[0])
    normed_mine = lax.dynamic_slice_in_dim(normed_t, shard * half, half, 0)
    column = GatherHigh(jnp.concatenate([normed_mine, normed_other], axis=1))
    rounds.begin(column)
    cot_t = tokens_last(cotangent)
    query_full = joined(w_query, query_other)
    mlp_gain = joined(gain_mlp, gain_other).astype(f32)[None]
    (cot_t, mlp_gain) = rounds.end(gathers, cot_t, mlp_gain)

    rounds.begin(gathers[1])
    cot_other = swap_fsdp(cot_t)
    queries_t = dot(query_full, normed_t, 0, 0).astype(bf16)
    (cot_other, queries_t) = rounds.end([gathers[1], column], cot_other, queries_t)
    queries = [queries_t[:, m * BLK : (m + 1) * BLK] for m in range(micro)]
    tables = (ids, seq_blocks, block_slots)

    rounds.begin(gathers[1], column)
    first = attention_forward(0, tables, *gathers[0].halves, queries[0])
    first = rounds.end(gathers[1:], *first)
    second = attention_forward(1, tables, *gathers[1].halves, queries[1])
    second = rounds.end([column], *second)
    rounds.run(column, 0)
    outs, lses = zip(first, second)
    attended_t = jnp.concatenate(outs, axis=1).astype(bf16)

    attended_other = swap_fsdp(theirs(attended_t, 0))
    (
        hidden,
        grad_inner,
        normed_mlp_t,
        layer_out_t,
        grad_mixed_t,
        grad_mixed_low,
        grad_attended_t,
        mlp_gain_grad,
    ) = feed_forward(
        x_t, cot_t, attended_t, out_full, mlp_gain, gate_full, up_full, down_full_t
    )
    hidden_other = swap_fsdp(theirs(hidden, 1))
    mlp_other = swap_fsdp(theirs(normed_mlp_t, 0))
    inner_other = swap_fsdp(grad_inner)

    part = hidden_other.shape[1]
    width = cot_t.shape[0]
    tokens, inner = hidden.shape
    near = pl.BlockSpec((tokens, part // 2), lambda i, ids: (0, ids[1] * 2 + i))
    far = pl.BlockSpec((tokens, part // 2), lambda i, ids: (0, i))
    down_job = Reduce(
        weight_grad(
            "down_grad",
            ids,
            ((False, False),),
            ((cot_t, cot_other, hidden, hidden_other),),
            ((near, far),),
            ((0, 0, half, 0), (0, half, half, 1)),
            2,
            part,
        ),
        (1, 0),
    )

    def attention_back(m):
        return attention_backward(
            m,
            tables,
            *gathers[m].halves,
            queries[m],
            grad_attended_t[:, m * BLK : (m + 1) * BLK],
            outs[m],
            lses[m],
        )

    rounds.prepare(down_job)
    (grad_inner, inner_other, grad_attended_t, grad_mixed_low, normed_mlp_t, mlp_other) = rounds.end(
        [], grad_inner, inner_other, grad_attended_t, grad_mixed_low, normed_mlp_t, mlp_other
    )

    rounds.begin(down_job)
    spec = pl.BlockSpec((1, tokens, inner // 5), lambda i, ids: (i // 5, 0, i % 5))
    inner_job = Reduce(
        weight_grad(
            "inner_grad",
            ids,
            ((True, False),),
            ((normed_mlp_t, mlp_other, grad_inner, inner_other),),
            ((spec, spec),),
            ((0, 0, half // 2, 0), (0, half // 2, half // 2, 1)),
            10,
            2 * inner,
        ),
        (1, 1),
    )
    rounds.prepare(inner_job)
    (grad_attended_t, grad_mixed_low) = rounds.end([], grad_attended_t, grad_mixed_low)

    rounds.begin(inner_job)
    (grad_attended_t, grad_mixed_low) = rounds.end([down_job], grad_attended_t, grad_mixed_low)

    back_first = attention_back(0)
    key_first = ScatterBlocks(*back_first[1:])
    rounds.prepare(down_job, key_first)
    (grad_attended_t, grad_mixed_low, *back_first) = rounds.end(
        [inner_job], grad_attended_t, grad_mixed_low, *back_first
    )
    key_first.halves = back_first[1:]

    rounds.begin(down_job, key_first)
    rounds.prepare(inner_job)
    back_second = attention_back(1)
    key_second = ScatterBlocks(*back_second[1:])
    rounds.prepare(key_second)
    mixed_other = swap_fsdp(grad_mixed_low)
    (mixed_other, *back_second) = rounds.end([down_job, key_first], mixed_other, *back_second)
    key_second.halves = back_second[1:]

    rounds.begin(inner_job, key_second, down_job)
    rounds.prepare(key_first)
    grad_queries_t = jnp.concatenate([back_first[0], back_second[0]], axis=1)
    queries_other = swap_fsdp(grad_queries_t)
    (queries_other, grad_queries_t) = rounds.end(
        [inner_job, down_job], queries_other, grad_queries_t
    )

    rounds.begin(down_job, inner_job, key_first)
    flat = pl.BlockSpec((width, tokens), lambda i, ids: (0, 0))
    flat_half = pl.BlockSpec((tokens, width), lambda i, ids: (0, 0))
    query_job = Reduce(
        weight_grad(
            "query_grad",
            ids,
            ((True, True), (True, False)),
            (
                (normed_t, normed_other, grad_queries_t, queries_other),
                (attended_t, attended_other, grad_mixed_low, mixed_other),
            ),
            ((flat, flat), (flat_half, flat_half)),
            ((0, 0, half, 0), (1, 0, half, 1)),
            1,
            width,
        ),
        (0, 1),
    )
    rounds.prepare(query_job)
    (grad_queries_t,) = rounds.end([key_second, down_job, inner_job], grad_queries_t)
    rounds.run(down_job, 0)
    rounds.run(inner_job, 1)
    down_spread = Spread(down_job)

    rounds.begin(query_job, down_spread, inner_job)
    rounds.prepare(key_second)
    rounds.end([key_first, down_spread, inner_job])
    rounds.run(down_spread, 3)
    inner_spread = Spread(inner_job)

    rounds.begin(key_second, down_spread, inner_spread)
    grad_normed_t = dot(query_full, grad_queries_t, 1, 0)
    (grad_normed_t,) = rounds.end(
        [key_second, query_job, down_spread, inner_spread], grad_normed_t
    )
    rounds.run(inner_spread, 3)

    parts = [part for job in (key_first, key_second) for part in job.halves]
    key_column = jnp.concatenate(parts, axis=1)
    rounds.begin(down_spread, query_job, inner_spread)
    key_other = swap_fsdp(key_column)
    last_job = Solo(keyval_grad(column.held, key_column, key_other))
    rounds.prepare(last_job)
    (key_column,) = rounds.end([down_spread, query_job, inner_spread], key_column)
    key_job = ScatterHigh(key_column)

    own = inner_spread.pair
    first = Exchange(own, (1, 0))
    second = Exchange(own, (0, 1))
    rounds.begin(last_job, query_job, key_job, first, down_spread, second)
    rounds.end([last_job, query_job, key_job])
    rounds.run(key_job, 1)
    rounds.begin(last_job, query_job, key_job)
    rounds.end([first, down_spread, last_job, key_job, query_job])
    rounds.run(query_job, 0)
    query_spread = Spread(query_job)

    third = Exchange(first.came, (0, 1))
    rounds.begin(third, last_job, query_spread)
    grad_keyvals = key_job.held[0]
    grad_normed_t = grad_normed_t + dot(keyval_full, grad_keyvals, 1, 1)
    attn_gain_grad = jnp.sum(grad_normed_t * in_t * inverse_attn, axis=1)
    gains = jnp.stack([attn_gain_grad, mlp_gain_grad[0]])
    gains_other = swap_fsdp(theirs(gains, 1))
    gains_mine = lax.dynamic_slice_in_dim(gains, shard * half, half, 1)
    (grad_normed_t, gains_mine, gains_other) = rounds.end(
        [last_job, query_spread, second], grad_normed_t, gains_mine, gains_other
    )
    rounds.run(query_spread, 3)
    rounds.run(last_job, 3)
    gain_job = SumVector((gains_mine + gains_other).reshape(-1))

    rounds.begin(last_job, query_spread, gain_job)
    down_sum = rows_of(down_spread.quarters)
    (down_sum,) = rounds.end([last_job, query_spread, gain_job, third], down_sum)

    rounds.begin(last_job, query_spread, gain_job)
    scaled = grad_normed_t * attn_gain
    cubed = inverse_attn * inverse_attn * inverse_attn
    input_grad_t = (
        grad_mixed_t
        + inverse_attn * scaled
        - in_t * cubed * jnp.mean(scaled * in_t, axis=0, keepdims=True)
    )
    tied = rounds.end(
        [last_job, query_spread, gain_job],
        input_grad_t,
        *own,
        *first.came,
        *second.came,
        *third.came,
    )
    input_grad_t = tied[0]
    quarters = four_rows(*[tied[i : i + 2] for i in (1, 3, 5, 7)], 1)

    rounds.begin(last_job, query_spread, gain_job)
    gate_sum = rows_of(quarters, slice(0, inner))
    (gate_sum,) = rounds.end([gain_job], gate_sum)
    rounds.run(gain_job, 1)
    rounds.begin(gain_job)
    up_sum = rows_of(quarters, slice(inner, None))
    (up_sum,) = rounds.end([last_job, query_spread, gain_job], up_sum)

    def by_token(value_t):
        parts = [value_t[:, m * BLK : (m + 1) * BLK].T[None] for m in range(micro)]
        return jnp.stack(parts)

    return (
        by_token(layer_out_t),
        by_token(input_grad_t),
        gain_job.value[:half],
        rows_of(query_spread.quarters[:2]),
        last_job.value,
        rows_of(query_spread.quarters[2:]),
        gain_job.value[half:],
        gate_sum,
        up_sum,
        down_sum.T,
    )


def solution(mesh):
    tokens = P(None, "fsdp", "ctx", None)
    vector = P("fsdp")
    matrix = P("fsdp", None)
    return jax.shard_map(
        per_device,
        mesh=mesh,
        in_specs=(
            tokens,
            vector,
            matrix,
            matrix,
            matrix,
            vector,
            matrix,
            matrix,
            matrix,
            tokens,
            P(),
            P(),
        ),
        out_specs=(
            tokens,
            tokens,
            vector,
            matrix,
            matrix,
            matrix,
            vector,
            matrix,
            matrix,
            matrix,
        ),
        check_vma=False,
    )
```
